128 devices in a mesh: src: 4 (over y_lo, core), tile: 32 (over x, z, y_hi).
Axes of the slice: x: 4, y: 4 (y_hi: 2, y_lo: 2; y = y_hi * 2 + y_lo), z: 4, core: 2. Of those that a mesh axis runs over, the one named last changes fastest.
Arguments:
- mask: bfloat16 [256, 16384], P('src', 'tile'), may hold values from -6 to 6
- target: bfloat16 [256, 16384], P('src', 'tile'), may hold values from 0 to 1
- start_block: float32 [2, 24, 128, 128], replicated, may hold values from -6 to 6
- zernike: float32 [32, 37], replicated, may hold values from -0.3 to 0.3
- source_points: int32 [512, 2], replicated, may hold values from -24 to 24
- source_weight: float32 [512], replicated, may hold values from 0.25 to 1
- tile_slit: int32 [64], P('tile'), may hold values from 0 to 31
Outputs:
- resist: bfloat16 [256, 16384], P('src', 'tile')
- mask_grad: bfloat16 [256, 16384], P('src', 'tile')
The draws below stay inside these ranges and needn't reach their ends.
All inputs are finite; a program needn't handle non-finite values.
Results may differ from the reference program's by a relative error of at most 0.024.
Values may be sent and summed in bfloat16 or wider, within the bound.
No kernel may reach another device: no remote copies, remote signals or barrier semaphores. Data moves between devices by JAX's collectives and lax.ppermute only.
A program may use at most 128 MiB of HBM per device.

```python
import math
import jax
import jax.numpy as jnp
from jax import lax

KB = 128
NR = 24
NZ = 37
SOURCE = 512
RAD = 40
SHIFT = 24
HALO = 64
ITERS = 4
TS = 256
TILES = 64
SLITS = 32


def draw_tile_slit(key, part):
    key_values, key_places = jax.random.split(key)
    values = jax.random.randint(key_values, (TILES,), 0, SLITS, dtype=jnp.int32)
    places = jax.random.permutation(key_places, TILES)
    values = values.at[places[0]].set(0)
    values = values.at[places[1]].set(SLITS - 1)
    return values


def touch_ends(values, key, smallest, top_value):
    longest = values.shape.index(max(values.shape))
    spots = []
    for shift in (0, 1):
        where = [jax.random.randint(jax.random.fold_in(key, axis), (), 0, length) for axis, length in enumerate(values.shape)]
        where[longest] = (where[longest] + shift) % values.shape[longest]
        spots.append(tuple(where))
    return values.at[spots[0]].set(smallest).at[spots[1]].set(top_value)


def steps_of(own_key, shape, cuts, low, largest):
    gain = 1.0
    for dim, blocks in cuts:
        draws = jax.random.uniform(jax.random.fold_in(jax.random.fold_in(own_key, 6), dim), (blocks,), jnp.float32, low / len(cuts), largest / len(cuts))
        gain = gain * jnp.repeat(jnp.exp(draws), shape[dim] // blocks).reshape((-1,) + (1,) * (len(shape) - 1 - dim))
    return gain


def bell_draw(rng, shape, width, most, cuts=(), held_as=jnp.bfloat16):
    array = jax.random.normal(rng, shape, jnp.float32) * width
    if len(cuts) > 0:
        array = steps_of(rng, shape, cuts, -0.22, 0.18) * array
    return jnp.clip(array, min=-most, max=most).astype(held_as)


def setup_inputs(seed: int = 0) -> dict:
    splits = jax.random.split(jax.random.key(seed), 8)
    return {
        "mask": bell_draw(splits[0], (TS, TILES * TS), 1.0, 6.0, ((0, 4), (1, 32))),
        "target": jnp.clip(1.0 * jax.random.uniform(splits[1], (TS, TILES * TS), jnp.float32) ** steps_of(splits[1], (TS, TILES * TS), ((0, 4), (1, 32)), -0.2, 0.2), 0.0, 1.0).astype(jnp.bfloat16),
        "start_block": bell_draw(splits[2], (2, NR, KB, KB), 1.0, 6.0, (), jnp.float32),
        "zernike": bell_draw(splits[3], (SLITS, NZ), 0.05, 0.3, (), jnp.float32),
        "source_points": touch_ends(jax.random.randint(splits[4], (SOURCE, 2), -SHIFT, SHIFT + 1), jax.random.fold_in(splits[4], 1), -SHIFT, SHIFT).astype(jnp.int32),
        "source_weight": jnp.clip(jnp.exp(jax.random.uniform(splits[5], (SOURCE,), jnp.float32, math.log(0.25), math.log(1.0))), 0.25, 1.0),
        "tile_slit": draw_tile_slit(jax.random.fold_in(splits[7], 71), 0),
    }


STEEPNESS = 4.0
THRESHOLD = 0.5
RIDGE_SHARE = 0.001
EXACT_MODE = lax.Precision.HIGHEST

def noll_terms(term_count):
    listing = []
    degree = 0
    while len(listing) < term_count:
        for azimuth in range(degree % 2, degree + 1, 2):
            if azimuth == 0:
                listing.append((degree, 0, 0))
            else:
                for repeat in range(2):
                    number = len(listing) + 1
                    listing.append((degree, azimuth, 2 if number % 2 == 0 else 1))
        degree += 1
    return listing[:term_count]

def radial_terms(degree, azimuth):
    powers = []
    for counter in range((degree - azimuth) // 2 + 1):
        factor = (-1) ** counter * math.factorial(degree - counter) / (math.factorial(counter) * math.factorial((degree + azimuth) // 2 - counter) * math.factorial((degree - azimuth) // 2 - counter))
        powers.append((degree - 2 * counter, factor))
    return powers

def pupil_grid(coefficients):
    extent = KB + 2 * SHIFT
    coords = jnp.arange(extent, dtype=jnp.int32) - (KB // 2 + SHIFT)
    row_coord = coords[:, None]
    col_coord = coords[None, :]
    radius_sq = row_coord * row_coord + col_coord * col_coord
    inside = (radius_sq <= RAD * RAD).astype(jnp.float32)
    radius = jnp.sqrt(radius_sq.astype(jnp.float32)) / RAD
    azimuth_angle = jnp.arctan2(col_coord.astype(jnp.float32) + 0.0 * radius, row_coord.astype(jnp.float32) + 0.0 * radius)
    aberration = jnp.zeros((extent, extent), jnp.float32)
    for position, (degree, azimuth, parity) in enumerate(noll_terms(NZ)):
        radial = jnp.zeros((extent, extent), jnp.float32)
        for exponent, factor in radial_terms(degree, azimuth):
            radial = radial + factor * radius ** exponent
        if azimuth == 0:
            profile = math.sqrt(degree + 1.0) * radial
        elif parity == 2:
            profile = math.sqrt(2.0 * degree + 2.0) * radial * jnp.cos(azimuth * azimuth_angle)
        else:
            profile = math.sqrt(2.0 * degree + 2.0) * radial * jnp.sin(azimuth * azimuth_angle)
        aberration = aberration + coefficients[position] * profile
    phase_angle = 2.0 * math.pi * aberration
    return jnp.stack([inside * jnp.cos(phase_angle), inside * jnp.sin(phase_angle)])

def source_windows(pupil_values, offsets, row_start, row_total):

    def single(offset):
        return lax.dynamic_slice(pupil_values, (jnp.zeros((), jnp.int32), (offset[0] + SHIFT + row_start).astype(jnp.int32), (offset[1] + SHIFT).astype(jnp.int32)), (2, row_total, KB))
    windowed = jax.vmap(single)(offsets)
    return windowed.reshape(offsets.shape[0], 2 * row_total * KB)

def pupil_products(windows, kernel_block):
    real_pairs = jnp.concatenate([kernel_block[0], kernel_block[1]], axis=1)
    imag_pairs = jnp.concatenate([kernel_block[1], -kernel_block[0]], axis=1)
    stacked = jnp.concatenate([real_pairs, imag_pairs], axis=0)
    return jnp.einsum('sf,kf->sk', windows, stacked, precision=EXACT_MODE)

def spread_terms(windows, products):
    spread = jnp.einsum('sk,sf->kf', products, windows, precision=EXACT_MODE)
    half_width = spread.shape[1] // 2
    image_re = spread[:NR, :half_width] - spread[NR:, half_width:]
    image_im = spread[NR:, :half_width] + spread[:NR, half_width:]
    return jnp.stack([image_re, image_im])

def inner_products(left_block, right_block):
    return jnp.einsum('zkf,zlf->kl', left_block, right_block, precision=EXACT_MODE)

def orthonormal(applied, gram_matrix):
    shift_term = RIDGE_SHARE * jnp.trace(gram_matrix) / NR + 1e-06
    factor = jnp.linalg.cholesky(gram_matrix + shift_term * jnp.eye(NR, dtype=jnp.float32))
    inverse = jax.scipy.linalg.solve_triangular(factor, jnp.eye(NR, dtype=jnp.float32), lower=True)
    return jnp.einsum('kl,zlf->zkf', inverse, applied, precision=EXACT_MODE)

def synthesize(coefficients, source_points, source_weight, start_block):
    pupil_values = pupil_grid(coefficients)
    windows = source_windows(pupil_values, source_points, 0, KB)
    weighting = source_weight / (math.pi * RAD * RAD * jnp.sum(source_weight))
    kernel_block = start_block.reshape(2, NR, KB * KB)
    for iteration in range(ITERS + 1):
        products = pupil_products(windows, kernel_block) * weighting[:, None]
        applied = spread_terms(windows, products)
        if iteration < ITERS:
            kernel_block = orthonormal(applied, inner_products(applied, applied))
    mixing = inner_products(kernel_block, applied)
    mixing = (0.5 * (mixing + mixing.T)).astype(jnp.bfloat16)
    return (kernel_block.reshape(2, NR, KB, KB).astype(jnp.bfloat16), mixing)

def phase_table(positions, period):
    frequency = jnp.arange(KB, dtype=jnp.int32) - KB // 2
    residue = jnp.mod(positions[:, None] * frequency[None, :], period)
    angles = 2.0 * math.pi / period * residue.astype(jnp.float32)
    return (jnp.cos(angles).astype(jnp.bfloat16), jnp.sin(angles).astype(jnp.bfloat16))

def row_phase_table(positions):
    cosine_table, sine_table = phase_table(positions, TS)
    return jnp.concatenate([cosine_table, sine_table], axis=1)

def column_tables():
    patch_width = TS + 2 * HALO
    cosine_table, sine_table = phase_table(jnp.arange(patch_width, dtype=jnp.int32), patch_width)
    column_forward = jnp.concatenate([cosine_table, -sine_table], axis=1)
    inner_cos = cosine_table[HALO:HALO + TS]
    inner_sin = sine_table[HALO:HALO + TS]
    column_inverse = jnp.concatenate([inner_cos, -inner_sin], axis=1)
    column_adjoint = jnp.concatenate([inner_cos, inner_sin], axis=1)
    return (column_forward, column_inverse, column_adjoint)

def contract(form, left_array, right_array):
    return jnp.einsum(form, left_array.astype(jnp.float32), right_array.astype(jnp.float32), precision=EXACT_MODE)

def image_tile(patch, goal_tile, kernel, mixing, row_table, column_forward, column_inverse, column_adjoint):
    patch_width = TS + 2 * HALO
    spectrum_scale = 1.0 / math.sqrt(TS * patch_width)
    columns = jnp.dot(patch.astype(jnp.float32), column_forward.astype(jnp.float32), preferred_element_type=jnp.float32).astype(jnp.bfloat16)
    row_sums = contract('xc,xd->cd', row_table, columns)
    spectrum_re = spectrum_scale * (row_sums[:KB, :KB] + row_sums[KB:, KB:])
    spectrum_im = spectrum_scale * (row_sums[:KB, KB:] - row_sums[KB:, :KB])
    kernel_re = kernel[0].astype(jnp.float32)
    kernel_im = kernel[1].astype(jnp.float32)
    product_re = (kernel_re * spectrum_re + kernel_im * spectrum_im).astype(jnp.bfloat16)
    product_im = (kernel_re * spectrum_im - kernel_im * spectrum_re).astype(jnp.bfloat16)
    blocks = jnp.concatenate([jnp.concatenate([product_re, product_im], axis=2), jnp.concatenate([-product_im, product_re], axis=2)], axis=1)
    rows_mixed = contract('xc,kcd->kxd', row_table, blocks).astype(jnp.bfloat16)
    fields = contract('kxc,yc->kxy', rows_mixed, column_inverse)
    mixed_fields = jnp.einsum('kl,lxy->kxy', mixing.astype(jnp.float32), fields, precision=EXACT_MODE)
    intensity = lax.optimization_barrier(jnp.sum(fields * mixed_fields, axis=0))
    resist = jax.nn.sigmoid(STEEPNESS * (intensity - THRESHOLD))
    resist_slope = 2.0 * (resist - goal_tile.astype(jnp.float32)) * STEEPNESS * resist * (1.0 - resist)
    field_grad = (2.0 * mixed_fields * resist_slope[None]).astype(jnp.bfloat16)
    adjoint_cols = contract('kxy,yc->kxc', field_grad, column_adjoint).astype(jnp.bfloat16)
    adjoint_rows = contract('xc,kxd->kcd', row_table, adjoint_cols)
    turned_re = adjoint_rows[:, :KB, :KB] - adjoint_rows[:, KB:, KB:]
    turned_im = adjoint_rows[:, :KB, KB:] + adjoint_rows[:, KB:, :KB]
    grad_re = lax.optimization_barrier(jnp.sum(kernel_re * turned_re + kernel_im * turned_im, axis=0))
    grad_im = lax.optimization_barrier(jnp.sum(kernel_im * turned_re - kernel_re * turned_im, axis=0))
    back_re = (spectrum_scale * grad_re).astype(jnp.bfloat16)
    back_im = (spectrum_scale * grad_im).astype(jnp.bfloat16)
    back_block = jnp.concatenate([jnp.concatenate([back_re, back_im], axis=1), jnp.concatenate([-back_im, back_re], axis=1)], axis=0)
    back_rows = jnp.dot(row_table.astype(jnp.float32), back_block.astype(jnp.float32), preferred_element_type=jnp.float32).astype(jnp.bfloat16)
    patch_grad = contract('xc,yc->xy', back_rows, column_forward)
    return (resist.astype(jnp.bfloat16), patch_grad)

def reference(mask, target, start_block, zernike, source_points, source_weight, tile_slit):

    def per_slit(coefficients):
        return synthesize(coefficients, source_points, source_weight, start_block)
    kernels, mixings = lax.map(per_slit, zernike)
    patch_width = TS + 2 * HALO
    padded = jnp.pad(mask, ((0, 0), (HALO, HALO)))
    row_table = row_phase_table(jnp.arange(TS, dtype=jnp.int32))
    column_forward, column_inverse, column_adjoint = column_tables()

    def per_tile(tile_number):
        start_col = (tile_number * TS).astype(jnp.int32)
        patch = lax.dynamic_slice_in_dim(padded, start_col, patch_width, 1)
        goal_tile = lax.dynamic_slice_in_dim(target, start_col, TS, 1)
        slit_index = tile_slit[tile_number]
        return image_tile(patch, goal_tile, kernels[slit_index], mixings[slit_index], row_table, column_forward, column_inverse, column_adjoint)
    resist_tiles, patch_grads = lax.map(per_tile, jnp.arange(TILES, dtype=jnp.int32))
    inner_part = patch_grads[:, :, HALO:HALO + TS]
    low_rims = patch_grads[:, :, :HALO]
    high_rims = patch_grads[:, :, TS + HALO:]
    empty_rim = jnp.zeros((1, TS, HALO), jnp.float32)
    from_left = jnp.concatenate([empty_rim, high_rims[:-1]], axis=0)
    from_right = jnp.concatenate([low_rims[1:], empty_rim], axis=0)
    total = inner_part + jnp.pad(from_left, ((0, 0), (0, 0), (0, TS - HALO))) + jnp.pad(from_right, ((0, 0), (0, 0), (TS - HALO, 0)))
    resist = jnp.transpose(resist_tiles, (1, 0, 2)).reshape(TS, TILES * TS)
    mask_grad = jnp.transpose(total, (1, 0, 2)).reshape(TS, TILES * TS).astype(jnp.bfloat16)
    return (resist, mask_grad)
```

```python
import math

import jax
import jax.numpy as jnp
import numpy as np
from jax import lax
from jax.sharding import PartitionSpec as P

KB = 128
NR = 24
NZ = 37
RAD = 40
SHIFT = 24
HALO = 64
ITERS = 4
TS = 256
PW = TS + 2 * HALO
GRID = 2 * SHIFT + 1
PUP = 2 * RAD + 1

STEEPNESS = 4.0
THRESHOLD = 0.5
RIDGE_SHARE = 0.001
BF = jnp.bfloat16
F32 = jnp.float32


def noll_terms(term_count):
    listing = []
    degree = 0
    while len(listing) < term_count:
        for azimuth in range(degree % 2, degree + 1, 2):
            if azimuth == 0:
                listing.append((degree, 0, 0))
            else:
                for repeat in range(2):
                    number = len(listing) + 1
                    listing.append((degree, azimuth, 2 if number % 2 == 0 else 1))
        degree += 1
    return listing[:term_count]


def radial_terms(degree, azimuth):
    powers = []
    for counter in range((degree - azimuth) // 2 + 1):
        factor = (
            (-1) ** counter
            * math.factorial(degree - counter)
            / (
                math.factorial(counter)
                * math.factorial((degree + azimuth) // 2 - counter)
                * math.factorial((degree - azimuth) // 2 - counter)
            )
        )
        powers.append((degree - 2 * counter, factor))
    return powers


def zernike_tables():
    coords = np.arange(PUP) - RAD
    row, col = np.meshgrid(coords, coords, indexing="ij")
    radius = np.sqrt(row * row + col * col) / RAD
    angle = np.arctan2(col * 1.0, row * 1.0)
    out = []
    for degree, azimuth, parity in noll_terms(NZ):
        radial = sum(factor * radius**power for power, factor in radial_terms(degree, azimuth))
        if azimuth == 0:
            out.append(math.sqrt(degree + 1.0) * radial)
        elif parity == 2:
            out.append(math.sqrt(2.0 * degree + 2.0) * radial * np.cos(azimuth * angle))
        else:
            out.append(math.sqrt(2.0 * degree + 2.0) * radial * np.sin(azimuth * angle))
    inside = row * row + col * col <= RAD * RAD
    return np.stack(out) * inside, inside.astype(np.float32)


def dft(rows, cols, sign, period=KB):
    return np.exp(sign * 2j * np.pi * np.mod(np.outer(rows, cols), period) / period)


def cmul(a, b):
    return (a[0] * b[0] - a[1] * b[1], a[0] * b[1] + a[1] * b[0])


def left(table, pair, form="xd,kdy->kxy"):
    tr, ti = jnp.asarray(table.real, BF), jnp.asarray(table.imag, BF)
    ar, ai = pair[0].astype(BF), pair[1].astype(BF)

    def e(t, a):
        return jnp.einsum(form, t, a, preferred_element_type=F32)

    return (e(tr, ar) - e(ti, ai), e(tr, ai) + e(ti, ar))


def right(pair, table):
    return left(table, pair, "yd,kxd->kxy")


def synthesize(coefficients, source_points, source_weight, start_block):
    ztab, inside = zernike_tables()
    zt = jnp.asarray(ztab, F32)
    turns = jnp.einsum("z,zuv->uv", coefficients, zt, precision=lax.Precision.HIGHEST)
    angle = 2.0 * math.pi * turns
    pr, pi = inside * jnp.cos(angle), inside * jnp.sin(angle)
    freq = np.arange(KB)
    signed = np.arange(KB) - KB // 2
    offs = np.arange(GRID) - SHIFT
    pup = np.arange(PUP) - RAD
    e_p = dft(freq, pup, -1)
    e_u = dft(freq, signed, -1)
    e_d = dft(freq, offs, 1)
    hat = right(left(e_p, (pr[None], pi[None])), e_p)
    hr, hi = hat[0][0], hat[1][0]
    q1 = (pr[80, 40], pi[80, 40])
    m1 = (pr[0, 40], pi[0, 40])
    q2 = (pr[40, 80], pi[40, 80])
    m2 = (pr[40, 0], pi[40, 0])
    conj = lambda z: (z[0], -z[1])
    z1 = cmul(conj(q1), m1)
    z2 = cmul(conj(q2), m2)
    scale = 1.0 / (math.pi * RAD * RAD * jnp.sum(source_weight))
    hot_x = (source_points[:, 0:1] == offs[None]).astype(F32)
    hot_y = (source_points[:, 1:2] == offs[None]).astype(F32)
    wmap = jnp.einsum("sx,sy->xy", hot_x, hot_y * (source_weight * scale)[:, None], precision=lax.Precision.HIGHEST)
    power = (hr * hr + hi * hi) / (KB * KB)
    b = (start_block[0], start_block[1])
    bh = right(left(e_u, b), e_u)
    bh = cmul((hr / (KB * KB), -hi / (KB * KB)), bh)
    d = right(left(e_d.conj().T, bh), e_d.conj().T)
    rev = slice(KB // 2 - SHIFT, KB // 2 + SHIFT + 1)
    row = cmul(conj(q1), tuple(x[:, 0, rev][:, ::-1] for x in b))
    col = cmul(conj(q2), tuple(x[:, rev, 0][:, ::-1] for x in b))
    d = tuple(x.at[:, 0, :].add(-r).at[:, :, 0].add(-c) for x, r, c in zip(d, row, col))

    def gapply(c):
        ch = left(e_d, right(c, e_d))
        h = right(left(e_d.conj().T, (power * ch[0], power * ch[1])), e_d.conj().T)
        r0 = cmul(z1, tuple(x[:, 48, :] for x in c))
        r1 = cmul(conj(z1), tuple(x[:, 0, :] for x in c))
        c0 = cmul(z2, tuple(x[:, :, 48] for x in c))
        c1 = cmul(conj(z2), tuple(x[:, :, 0] for x in c))
        return tuple(
            x.at[:, 0, :].add(-y[:, 0, :] - a0).at[:, 48, :].add(-a1).at[:, :, 0].add(-y[:, :, 0] - e0).at[:, :, 48].add(-e1)
            for x, y, a0, a1, e0, e1 in zip(h, c, r0, r1, c0, c1)
        )

    hp = lax.Precision.HIGHEST
    inner = lambda a, c: sum(jnp.einsum("kxy,lxy->kl", x, y, precision=hp) for x, y in zip(a, c))
    comb = lambda z, a: tuple(jnp.einsum("kl,lxy->kxy", z, x, precision=hp) for x in a)
    c = tuple(wmap * x for x in d)
    for iteration in range(ITERS):
        h = gapply(c)
        gram = inner(c, h)
        gram = 0.5 * (gram + gram.T)
        shift_term = RIDGE_SHARE * jnp.trace(gram) / NR + 1e-06
        factor = jnp.linalg.cholesky(gram + shift_term * jnp.eye(NR, dtype=F32))
        inverse = jax.scipy.linalg.solve_triangular(factor, jnp.eye(NR, dtype=F32), lower=True)
        h = comb(inverse, h)
        if iteration < ITERS - 1:
            c = tuple(wmap * x for x in h)
        else:
            c = comb(inverse, c)
    mixing = inner(tuple(wmap * x for x in h), h)
    mixing = 0.5 * (mixing + mixing.T)
    ch = left(e_d, right(c, e_d))
    kern = right(left(e_u.conj().T, cmul((hr / (KB * KB), hi / (KB * KB)), ch)), e_u.conj().T)
    row = cmul(q1, tuple(x[:, 0, ::-1] for x in c))
    col = cmul(q2, tuple(x[:, ::-1, 0] for x in c))
    kern = tuple(x.at[:, 0, rev].add(-r).at[:, rev, 0].add(-k) for x, r, k in zip(kern, row, col))
    return (kern[0].astype(BF), kern[1].astype(BF), mixing)


def tables_of(count, period):
    t = dft(np.arange(count), np.arange(KB) - KB // 2, 1, period)
    return t.real.astype(np.float32), t.imag.astype(np.float32)


def imaging(patch, goal, kr, ki, mixing, full_rows, my_rows):
    col_c, col_s = tables_of(PW, PW)
    col_fwd = jnp.asarray(np.concatenate([col_c, -col_s], 1), BF)
    col_inv = jnp.asarray(np.concatenate([col_c, -col_s], 1)[HALO : HALO + TS], BF)
    col_adj = jnp.asarray(np.concatenate([col_c, col_s], 1)[HALO : HALO + TS], BF)
    s = 1.0 / math.sqrt(TS * PW)
    columns = jnp.dot(patch, col_fwd, preferred_element_type=F32).astype(BF)
    sums = jnp.einsum("xc,xd->cd", full_rows, columns, preferred_element_type=F32)
    sr = s * (sums[:KB, :KB] + sums[KB:, KB:])
    si = s * (sums[:KB, KB:] - sums[KB:, :KB])
    kr, ki = kr.astype(F32), ki.astype(F32)
    wr = (kr * sr + ki * si).astype(BF)
    wi = (kr * si - ki * sr).astype(BF)
    blocks = jnp.concatenate([jnp.concatenate([wr, wi], 2), jnp.concatenate([-wi, wr], 2)], 1)
    rows_mixed = jnp.einsum("xc,kcd->kxd", my_rows, blocks, preferred_element_type=F32).astype(BF)
    fields = jnp.einsum("kxc,yc->kxy", rows_mixed, col_inv, preferred_element_type=F32)
    mixed = jnp.einsum("kl,lxy->kxy", mixing, fields, precision=lax.Precision.HIGHEST)
    intensity = jnp.sum(fields * mixed, axis=0)
    resist = jax.nn.sigmoid(STEEPNESS * (intensity - THRESHOLD))
    slope = 2.0 * (resist - goal.astype(F32)) * STEEPNESS * resist * (1.0 - resist)
    grad = (2.0 * mixed * slope[None]).astype(BF)
    acols = jnp.einsum("kxy,yc->kxc", grad, col_adj, preferred_element_type=F32).astype(BF)
    arows = jnp.einsum("xc,kxd->kcd", my_rows, acols, preferred_element_type=F32)
    tr = arows[:, :KB, :KB] - arows[:, KB:, KB:]
    ti = arows[:, :KB, KB:] + arows[:, KB:, :KB]
    gr = s * jnp.sum(kr * tr + ki * ti, axis=0)
    gi = s * jnp.sum(ki * tr - kr * ti, axis=0)
    return resist.astype(BF), jnp.stack([gr, gi]).astype(BF)


def back(total, own_rows):
    col_c, col_s = tables_of(PW, PW)
    col_fwd = jnp.asarray(np.concatenate([col_c, -col_s], 1), BF)
    br, bi = total[0].astype(BF), total[1].astype(BF)
    block = jnp.concatenate([jnp.concatenate([br, bi], 1), jnp.concatenate([-bi, br], 1)], 0)
    rows = jnp.dot(own_rows, block, preferred_element_type=F32).astype(BF)
    return jnp.einsum("xc,yc->xy", rows, col_fwd, preferred_element_type=F32)


def swap(x, m, size):
    return lax.ppermute(x, "src", [(i, i ^ m) for i in range(size)])


def shift(x, step, count):
    pairs = [(i, i + step) for i in range(count) if 0 <= i + step < count]
    return lax.ppermute(x, "tile", pairs)


def on_device(mask, target, start_block, zernike, source_points, source_weight, tile_slit):
    groups = lax.axis_size("tile")
    size = lax.axis_size("src")
    rank = lax.axis_index("src")
    t = rank % 2
    rows_here = mask.shape[0]
    from_left = shift(mask[:, -HALO:], 1, groups)
    from_right = shift(mask[:, :HALO], -1, groups)
    ext = jnp.concatenate([from_left, mask, from_right], axis=1)
    parts = [ext[:, :PW], ext[:, TS:]]
    pick = lambda a, b: jnp.where(t == 0, a, b)
    mine, other = pick(parts[0], parts[1]), pick(parts[1], parts[0])
    patch = jnp.concatenate([mine, swap(other, 1, size), swap(mine, 2, size), swap(other, 3, size)], axis=0)
    halves = [target[:, :TS], target[:, TS:]]
    goal = jnp.concatenate([pick(halves[0], halves[1]), swap(pick(halves[1], halves[0]), 1, size)], axis=0)
    tc, ts = tables_of(TS, TS)
    rtab = jnp.asarray(np.concatenate([tc, ts], 1), BF)
    rows_of = lambda m: lax.dynamic_slice_in_dim(rtab, rows_here * (rank ^ m), rows_here, 0)
    rr = [rows_of(m) for m in range(4)]
    full_rows = jnp.concatenate(rr, 0)
    my_rows = jnp.concatenate(rr[:2], 0)

    slit = pick(tile_slit[0], tile_slit[1])
    kr, ki, mixing = synthesize(zernike[slit], source_points, source_weight, start_block)
    resist, grad = imaging(patch, goal, kr, ki, mixing, full_rows, my_rows)
    got = swap(resist[rows_here:], 1, size)
    keep = resist[:rows_here]
    resist_out = jnp.concatenate([pick(keep, got), pick(got, keep)], axis=1)
    g1, g2, g3 = (swap(grad, m, size).astype(F32) for m in (1, 2, 3))
    tot_mine = grad.astype(F32) + g2
    tot_other = g1 + g3
    pg = [back(pick(tot_mine, tot_other), rr[0]), back(pick(tot_other, tot_mine), rr[0])]
    width = mask.shape[1]
    acc = jnp.pad(pg[0], ((0, 0), (0, width + 2 * HALO - PW))) + jnp.pad(pg[1], ((0, 0), (width + 2 * HALO - PW, 0)))
    in_left = shift(acc[:, -HALO:].astype(BF), 1, groups).astype(F32)
    in_right = shift(acc[:, :HALO].astype(BF), -1, groups).astype(F32)
    inner = acc[:, HALO : HALO + width]
    inner = inner + jnp.pad(in_left, ((0, 0), (0, width - HALO))) + jnp.pad(in_right, ((0, 0), (width - HALO, 0)))
    return (resist_out, inner.astype(BF))


def solution(mesh):
    placed = (P("src", "tile"), P("src", "tile"), P(), P(), P(), P(), P("tile"))
    return jax.shard_map(
        on_device,
        mesh=mesh,
        in_specs=placed,
        out_specs=(P("src", "tile"), P("src", "tile")),
        check_vma=False,
    )
```

```python
import math

import jax
import jax.numpy as jnp
import numpy as np
from jax import lax
from jax.experimental import pallas as pl
from jax.experimental.pallas import tpu as pltpu
from jax.sharding import PartitionSpec as P

KB = 128
NR = 24
NZ = 37
RAD = 40
SHIFT = 24
HALO = 64
ITERS = 4
TS = 256
PW = TS + 2 * HALO
GRID = 2 * SHIFT + 1
PUP = 2 * RAD + 1

STEEPNESS = 4.0
THRESHOLD = 0.5
RIDGE_SHARE = 0.001
BF = jnp.bfloat16
F32 = jnp.float32


def noll_terms(term_count):
    listing = []
    degree = 0
    while len(listing) < term_count:
        for azimuth in range(degree % 2, degree + 1, 2):
            if azimuth == 0:
                listing.append((degree, 0, 0))
            else:
                for repeat in range(2):
                    number = len(listing) + 1
                    listing.append((degree, azimuth, 2 if number % 2 == 0 else 1))
        degree += 1
    return listing[:term_count]


def radial_terms(degree, azimuth):
    powers = []
    for counter in range((degree - azimuth) // 2 + 1):
        factor = (
            (-1) ** counter
            * math.factorial(degree - counter)
            / (
                math.factorial(counter)
                * math.factorial((degree + azimuth) // 2 - counter)
                * math.factorial((degree - azimuth) // 2 - counter)
            )
        )
        powers.append((degree - 2 * counter, factor))
    return powers


def zernike_tables():
    coords = np.arange(PUP) - RAD
    row, col = np.meshgrid(coords, coords, indexing="ij")
    radius = np.sqrt(row * row + col * col) / RAD
    angle = np.arctan2(col * 1.0, row * 1.0)
    out = []
    for degree, azimuth, parity in noll_terms(NZ):
        radial = sum(factor * radius**power for power, factor in radial_terms(degree, azimuth))
        if azimuth == 0:
            out.append(math.sqrt(degree + 1.0) * radial)
        elif parity == 2:
            out.append(math.sqrt(2.0 * degree + 2.0) * radial * np.cos(azimuth * angle))
        else:
            out.append(math.sqrt(2.0 * degree + 2.0) * radial * np.sin(azimuth * angle))
    inside = row * row + col * col <= RAD * RAD
    return np.stack(out) * inside, inside.astype(np.float32)


def dft(rows, cols, sign, period=KB):
    return np.exp(sign * 2j * np.pi * np.mod(np.outer(rows, cols), period) / period)


def cmul(a, b):
    return (a[0] * b[0] - a[1] * b[1], a[0] * b[1] + a[1] * b[0])


SLOTS = 50
ROWS = SLOTS * NR
PAD = 64
HI = lax.Precision.HIGHEST


def real_form(table):
    return np.block([[table.real, -table.imag], [table.imag, table.real]])


def split(table):
    high = table.astype(np.float32).astype(jnp.bfloat16)
    low = (table - high.astype(np.float64)).astype(jnp.bfloat16)
    return high, low


def block_tables():
    freq = np.arange(KB)
    big = real_form(dft(freq, np.arange(KB) - KB // 2, -1))
    offs = np.zeros((KB, PAD), np.complex128)
    offs[:, :GRID] = dft(freq, np.arange(GRID) - SHIFT, 1)
    small = real_form(offs)
    rev = np.zeros((PAD, KB), np.float32)
    for spot in range(GRID):
        rev[spot, KB // 2 + SHIFT - spot] = 1.0
    lb, lb_lo = split(big)
    lbt, lbt_lo = split(big.T.copy())
    lc, lc_lo = split(small)
    lct, lct_lo = split(small.T.copy())
    wide = lambda a, b: np.concatenate([a, b], axis=1)
    tall = lambda a, b: np.concatenate([a, b], axis=0)
    return (lb, lbt, lc, lct, tall(lct, lct_lo), wide(lc, lc_lo), lbt_lo, lb_lo, rev.astype(jnp.bfloat16), rev.T.copy().astype(jnp.bfloat16))


def mm(a, b):
    return jnp.dot(a, b, preferred_element_type=F32)


def nt(a, b, precision=None):
    return lax.dot_general(a, b, (((1,), (1,)), ((), ())), precision=precision, preferred_element_type=F32)


def lanes(shape):
    return lax.broadcasted_iota(jnp.int32, shape, 1)


def sublanes(shape):
    return lax.broadcasted_iota(jnp.int32, shape, 0)


def factor(gram, floor):
    eye = (sublanes((NR, PAD)) == lanes((NR, PAD))).astype(F32)
    work = jnp.concatenate([gram, jnp.zeros((NR, PAD - NR), F32), eye], axis=1)
    row_no = sublanes((NR, 1))
    diag = jnp.zeros((NR, 1), F32)
    for k in range(NR):
        row = work[k : k + 1, :]
        col = work[:, k : k + 1]
        pivot = jnp.maximum(col[k : k + 1, :], floor)
        diag = jnp.where(row_no == k, pivot, diag)
        ratio = jnp.where(row_no > k, col / pivot, 0.0)
        work = work - ratio * row
    scale = lax.rsqrt(diag)
    return work[:, :NR] * scale, work[:, PAD : PAD + NR] * scale


def synth_kernel(rank_ref, slit_ref, zern_ref, sp_ref, sw_ref, zt_ref, ins_ref, b0_ref, lb, lbt, lc, lct, lct2, lc2, lbt_lo, lb_lo, rev, revt, out_ref, pup, hat, a1, f2, ab, c_ref, h_ref, wf, bx, c2):
    slit = slit_ref[lax.rem(rank_ref[0], 2)]
    turns = jnp.zeros((96, KB), F32)
    for z in range(NZ):
        turns = turns + zern_ref[slit, z] * zt_ref[z]
    turns = turns - jnp.floor(turns + 0.5)
    half = math.pi * turns
    sq = half * half
    sine = jnp.full_like(half, 1.0 / math.factorial(15))
    for n in (13, 11, 9, 7, 5, 3, 1):
        sine = 1.0 / math.factorial(n) - sine * sq
    sine = sine * half
    cosine = jnp.full_like(half, 1.0 / math.factorial(14))
    for n in (12, 10, 8, 6, 4, 2, 0):
        cosine = 1.0 / math.factorial(n) - cosine * sq
    pr = ins_ref[...] * (1.0 - 2.0 * sine * sine)
    pi = ins_ref[...] * (2.0 * sine * cosine)
    spot = lambda a, i, j: a[i : i + 1, j : j + 1]
    q1r, q1i = spot(pr, 88, 64), spot(pi, 88, 64)
    m1r, m1i = spot(pr, 8, 64), spot(pi, 8, 64)
    q2r, q2i = spot(pr, 48, 104), spot(pi, 48, 104)
    m2r, m2i = spot(pr, 48, 24), spot(pi, 48, 24)
    z1r, z1i = q1r * m1r + q1i * m1i, q1r * m1i - q1i * m1r
    z2r, z2i = q2r * m2r + q2i * m2i, q2r * m2i - q2i * m2r
    edge = jnp.zeros((16, 2 * KB), F32)
    both = jnp.concatenate([edge, jnp.concatenate([pr, pi], axis=1), edge], axis=0).astype(BF)
    ph = mm(both, lbt[...])
    stacked = jnp.concatenate([ph[:, :KB], ph[:, KB:]], axis=0).astype(BF)
    ph = mm(lb[...], stacked)
    hr, hi = ph[:KB], ph[KB:]
    hat[0] = jnp.concatenate([hr, hr], axis=1) / (KB * KB)
    hat[1] = jnp.concatenate([hi, hi], axis=1) / (KB * KB)
    power = (hr * hr + hi * hi) / (KB * KB)
    power = jnp.concatenate([power, power], axis=1)
    hat[2] = power

    weights = sw_ref[...]
    weights = weights / (math.pi * RAD * RAD * jnp.sum(weights, axis=1, keepdims=True))
    count = sp_ref.shape[0]
    lane = lanes((count, KB))
    hot_x = (lane - SHIFT == sp_ref[:, 0:1]).astype(F32)
    hot_y = (jnp.where(lane >= PAD, lane - PAD, lane) - SHIFT == sp_ref[:, 1:2]).astype(F32)
    wmap = jnp.dot(hot_x.T * weights, hot_y, precision=HI, preferred_element_type=F32)
    for s in range(SLOTS):
        wf[s * NR : (s + 1) * NR, :] = jnp.broadcast_to(wmap[s : s + 1, :], (NR, KB))

    rs, cs = sublanes((KB, KB)), lanes((KB, KB))
    at = lambda i, j, v: jnp.where((rs == i) & (cs == j), v, 0.0)
    one = jnp.ones((1, 1), F32)
    top = 2 * SHIFT
    ky = (
        at(0, 0, one) + at(PAD, PAD, one)
        + at(top, 0, z2r) + at(PAD + top, 0, -z2i) + at(top, PAD, z2i) + at(PAD + top, PAD, z2r)
        + at(0, top, z2r) + at(PAD, top, z2i) + at(0, PAD + top, -z2i) + at(PAD, PAD + top, z2r)
    ).astype(BF)
    kq0 = jnp.concatenate([at(0, 0, q2r) + at(0, PAD, -q2i), at(0, 0, q2i) + at(0, PAD, q2r)], axis=0).astype(BF)
    kq2 = jnp.concatenate([at(0, 0, q2r) + at(PAD, 0, -q2i), at(0, 0, q2i) + at(PAD, 0, q2r)], axis=1).astype(BF)

    a1[:, ROWS:, :] = jnp.zeros((2, PAD * NR - ROWS, KB), F32)

    def pack(x0, x1):
        return jnp.concatenate(
            [jnp.concatenate([x0[:, :KB], x1[:, :KB]], axis=1), jnp.concatenate([x0[:, KB:], x1[:, KB:]], axis=1)], axis=0
        )

    def unpack(y, height):
        return (
            jnp.concatenate([y[:height, :KB], y[height:, :KB]], axis=1),
            jnp.concatenate([y[:height, KB:], y[height:, KB:]], axis=1),
        )

    def put(ref, k, x):
        ref[0, pl.ds(k, PAD, stride=NR), :] = x[:, :KB]
        ref[1, pl.ds(k, PAD, stride=NR), :] = x[:, KB:]

    def get(ref, k):
        return jnp.concatenate([ref[0, pl.ds(k, PAD, stride=NR), :], ref[1, pl.ds(k, PAD, stride=NR), :]], axis=1)

    def both_halves(ref):
        return jnp.concatenate([ref[0, :ROWS, :], ref[1, :ROWS, :]], axis=1).astype(BF)

    prow = sublanes((KB, 2 * KB))
    urow = sublanes((2 * KB, 2 * KB))

    def start(p, carry):
        k = 2 * p
        parts = []
        for step in range(2):
            block = jnp.concatenate([b0_ref[0, k + step], b0_ref[1, k + step]], axis=1).astype(BF)
            put(bx, k + step, mm(rev[...], block))
            parts.append(mm(block, lbt[...]))
        x = pack(parts[0], parts[1])
        y = mm(lb[...], x.astype(BF))
        yr, yi = y[:KB], y[KB:]
        y = jnp.concatenate([hat[0] * yr + hat[1] * yi, hat[0] * yi - hat[1] * yr], axis=0)
        d = mm(lct[...], y.astype(BF))
        xr, xi = x[0:1], x[KB : KB + 1]
        cr, ci = (q1r * xr + q1i * xi) / KB, (q1r * xi - q1i * xr) / KB
        d = d - jnp.where(prow == 0, cr, 0.0) - jnp.where(prow == PAD, ci, 0.0)
        d0, d1 = unpack(d, PAD)
        put(f2, k, d0)
        put(f2, k + 1, d1)
        return carry

    lax.fori_loop(0, NR // 2, start, 0)
    first = mm(both_halves(f2), lc[...]) - mm(both_halves(bx), kq0)
    c_ref[...] = wf[...] * first

    def wide(ref):
        return jnp.concatenate([ref[s * NR : (s + 1) * NR, :] for s in range(SLOTS)], axis=1)

    def tallput(ref, x):
        for s in range(SLOTS):
            ref[s * NR : (s + 1) * NR, :] = x[:, s * KB : (s + 1) * KB]

    def forward(p):
        return pack(get(a1, 2 * p), get(a1, 2 * p + 1)).astype(BF)

    def middle(p, carry):
        y = mm(lc[...], forward(p))
        y = jnp.concatenate([hat[2] * y[:KB], hat[2] * y[KB:]], axis=0)
        d0, d1 = unpack(mm(lct[...], y.astype(BF)), PAD)
        put(f2, 2 * p, d0)
        put(f2, 2 * p + 1, d1)
        return carry

    def apply():
        coef = c_ref[...].astype(BF)
        full = mm(coef, lct[...])
        a1[0, :ROWS, :] = full[:, :KB]
        a1[1, :ROWS, :] = full[:, KB:]
        lax.fori_loop(0, NR // 2, middle, 0)
        last = slice(top * NR, (top + 1) * NR)
        lr, li, ur, ui = a1[0, 0:NR, :], a1[1, 0:NR, :], a1[0, last, :], a1[1, last, :]
        f2[0, 0:NR, :] = f2[0, 0:NR, :] - (lr + z1r * ur - z1i * ui) / KB
        f2[1, 0:NR, :] = f2[1, 0:NR, :] - (li + z1r * ui + z1i * ur) / KB
        f2[0, last, :] = f2[0, last, :] - (z1r * lr + z1i * li) / KB
        f2[1, last, :] = f2[1, last, :] - (z1r * li - z1i * lr) / KB
        h_ref[...] = mm(both_halves(f2), lc[...]) - mm(coef, ky)
        gram = nt(wide(c_ref), wide(h_ref), HI)
        gram = 0.5 * (gram + gram.T)
        eye = sublanes((NR, NR)) == lanes((NR, NR))
        trace = jnp.sum(jnp.sum(jnp.where(eye, gram, 0.0), axis=1, keepdims=True), axis=0, keepdims=True)
        return factor(gram + jnp.where(eye, RIDGE_SHARE * trace / NR + 1e-06, 0.0), 0.0)[1]

    def step(iteration, carry):
        inverse = apply()
        new = jnp.dot(inverse, wide(h_ref), precision=HI, preferred_element_type=F32)
        tallput(h_ref, new)
        c_ref[...] = wf[...] * h_ref[...]
        return carry

    lax.fori_loop(0, ITERS - 1, step, 0)
    inverse = apply()
    f2[0, :ROWS, :] = wf[...] * h_ref[...]
    moment = nt(jnp.concatenate([f2[0, s * NR : (s + 1) * NR, :] for s in range(SLOTS)], axis=1), wide(h_ref), HI)
    moment = jnp.dot(inverse, moment, precision=HI, preferred_element_type=F32)
    mixing = nt(moment, inverse, HI)
    mixing = 0.5 * (mixing + mixing.T)
    eye = sublanes((NR, NR)) == lanes((NR, NR))
    trace = jnp.sum(jnp.sum(jnp.where(eye, mixing, 0.0), axis=1, keepdims=True), axis=0, keepdims=True)
    root = factor(mixing, 1e-6 * trace + 1e-30)[0]
    combine = jnp.dot(root, inverse, precision=HI, preferred_element_type=F32)
    tallput(c_ref, jnp.dot(combine, wide(c_ref), precision=HI, preferred_element_type=F32))
    coef = c_ref[...].astype(BF)
    full = mm(jnp.concatenate([coef, coef], axis=1), lct2[...])
    a1[0, :ROWS, :] = full[:, :KB]
    a1[1, :ROWS, :] = full[:, KB:]
    c2[:ROWS, :] = c_ref[...]
    c2[ROWS:, :] = jnp.zeros((PAD * NR - ROWS, KB), F32)

    def finish(p, carry):
        k = 2 * p
        x = pack(get(a1, k), get(a1, k + 1))
        xb = x.astype(BF)
        y = mm(lc2[...], jnp.concatenate([xb, xb], axis=0))
        yr, yi = y[:KB], y[KB:]
        y = jnp.concatenate([hat[0] * yr - hat[1] * yi, hat[0] * yi + hat[1] * yr], axis=0).astype(BF)
        u = mm(lbt[...], y) + mm(lbt_lo[...], y)
        xr, xi = x[0:1], x[PAD : PAD + 1]
        cr, ci = (q1r * xr - q1i * xi) / KB, (q1r * xi + q1i * xr) / KB
        u = u - jnp.where(urow == 0, cr, 0.0) - jnp.where(urow == KB, ci, 0.0)
        pair = unpack(u, KB)
        for step in range(2):
            cols = mm(revt[...], c2[pl.ds(k + step, PAD, stride=NR), :].astype(BF))
            ub = pair[step].astype(BF)
            kern = mm(ub, lb[...]) + mm(ub, lb_lo[...]) - mm(cols.astype(BF), kq2)
            out_ref[k + step] = kern.astype(BF)
        return carry

    lax.fori_loop(0, NR // 2, finish, 0)


def synthesize(rank, tile_slit, zernike, source_points, source_weight, start_block):
    ztab, inside = zernike_tables()
    wide = np.zeros((NZ, 96, KB), np.float32)
    wide[:, 8:89, 24:105] = ztab
    ins = np.zeros((96, KB), np.float32)
    ins[8:89, 24:105] = inside
    smem = pl.BlockSpec(memory_space=pltpu.SMEM)
    vmem = pl.BlockSpec(memory_space=pltpu.VMEM)
    tables = [jnp.asarray(t) for t in block_tables()]
    big = (2, PAD * NR, KB)
    return pl.pallas_call(
        synth_kernel,
        out_shape=jax.ShapeDtypeStruct((NR, KB, 2 * KB), BF),
        in_specs=[smem] * 3 + [vmem] * (5 + len(tables)),
        out_specs=vmem,
        scratch_shapes=[
            pltpu.VMEM((8, KB), F32),
            pltpu.VMEM((3, KB, 2 * KB), F32),
            pltpu.VMEM(big, F32),
            pltpu.VMEM(big, F32),
            pltpu.VMEM((8, KB), F32),
            pltpu.VMEM((ROWS, KB), F32),
            pltpu.VMEM((ROWS, KB), F32),
            pltpu.VMEM((ROWS, KB), F32),
            pltpu.VMEM(big, F32),
            pltpu.VMEM((PAD * NR, KB), F32),
        ],
    )(rank.reshape(1), tile_slit, zernike, source_points, source_weight.reshape(1, -1), jnp.asarray(wide), jnp.asarray(ins), start_block, *tables)


def tables_of(count, period):
    t = dft(np.arange(count), np.arange(KB) - KB // 2, 1, period)
    return t.real.astype(np.float32), t.imag.astype(np.float32)


def imaging(patch, goal, kern, full_rows, my_rows):
    col_c, col_s = tables_of(PW, PW)
    col_fwd = jnp.asarray(np.concatenate([col_c, -col_s], 1), BF)
    col_inv = jnp.asarray(np.concatenate([col_c, -col_s], 1)[HALO : HALO + TS], BF)
    col_adj = jnp.asarray(np.concatenate([col_c, col_s], 1)[HALO : HALO + TS], BF)
    s = 1.0 / math.sqrt(TS * PW)
    columns = jnp.dot(patch, col_fwd, preferred_element_type=F32).astype(BF)
    sums = jnp.einsum("xc,xd->cd", full_rows, columns, preferred_element_type=F32)
    sr = s * (sums[:KB, :KB] + sums[KB:, KB:])
    si = s * (sums[:KB, KB:] - sums[KB:, :KB])
    kr, ki = kern[:, :, :KB].astype(F32), kern[:, :, KB:].astype(F32)
    wr = (kr * sr + ki * si).astype(BF)
    wi = (kr * si - ki * sr).astype(BF)
    blocks = jnp.concatenate([jnp.concatenate([wr, wi], 2), jnp.concatenate([-wi, wr], 2)], 1)
    rows_mixed = jnp.einsum("xc,kcd->kxd", my_rows, blocks, preferred_element_type=F32).astype(BF)
    fields = jnp.einsum("kxc,yc->kxy", rows_mixed, col_inv, preferred_element_type=F32)
    intensity = jnp.sum(fields * fields, axis=0)
    resist = jax.nn.sigmoid(STEEPNESS * (intensity - THRESHOLD))
    slope = 2.0 * (resist - goal.astype(F32)) * STEEPNESS * resist * (1.0 - resist)
    grad = (2.0 * fields * slope[None]).astype(BF)
    acols = jnp.einsum("kxy,yc->kxc", grad, col_adj, preferred_element_type=F32).astype(BF)
    arows = jnp.einsum("xc,kxd->kcd", my_rows, acols, preferred_element_type=F32)
    tr = arows[:, :KB, :KB] - arows[:, KB:, KB:]
    ti = arows[:, :KB, KB:] + arows[:, KB:, :KB]
    gr = s * jnp.sum(kr * tr + ki * ti, axis=0)
    gi = s * jnp.sum(ki * tr - kr * ti, axis=0)
    return resist.astype(BF), jnp.stack([gr, gi]).astype(BF)


def back(total, own_rows):
    col_c, col_s = tables_of(PW, PW)
    col_fwd = jnp.asarray(np.concatenate([col_c, -col_s], 1), BF)
    br, bi = total[0].astype(BF), total[1].astype(BF)
    block = jnp.concatenate([jnp.concatenate([br, bi], 1), jnp.concatenate([-bi, br], 1)], 0)
    rows = jnp.dot(own_rows, block, preferred_element_type=F32).astype(BF)
    return jnp.einsum("xc,yc->xy", rows, col_fwd, preferred_element_type=F32)


def swap(x, m, size):
    return lax.ppermute(x, "src", [(i, i ^ m) for i in range(size)])


def shift(x, step, count):
    pairs = [(i, i + step) for i in range(count) if 0 <= i + step < count]
    return lax.ppermute(x, "tile", pairs)


def on_device(mask, target, start_block, zernike, source_points, source_weight, tile_slit):
    groups = lax.axis_size("tile")
    size = lax.axis_size("src")
    rank = lax.axis_index("src")
    t = rank % 2
    rows_here = mask.shape[0]
    from_left = shift(mask[:, -HALO:], 1, groups)
    from_right = shift(mask[:, :HALO], -1, groups)
    ext = jnp.concatenate([from_left, mask, from_right], axis=1)
    parts = [ext[:, :PW], ext[:, TS:]]
    pick = lambda a, b: jnp.where(t == 0, a, b)
    mine, other = pick(parts[0], parts[1]), pick(parts[1], parts[0])
    patch = jnp.concatenate([mine, swap(other, 1, size), swap(mine, 2, size), swap(other, 3, size)], axis=0)
    halves = [target[:, :TS], target[:, TS:]]
    goal = jnp.concatenate([pick(halves[0], halves[1]), swap(pick(halves[1], halves[0]), 1, size)], axis=0)
    tc, ts = tables_of(TS, TS)
    rtab = jnp.asarray(np.concatenate([tc, ts], 1), BF)
    rows_of = lambda m: lax.dynamic_slice_in_dim(rtab, rows_here * (rank ^ m), rows_here, 0)
    rr = [rows_of(m) for m in range(4)]
    full_rows = jnp.concatenate(rr, 0)
    my_rows = jnp.concatenate(rr[:2], 0)

    kern = synthesize(rank, tile_slit, zernike, source_points, source_weight, start_block)
    resist, grad = imaging(patch, goal, kern, full_rows, my_rows)
    got = swap(resist[rows_here:], 1, size)
    keep = resist[:rows_here]
    resist_out = jnp.concatenate([pick(keep, got), pick(got, keep)], axis=1)
    g1, g2, g3 = (swap(grad, m, size).astype(F32) for m in (1, 2, 3))
    tot_mine = grad.astype(F32) + g2
    tot_other = g1 + g3
    pg = [back(pick(tot_mine, tot_other), rr[0]), back(pick(tot_other, tot_mine), rr[0])]
    width = mask.shape[1]
    acc = jnp.pad(pg[0], ((0, 0), (0, width + 2 * HALO - PW))) + jnp.pad(pg[1], ((0, 0), (width + 2 * HALO - PW, 0)))
    in_left = shift(acc[:, -HALO:].astype(BF), 1, groups).astype(F32)
    in_right = shift(acc[:, :HALO].astype(BF), -1, groups).astype(F32)
    inner = acc[:, HALO : HALO + width]
    inner = inner + jnp.pad(in_left, ((0, 0), (0, width - HALO))) + jnp.pad(in_right, ((0, 0), (width - HALO, 0)))
    return (resist_out, inner.astype(BF))


def solution(mesh):
    placed = (P("src", "tile"), P("src", "tile"), P(), P(), P(), P(), P("tile"))
    return jax.shard_map(
        on_device,
        mesh=mesh,
        in_specs=placed,
        out_specs=(P("src", "tile"), P("src", "tile")),
        check_vma=False,
    )
```

```python
import math

import jax
import jax.numpy as jnp
import numpy as np
from jax import lax
from jax.experimental import pallas as pl
from jax.experimental.pallas import tpu as pltpu
from jax.sharding import PartitionSpec as P

KB = 128
NR = 24
NZ = 37
RAD = 40
SHIFT = 24
HALO = 64
ITERS = 4
TS = 256
PW = TS + 2 * HALO
GRID = 2 * SHIFT + 1
PUP = 2 * RAD + 1

STEEPNESS = 4.0
THRESHOLD = 0.5
RIDGE_SHARE = 0.001
BF = jnp.bfloat16
F32 = jnp.float32


def noll_terms(term_count):
    listing = []
    degree = 0
    while len(listing) < term_count:
        for azimuth in range(degree % 2, degree + 1, 2):
            if azimuth == 0:
                listing.append((degree, 0, 0))
            else:
                for repeat in range(2):
                    number = len(listing) + 1
                    listing.append((degree, azimuth, 2 if number % 2 == 0 else 1))
        degree += 1
    return listing[:term_count]


def radial_terms(degree, azimuth):
    powers = []
    for counter in range((degree - azimuth) // 2 + 1):
        factor = (
            (-1) ** counter
            * math.factorial(degree - counter)
            / (
                math.factorial(counter)
                * math.factorial((degree + azimuth) // 2 - counter)
                * math.factorial((degree - azimuth) // 2 - counter)
            )
        )
        powers.append((degree - 2 * counter, factor))
    return powers


def zernike_tables():
    coords = np.arange(PUP) - RAD
    row, col = np.meshgrid(coords, coords, indexing="ij")
    radius = np.sqrt(row * row + col * col) / RAD
    angle = np.arctan2(col * 1.0, row * 1.0)
    out = []
    for degree, azimuth, parity in noll_terms(NZ):
        radial = sum(factor * radius**power for power, factor in radial_terms(degree, azimuth))
        if azimuth == 0:
            out.append(math.sqrt(degree + 1.0) * radial)
        elif parity == 2:
            out.append(math.sqrt(2.0 * degree + 2.0) * radial * np.cos(azimuth * angle))
        else:
            out.append(math.sqrt(2.0 * degree + 2.0) * radial * np.sin(azimuth * angle))
    inside = row * row + col * col <= RAD * RAD
    return np.stack(out) * inside, inside.astype(np.float32)


def dft(rows, cols, sign, period=KB):
    return np.exp(sign * 2j * np.pi * np.mod(np.outer(rows, cols), period) / period)


def cmul(a, b):
    return (a[0] * b[0] - a[1] * b[1], a[0] * b[1] + a[1] * b[0])


SLOTS = 50
ROWS = SLOTS * NR
PAD = 64
HI = lax.Precision.HIGHEST


def real_form(table):
    return np.block([[table.real, -table.imag], [table.imag, table.real]])


def split(table):
    high = table.astype(np.float32).astype(jnp.bfloat16)
    low = (table - high.astype(np.float64)).astype(jnp.bfloat16)
    return high, low


def block_tables():
    freq = np.arange(KB)
    big = real_form(dft(freq, np.arange(KB) - KB // 2, -1))
    offs = np.zeros((KB, PAD), np.complex128)
    offs[:, :GRID] = dft(freq, np.arange(GRID) - SHIFT, 1)
    small = real_form(offs)
    rev = np.zeros((PAD, KB), np.float32)
    for spot in range(GRID):
        rev[spot, KB // 2 + SHIFT - spot] = 1.0
    lb, lb_lo = split(big)
    lbt, lbt_lo = split(big.T.copy())
    lc, lc_lo = split(small)
    lct, lct_lo = split(small.T.copy())
    wide = lambda a, b: np.concatenate([a, b], axis=1)
    tall = lambda a, b: np.concatenate([a, b], axis=0)
    return (lb, lbt, lc, lct, tall(lct, lct_lo), wide(lc, lc_lo), lbt_lo, lb_lo, rev.astype(jnp.bfloat16), rev.T.copy().astype(jnp.bfloat16))


def mm(a, b):
    return jnp.dot(a, b, preferred_element_type=F32)


def nt(a, b, precision=None):
    return lax.dot_general(a, b, (((1,), (1,)), ((), ())), precision=precision, preferred_element_type=F32)


def lanes(shape):
    return lax.broadcasted_iota(jnp.int32, shape, 1)


def sublanes(shape):
    return lax.broadcasted_iota(jnp.int32, shape, 0)


def factor(gram, floor):
    eye = (sublanes((NR, PAD)) == lanes((NR, PAD))).astype(F32)
    work = jnp.concatenate([gram, jnp.zeros((NR, PAD - NR), F32), eye], axis=1)
    row_no = sublanes((NR, 1))
    diag = jnp.zeros((NR, 1), F32)
    for k in range(NR):
        row = work[k : k + 1, :]
        col = work[:, k : k + 1]
        pivot = jnp.maximum(col[k : k + 1, :], floor)
        diag = jnp.where(row_no == k, pivot, diag)
        ratio = jnp.where(row_no > k, col / pivot, 0.0)
        work = work - ratio * row
    scale = lax.rsqrt(diag)
    return work[:, :NR] * scale, work[:, PAD : PAD + NR] * scale


def synth_kernel(rank_ref, slit_ref, zern_ref, sp_ref, sw_ref, zt_ref, ins_ref, b0_ref, lb, lbt, lc, lct, lct2, lc2, lbt_lo, lb_lo, rev, revt, out_ref, pup, hat, a1, f2, ab, c_ref, h_ref, wf, bx, c2):
    slit = slit_ref[lax.rem(rank_ref[0], 2)]
    turns = jnp.zeros((96, KB), F32)
    for z in range(NZ):
        turns = turns + zern_ref[slit, z] * zt_ref[z]
    turns = turns - jnp.floor(turns + 0.5)
    half = math.pi * turns
    sq = half * half
    sine = jnp.full_like(half, 1.0 / math.factorial(15))
    for n in (13, 11, 9, 7, 5, 3, 1):
        sine = 1.0 / math.factorial(n) - sine * sq
    sine = sine * half
    cosine = jnp.full_like(half, 1.0 / math.factorial(14))
    for n in (12, 10, 8, 6, 4, 2, 0):
        cosine = 1.0 / math.factorial(n) - cosine * sq
    pr = ins_ref[...] * (1.0 - 2.0 * sine * sine)
    pi = ins_ref[...] * (2.0 * sine * cosine)
    spot = lambda a, i, j: a[i : i + 1, j : j + 1]
    q1r, q1i = spot(pr, 88, 64), spot(pi, 88, 64)
    m1r, m1i = spot(pr, 8, 64), spot(pi, 8, 64)
    q2r, q2i = spot(pr, 48, 104), spot(pi, 48, 104)
    m2r, m2i = spot(pr, 48, 24), spot(pi, 48, 24)
    z1r, z1i = q1r * m1r + q1i * m1i, q1r * m1i - q1i * m1r
    z2r, z2i = q2r * m2r + q2i * m2i, q2r * m2i - q2i * m2r
    edge = jnp.zeros((16, 2 * KB), F32)
    both = jnp.concatenate([edge, jnp.concatenate([pr, pi], axis=1), edge], axis=0).astype(BF)
    ph = mm(both, lbt[...])
    stacked = jnp.concatenate([ph[:, :KB], ph[:, KB:]], axis=0).astype(BF)
    ph = mm(lb[...], stacked)
    hr, hi = ph[:KB], ph[KB:]
    hat[0] = jnp.concatenate([hr, hr], axis=1) / (KB * KB)
    hat[1] = jnp.concatenate([hi, hi], axis=1) / (KB * KB)
    power = (hr * hr + hi * hi) / (KB * KB)
    power = jnp.concatenate([power, power], axis=1)
    hat[2] = power

    weights = sw_ref[...]
    weights = weights / (math.pi * RAD * RAD * jnp.sum(weights, axis=1, keepdims=True))
    count = sp_ref.shape[0]
    lane = lanes((count, KB))
    hot_x = (lane - SHIFT == sp_ref[:, 0:1]).astype(F32)
    hot_y = (jnp.where(lane >= PAD, lane - PAD, lane) - SHIFT == sp_ref[:, 1:2]).astype(F32)
    wmap = jnp.dot(hot_x.T * weights, hot_y, precision=HI, preferred_element_type=F32)
    for s in range(SLOTS):
        wf[s * NR : (s + 1) * NR, :] = jnp.broadcast_to(wmap[s : s + 1, :], (NR, KB))

    rs, cs = sublanes((KB, KB)), lanes((KB, KB))
    at = lambda i, j, v: jnp.where((rs == i) & (cs == j), v, 0.0)
    one = jnp.ones((1, 1), F32)
    top = 2 * SHIFT
    ky = (
        at(0, 0, one) + at(PAD, PAD, one)
        + at(top, 0, z2r) + at(PAD + top, 0, -z2i) + at(top, PAD, z2i) + at(PAD + top, PAD, z2r)
        + at(0, top, z2r) + at(PAD, top, z2i) + at(0, PAD + top, -z2i) + at(PAD, PAD + top, z2r)
    ).astype(BF)
    kq0 = jnp.concatenate([at(0, 0, q2r) + at(0, PAD, -q2i), at(0, 0, q2i) + at(0, PAD, q2r)], axis=0).astype(BF)
    kq2 = jnp.concatenate([at(0, 0, q2r) + at(PAD, 0, -q2i), at(0, 0, q2i) + at(PAD, 0, q2r)], axis=1).astype(BF)

    a1[:, ROWS:, :] = jnp.zeros((2, PAD * NR - ROWS, KB), F32)

    def pack(x0, x1):
        return jnp.concatenate(
            [jnp.concatenate([x0[:, :KB], x1[:, :KB]], axis=1), jnp.concatenate([x0[:, KB:], x1[:, KB:]], axis=1)], axis=0
        )

    def unpack(y, height):
        return (
            jnp.concatenate([y[:height, :KB], y[height:, :KB]], axis=1),
            jnp.concatenate([y[:height, KB:], y[height:, KB:]], axis=1),
        )

    def put(ref, k, x):
        ref[0, pl.ds(k, PAD, stride=NR), :] = x[:, :KB]
        ref[1, pl.ds(k, PAD, stride=NR), :] = x[:, KB:]

    def get(ref, k):
        return jnp.concatenate([ref[0, pl.ds(k, PAD, stride=NR), :], ref[1, pl.ds(k, PAD, stride=NR), :]], axis=1)

    def both_halves(ref):
        return jnp.concatenate([ref[0, :ROWS, :], ref[1, :ROWS, :]], axis=1).astype(BF)

    prow = sublanes((KB, 2 * KB))
    urow = sublanes((2 * KB, 2 * KB))

    def start(p, carry):
        k = 2 * p
        parts = []
        for step in range(2):
            block = jnp.concatenate([b0_ref[0, k + step], b0_ref[1, k + step]], axis=1).astype(BF)
            put(bx, k + step, mm(rev[...], block))
            parts.append(mm(block, lbt[...]))
        x = pack(parts[0], parts[1])
        y = mm(lb[...], x.astype(BF))
        yr, yi = y[:KB], y[KB:]
        y = jnp.concatenate([hat[0] * yr + hat[1] * yi, hat[0] * yi - hat[1] * yr], axis=0)
        d = mm(lct[...], y.astype(BF))
        xr, xi = x[0:1], x[KB : KB + 1]
        cr, ci = (q1r * xr + q1i * xi) / KB, (q1r * xi - q1i * xr) / KB
        d = d - jnp.where(prow == 0, cr, 0.0) - jnp.where(prow == PAD, ci, 0.0)
        d0, d1 = unpack(d, PAD)
        put(f2, k, d0)
        put(f2, k + 1, d1)
        return carry

    lax.fori_loop(0, NR // 2, start, 0)
    first = mm(both_halves(f2), lc[...]) - mm(both_halves(bx), kq0)
    c_ref[...] = wf[...] * first

    def wide(ref):
        return jnp.concatenate([ref[s * NR : (s + 1) * NR, :] for s in range(SLOTS)], axis=1)

    def tallput(ref, x):
        for s in range(SLOTS):
            ref[s * NR : (s + 1) * NR, :] = x[:, s * KB : (s + 1) * KB]

    def forward(p):
        return pack(get(a1, 2 * p), get(a1, 2 * p + 1)).astype(BF)

    def middle(p, carry):
        y = mm(lc[...], forward(p))
        y = jnp.concatenate([hat[2] * y[:KB], hat[2] * y[KB:]], axis=0)
        d0, d1 = unpack(mm(lct[...], y.astype(BF)), PAD)
        put(f2, 2 * p, d0)
        put(f2, 2 * p + 1, d1)
        return carry

    def apply():
        coef = c_ref[...].astype(BF)
        full = mm(coef, lct[...])
        a1[0, :ROWS, :] = full[:, :KB]
        a1[1, :ROWS, :] = full[:, KB:]
        lax.fori_loop(0, NR // 2, middle, 0)
        last = slice(top * NR, (top + 1) * NR)
        lr, li, ur, ui = a1[0, 0:NR, :], a1[1, 0:NR, :], a1[0, last, :], a1[1, last, :]
        f2[0, 0:NR, :] = f2[0, 0:NR, :] - (lr + z1r * ur - z1i * ui) / KB
        f2[1, 0:NR, :] = f2[1, 0:NR, :] - (li + z1r * ui + z1i * ur) / KB
        f2[0, last, :] = f2[0, last, :] - (z1r * lr + z1i * li) / KB
        f2[1, last, :] = f2[1, last, :] - (z1r * li - z1i * lr) / KB
        h_ref[...] = mm(both_halves(f2), lc[...]) - mm(coef, ky)
        gram = nt(wide(c_ref), wide(h_ref), HI)
        gram = 0.5 * (gram + gram.T)
        eye = sublanes((NR, NR)) == lanes((NR, NR))
        trace = jnp.sum(jnp.sum(jnp.where(eye, gram, 0.0), axis=1, keepdims=True), axis=0, keepdims=True)
        return factor(gram + jnp.where(eye, RIDGE_SHARE * trace / NR + 1e-06, 0.0), 0.0)[1]

    def step(iteration, carry):
        inverse = apply()
        new = jnp.dot(inverse, wide(h_ref), precision=HI, preferred_element_type=F32)
        tallput(h_ref, new)
        c_ref[...] = wf[...] * h_ref[...]
        return carry

    lax.fori_loop(0, ITERS - 1, step, 0)
    inverse = apply()
    f2[0, :ROWS, :] = wf[...] * h_ref[...]
    moment = nt(jnp.concatenate([f2[0, s * NR : (s + 1) * NR, :] for s in range(SLOTS)], axis=1), wide(h_ref), HI)
    moment = jnp.dot(inverse, moment, precision=HI, preferred_element_type=F32)
    mixing = nt(moment, inverse, HI)
    mixing = 0.5 * (mixing + mixing.T)
    eye = sublanes((NR, NR)) == lanes((NR, NR))
    trace = jnp.sum(jnp.sum(jnp.where(eye, mixing, 0.0), axis=1, keepdims=True), axis=0, keepdims=True)
    root = factor(mixing, 1e-6 * trace + 1e-30)[0]
    combine = jnp.dot(root, inverse, precision=HI, preferred_element_type=F32)
    tallput(c_ref, jnp.dot(combine, wide(c_ref), precision=HI, preferred_element_type=F32))
    coef = c_ref[...].astype(BF)
    full = mm(jnp.concatenate([coef, coef], axis=1), lct2[...])
    a1[0, :ROWS, :] = full[:, :KB]
    a1[1, :ROWS, :] = full[:, KB:]
    c2[:ROWS, :] = c_ref[...]
    c2[ROWS:, :] = jnp.zeros((PAD * NR - ROWS, KB), F32)

    def finish(p, carry):
        k = 2 * p
        x = pack(get(a1, k), get(a1, k + 1))
        xb = x.astype(BF)
        y = mm(lc2[...], jnp.concatenate([xb, xb], axis=0))
        yr, yi = y[:KB], y[KB:]
        y = jnp.concatenate([hat[0] * yr - hat[1] * yi, hat[0] * yi + hat[1] * yr], axis=0).astype(BF)
        u = mm(lbt[...], y) + mm(lbt_lo[...], y)
        xr, xi = x[0:1], x[PAD : PAD + 1]
        cr, ci = (q1r * xr - q1i * xi) / KB, (q1r * xi + q1i * xr) / KB
        u = u - jnp.where(urow == 0, cr, 0.0) - jnp.where(urow == KB, ci, 0.0)
        pair = unpack(u, KB)
        for step in range(2):
            cols = mm(revt[...], c2[pl.ds(k + step, PAD, stride=NR), :].astype(BF))
            ub = pair[step].astype(BF)
            kern = mm(ub, lb[...]) + mm(ub, lb_lo[...]) - mm(cols.astype(BF), kq2)
            out_ref[k + step] = kern.astype(BF)
        return carry

    lax.fori_loop(0, NR // 2, finish, 0)


def synthesize(rank, tile_slit, zernike, source_points, source_weight, start_block):
    ztab, inside = zernike_tables()
    wide = np.zeros((NZ, 96, KB), np.float32)
    wide[:, 8:89, 24:105] = ztab
    ins = np.zeros((96, KB), np.float32)
    ins[8:89, 24:105] = inside
    smem = pl.BlockSpec(memory_space=pltpu.SMEM)
    vmem = pl.BlockSpec(memory_space=pltpu.VMEM)
    tables = [jnp.asarray(t) for t in block_tables()]
    big = (2, PAD * NR, KB)
    return pl.pallas_call(
        synth_kernel,
        out_shape=jax.ShapeDtypeStruct((NR, KB, 2 * KB), BF),
        in_specs=[smem] * 3 + [vmem] * (5 + len(tables)),
        out_specs=vmem,
        scratch_shapes=[
            pltpu.VMEM((8, KB), F32),
            pltpu.VMEM((3, KB, 2 * KB), F32),
            pltpu.VMEM(big, F32),
            pltpu.VMEM(big, F32),
            pltpu.VMEM((8, KB), F32),
            pltpu.VMEM((ROWS, KB), F32),
            pltpu.VMEM((ROWS, KB), F32),
            pltpu.VMEM((ROWS, KB), F32),
            pltpu.VMEM(big, F32),
            pltpu.VMEM((PAD * NR, KB), F32),
        ],
    )(rank.reshape(1), tile_slit, zernike, source_points, source_weight.reshape(1, -1), jnp.asarray(wide), jnp.asarray(ins), start_block, *tables)


def tables_of(count, period):
    t = dft(np.arange(count), np.arange(KB) - KB // 2, 1, period)
    return t.real.astype(np.float32), t.imag.astype(np.float32)


def image_tables():
    rc, rs = tables_of(TS, TS)
    cc, cs = tables_of(PW, PW)
    fwd = np.concatenate([cc, -cs], 1)
    cast = lambda x: np.ascontiguousarray(x).astype(jnp.bfloat16)
    rows_t = np.concatenate([rc, rs], 1).T
    row_half = np.concatenate([rc, rs], 1).reshape(2, KB, 2 * KB)
    turn = np.stack([np.concatenate([rc[i : i + KB].T, rs[i : i + KB].T], 1) for i in (0, KB)])
    inv_t = fwd[HALO : HALO + TS].T
    adj = np.concatenate([cc, cs], 1)[HALO : HALO + TS]
    return tuple(cast(x) for x in (fwd, rows_t, row_half, turn, inv_t, adj))


def back_tables():
    rc, rs = tables_of(TS, TS)
    cc, cs = tables_of(PW, PW)
    fwd_t = np.concatenate([cc, -cs], 1).T
    cols = np.zeros((2, 2 * KB, 5 * KB), np.float32)
    cols[0, :, : PW - HALO] = fwd_t[:, HALO:]
    cols[0, :, 2 * TS : 2 * TS + HALO] = fwd_t[:, :HALO]
    cols[1, :, 2 * TS - PW + HALO : 2 * TS] = fwd_t[:, : PW - HALO]
    cols[1, :, 2 * TS + HALO :] = fwd_t[:, PW - HALO :]
    cast = lambda x: np.ascontiguousarray(x).astype(jnp.bfloat16)
    return cast(np.concatenate([rc, rs], 1)), cast(cols.reshape(4 * KB, 5 * KB))


def image_kernel(rank_ref, p0, p1, p2, p3, g0, g1, kern_ref, fwd, rows_t, row_half, turn, inv_t, adj, keep_ref, send_ref, grad_ref, patch, goal, fields):
    rank = rank_ref[0]
    t, h = lax.rem(rank, 2), lax.div(rank, 2)
    quarter = p0.shape[0]
    spot = lambda a, b: pl.ds(pl.multiple_of((2 * a + b) * quarter, quarter), quarter)
    patch[spot(h, t), :] = p0[...]
    patch[spot(h, 1 - t), :] = p1[...]
    patch[spot(1 - h, t), :] = p2[...]
    patch[spot(1 - h, 1 - t), :] = p3[...]
    goal[spot(0, t), :] = g0[...]
    goal[spot(0, 1 - t), :] = g1[...]
    s = 1.0 / math.sqrt(TS * PW)
    columns = mm(patch[...], fwd[...]).astype(BF)
    sums = mm(rows_t[...], columns)
    sr = s * (sums[:KB, :KB] + sums[KB:, KB:])
    si = s * (sums[:KB, KB:] - sums[KB:, :KB])
    rows = row_half[h]
    inten = jnp.zeros((KB, TS), F32)
    for k in range(NR):
        kr, ki = kern_ref[k, :, :KB].astype(F32), kern_ref[k, :, KB:].astype(F32)
        wr, wi = kr * sr + ki * si, kr * si - ki * sr
        block = jnp.concatenate([jnp.concatenate([wr, wi], axis=1), jnp.concatenate([-wi, wr], axis=1)], axis=0).astype(BF)
        field = mm(mm(rows, block).astype(BF), inv_t[...])
        fields[k] = field
        inten = inten + field * field
    resist = 1.0 / (1.0 + jnp.exp(-STEEPNESS * (inten - THRESHOLD)))
    goal_f = goal[...].astype(F32)
    slope = 4.0 * (resist - goal_f) * STEEPNESS * resist * (1.0 - resist)
    goal[...] = resist.astype(BF)
    keep_ref[...] = goal[spot(0, t), :]
    send_ref[...] = goal[spot(0, 1 - t), :]
    back = turn[h]
    gr = jnp.zeros((KB, KB), F32)
    gi = jnp.zeros((KB, KB), F32)
    for k in range(NR):
        cols = mm((fields[k] * slope).astype(BF), adj[...])
        cr, ci = cols[:, :KB], cols[:, KB:]
        block = jnp.concatenate([cols, jnp.concatenate([-ci, cr], axis=1)], axis=0).astype(BF)
        turned = mm(back, block)
        tr, ti = turned[:, :KB], turned[:, KB:]
        kr, ki = kern_ref[k, :, :KB].astype(F32), kern_ref[k, :, KB:].astype(F32)
        gr = gr + kr * tr + ki * ti
        gi = gi + ki * tr - kr * ti
    grad_ref[...] = (s * jnp.concatenate([gr, gi], axis=1)).astype(BF)


def imaging(rank, patches, goals, kern):
    quarter = patches[0].shape[0]
    smem = pl.BlockSpec(memory_space=pltpu.SMEM)
    vmem = pl.BlockSpec(memory_space=pltpu.VMEM)
    tables = [jnp.asarray(x) for x in image_tables()]
    return pl.pallas_call(
        image_kernel,
        out_shape=(
            jax.ShapeDtypeStruct((quarter, TS), BF),
            jax.ShapeDtypeStruct((quarter, TS), BF),
            jax.ShapeDtypeStruct((KB, 2 * KB), BF),
        ),
        in_specs=[smem] + [vmem] * (7 + len(tables)),
        out_specs=(vmem, vmem, vmem),
        scratch_shapes=[
            pltpu.VMEM((TS, PW), BF),
            pltpu.VMEM((2 * quarter, TS), BF),
            pltpu.VMEM((NR, 2 * quarter, TS), F32),
        ],
    )(rank.reshape(1), *patches, *goals, kern, *tables)


def back_kernel(rank_ref, own, got1, got2, got3, row_tab, cols, inner_ref, rim_ref):
    rank = rank_ref[0]
    quarter = inner_ref.shape[0]
    first = lax.rem(rank, 2) == 0
    mine = own[...].astype(F32) + got2[...].astype(F32)
    other = got1[...].astype(F32) + got3[...].astype(F32)
    rows = row_tab[pl.ds(pl.multiple_of(rank * quarter, quarter), quarter), :]
    parts = []
    for total in (jnp.where(first, mine, other), jnp.where(first, other, mine)):
        br, bi = total[:, :KB], total[:, KB:]
        block = jnp.concatenate([total, jnp.concatenate([-bi, br], axis=1)], axis=0).astype(BF)
        parts.append(mm(rows, block))
    result = mm(jnp.concatenate(parts, axis=1).astype(BF), cols[...])
    inner_ref[...] = result[:, : 4 * KB]
    rim_ref[...] = result[:, 4 * KB :].astype(BF)


def back(rank, grads, quarter):
    smem = pl.BlockSpec(memory_space=pltpu.SMEM)
    vmem = pl.BlockSpec(memory_space=pltpu.VMEM)
    tables = [jnp.asarray(x) for x in back_tables()]
    return pl.pallas_call(
        back_kernel,
        out_shape=(jax.ShapeDtypeStruct((quarter, 2 * TS), F32), jax.ShapeDtypeStruct((quarter, 2 * HALO), BF)),
        in_specs=[smem] + [vmem] * (4 + len(tables)),
        out_specs=(vmem, vmem),
    )(rank.reshape(1), *grads, *tables)


def swap(x, m, size):
    return lax.ppermute(x, "src", [(i, i ^ m) for i in range(size)])


def shift(x, step, count):
    pairs = [(i, i + step) for i in range(count) if 0 <= i + step < count]
    return lax.ppermute(x, "tile", pairs)


def on_device(mask, target, start_block, zernike, source_points, source_weight, tile_slit):
    groups = lax.axis_size("tile")
    size = lax.axis_size("src")
    rank = lax.axis_index("src").astype(jnp.int32)
    t = rank % 2
    rows_here, width = mask.shape
    from_left = shift(mask[:, -HALO:], 1, groups)
    from_right = shift(mask[:, :HALO], -1, groups)
    ext = jnp.concatenate([from_left, mask, from_right], axis=1)
    parts = [ext[:, :PW], ext[:, TS:]]
    pick = lambda a, b: jnp.where(t == 0, a, b)
    mine, other = pick(parts[0], parts[1]), pick(parts[1], parts[0])
    patches = [mine, swap(other, 1, size), swap(mine, 2, size), swap(other, 3, size)]
    halves = [target[:, :TS], target[:, TS:]]
    goals = [pick(halves[0], halves[1]), swap(pick(halves[1], halves[0]), 1, size)]
    kern = synthesize(rank, tile_slit, zernike, source_points, source_weight, start_block)
    keep, send, grad = imaging(rank, patches, goals, kern)
    got = swap(send, 1, size)
    resist_out = jnp.concatenate([pick(keep, got), pick(got, keep)], axis=1)
    inner, rims = back(rank, [grad] + [swap(grad, m, size) for m in (1, 2, 3)], rows_here)
    in_left = shift(rims[:, HALO:], 1, groups).astype(F32)
    in_right = shift(rims[:, :HALO], -1, groups).astype(F32)
    inner = inner + jnp.pad(in_left, ((0, 0), (0, width - HALO))) + jnp.pad(in_right, ((0, 0), (width - HALO, 0)))
    return (resist_out, inner.astype(BF))


def solution(mesh):
    placed = (P("src", "tile"), P("src", "tile"), P(), P(), P(), P(), P("tile"))
    return jax.shard_map(
        on_device,
        mesh=mesh,
        in_specs=placed,
        out_specs=(P("src", "tile"), P("src", "tile")),
        check_vma=False,
    )
```

```python
import math

import jax
import jax.numpy as jnp
import numpy as np
from jax import lax
from jax.experimental import pallas as pl
from jax.experimental.pallas import tpu as pltpu
from jax.sharding import PartitionSpec as P

KB = 128
NR = 24
NZ = 37
RAD = 40
SHIFT = 24
HALO = 64
ITERS = 4
TS = 256
PW = TS + 2 * HALO
GRID = 2 * SHIFT + 1
PUP = 2 * RAD + 1

STEEPNESS = 4.0
THRESHOLD = 0.5
RIDGE_SHARE = 0.001
BF = jnp.bfloat16
F32 = jnp.float32


def noll_terms(term_count):
    listing = []
    degree = 0
    while len(listing) < term_count:
        for azimuth in range(degree % 2, degree + 1, 2):
            if azimuth == 0:
                listing.append((degree, 0, 0))
            else:
                for repeat in range(2):
                    number = len(listing) + 1
                    listing.append((degree, azimuth, 2 if number % 2 == 0 else 1))
        degree += 1
    return listing[:term_count]


def radial_terms(degree, azimuth):
    powers = []
    for counter in range((degree - azimuth) // 2 + 1):
        factor = (
            (-1) ** counter
            * math.factorial(degree - counter)
            / (
                math.factorial(counter)
                * math.factorial((degree + azimuth) // 2 - counter)
                * math.factorial((degree - azimuth) // 2 - counter)
            )
        )
        powers.append((degree - 2 * counter, factor))
    return powers


def zernike_tables():
    coords = np.arange(PUP) - RAD
    row, col = np.meshgrid(coords, coords, indexing="ij")
    radius = np.sqrt(row * row + col * col) / RAD
    angle = np.arctan2(col * 1.0, row * 1.0)
    out = []
    for degree, azimuth, parity in noll_terms(NZ):
        radial = sum(factor * radius**power for power, factor in radial_terms(degree, azimuth))
        if azimuth == 0:
            out.append(math.sqrt(degree + 1.0) * radial)
        elif parity == 2:
            out.append(math.sqrt(2.0 * degree + 2.0) * radial * np.cos(azimuth * angle))
        else:
            out.append(math.sqrt(2.0 * degree + 2.0) * radial * np.sin(azimuth * angle))
    inside = row * row + col * col <= RAD * RAD
    return np.stack(out) * inside, inside.astype(np.float32)


def dft(rows, cols, sign, period=KB):
    return np.exp(sign * 2j * np.pi * np.mod(np.outer(rows, cols), period) / period)


def cmul(a, b):
    return (a[0] * b[0] - a[1] * b[1], a[0] * b[1] + a[1] * b[0])


SLOTS = 50
ROWS = SLOTS * NR
PAD = 64
HI = lax.Precision.HIGHEST
UNROLL = 6
UNROLL_S = 4
UNROLL_F = 4


def real_form(table):
    return np.block([[table.real, -table.imag], [table.imag, table.real]])


def split(table):
    high = table.astype(np.float32).astype(jnp.bfloat16)
    low = (table - high.astype(np.float64)).astype(jnp.bfloat16)
    return high, low


def block_tables():
    freq = np.arange(KB)
    big = real_form(dft(freq, np.arange(KB) - KB // 2, -1))
    offs = np.zeros((KB, PAD), np.complex128)
    offs[:, :GRID] = dft(freq, np.arange(GRID) - SHIFT, 1)
    small = real_form(offs)
    rev = np.zeros((PAD, KB), np.float32)
    for spot in range(GRID):
        rev[spot, KB // 2 + SHIFT - spot] = 1.0
    lb, lb_lo = split(big)
    lbt, lbt_lo = split(big.T.copy())
    lc, lc_lo = split(small)
    lct, lct_lo = split(small.T.copy())
    wide = lambda a, b: np.concatenate([a, b], axis=1)
    tall = lambda a, b: np.concatenate([a, b], axis=0)
    return (lb, lbt, lc, lct, tall(lct, lct_lo), wide(lc, lc_lo), lbt_lo, lb_lo, rev.astype(jnp.bfloat16), rev.T.copy().astype(jnp.bfloat16))


def mm(a, b):
    return jnp.dot(a, b, preferred_element_type=F32)


def nt(a, b, precision=None):
    return lax.dot_general(a, b, (((1,), (1,)), ((), ())), precision=precision, preferred_element_type=F32)


def lanes(shape):
    return lax.broadcasted_iota(jnp.int32, shape, 1)


def sublanes(shape):
    return lax.broadcasted_iota(jnp.int32, shape, 0)


def halves(x):
    high = x.astype(BF)
    return high, (x - high.astype(F32)).astype(BF)


def fine_nt(a, b):
    ah, al = halves(a)
    bh, bl = halves(b)
    return nt(ah, bh) + nt(ah, bl) + nt(al, bh)


def fine_mm(a, b):
    ah, al = (x.astype(F32) for x in halves(a))
    bh, bl = (x.astype(F32) for x in halves(b))
    return mm(jnp.concatenate([ah, al, ah], axis=1).astype(BF), jnp.concatenate([bh, bh, bl], axis=0).astype(BF))


def factor(gram, floor):
    tile, blocks = 8, NR // 8
    rows = [slice(b * tile, (b + 1) * tile) for b in range(blocks)]
    wide_eye = (sublanes((NR, PAD)) == lanes((NR, PAD))).astype(F32)
    start = jnp.concatenate([gram, jnp.zeros((NR, PAD - NR), F32), wide_eye], axis=1)
    work = [start[x] for x in rows]
    col = [[jnp.broadcast_to(gram[x, j : j + 1], (tile, KB)) for x in rows] for j in range(NR)]
    row_no = sublanes((tile, KB))
    diag = [jnp.zeros((tile, KB), F32) for _ in rows]
    for k in range(NR):
        b0, r0 = divmod(k, tile)
        pick = lambda x: jnp.broadcast_to(x[r0 : r0 + 1, :], (tile, KB))
        pivot = jnp.maximum(pick(col[k][b0]), floor)
        diag[b0] = jnp.where(row_no == r0, pivot, diag[b0])
        inv = 1.0 / pivot
        ratio = [c * inv for c in col[k]]
        lead = pick(work[b0])
        for j in range(k + 1, NR):
            entry = pick(col[j][b0])
            for b in range(b0, blocks):
                col[j][b] = col[j][b] - ratio[b] * entry
        for b in range(b0, blocks):
            part = ratio[b] if b > b0 else jnp.where(row_no > r0, ratio[b], 0.0)
            work[b] = work[b] - part * lead
    done = jnp.concatenate([w * lax.rsqrt(d) for w, d in zip(work, diag)], axis=0)
    return done[:, :NR], done[:, PAD : PAD + NR]


def synth_kernel(rank_ref, slit_ref, zern_ref, sp_ref, sw_ref, zt_ref, ins_ref, b0_ref, lb, lbt, lc, lct, lct2, lc2, lbt_lo, lb_lo, rev, revt, out_ref, inv_ref, hat, a1, f2, c_ref, h_ref, wf, bx, c2):
    slit = slit_ref[lax.rem(rank_ref[0], 2)]
    turns = jnp.zeros((96, KB), F32)
    for z in range(NZ):
        turns = turns + zern_ref[slit, z] * zt_ref[z]
    turns = turns - jnp.floor(turns + 0.5)
    half = math.pi * turns
    sq = half * half
    sine = jnp.full_like(half, 1.0 / math.factorial(15))
    for n in (13, 11, 9, 7, 5, 3, 1):
        sine = 1.0 / math.factorial(n) - sine * sq
    sine = sine * half
    cosine = jnp.full_like(half, 1.0 / math.factorial(14))
    for n in (12, 10, 8, 6, 4, 2, 0):
        cosine = 1.0 / math.factorial(n) - cosine * sq
    pr = ins_ref[...] * (1.0 - 2.0 * sine * sine)
    pi = ins_ref[...] * (2.0 * sine * cosine)
    spot = lambda a, i, j: a[i : i + 1, j : j + 1]
    q1r, q1i = spot(pr, 88, 64), spot(pi, 88, 64)
    m1r, m1i = spot(pr, 8, 64), spot(pi, 8, 64)
    q2r, q2i = spot(pr, 48, 104), spot(pi, 48, 104)
    m2r, m2i = spot(pr, 48, 24), spot(pi, 48, 24)
    z1r, z1i = q1r * m1r + q1i * m1i, q1r * m1i - q1i * m1r
    z2r, z2i = q2r * m2r + q2i * m2i, q2r * m2i - q2i * m2r
    edge = jnp.zeros((16, 2 * KB), F32)
    both = jnp.concatenate([edge, jnp.concatenate([pr, pi], axis=1), edge], axis=0).astype(BF)
    ph = mm(both, lbt[...])
    stacked = jnp.concatenate([ph[:, :KB], ph[:, KB:]], axis=0).astype(BF)
    ph = mm(lb[...], stacked)
    hr, hi = ph[:KB], ph[KB:]
    hat[0] = jnp.concatenate([hr, hr], axis=1) / (KB * KB)
    hat[1] = jnp.concatenate([hi, hi], axis=1) / (KB * KB)
    power = (hr * hr + hi * hi) / (KB * KB)
    power = jnp.concatenate([power, power], axis=1)
    hat[2] = power

    weights = sw_ref[...]
    weights = weights / (math.pi * RAD * RAD * jnp.sum(weights, axis=1, keepdims=True))
    count = sp_ref.shape[1]
    offset = sublanes((KB, count))
    hot_x = jnp.where(offset - SHIFT == sp_ref[0:1, :], weights, 0.0)
    hot_y = (jnp.where(offset >= PAD, offset - PAD, offset) - SHIFT == sp_ref[1:2, :]).astype(F32).astype(BF)
    high, low = halves(hot_x)
    wmap = nt(high, hot_y) + nt(low, hot_y)
    for s in range(SLOTS):
        wf[s * NR : (s + 1) * NR, :] = jnp.broadcast_to(wmap[s : s + 1, :], (NR, KB))

    rs, cs = sublanes((KB, KB)), lanes((KB, KB))
    at = lambda i, j, v: jnp.where((rs == i) & (cs == j), v, 0.0)
    one = jnp.ones((1, 1), F32)
    top = 2 * SHIFT
    ky = (
        at(0, 0, one) + at(PAD, PAD, one)
        + at(top, 0, z2r) + at(PAD + top, 0, -z2i) + at(top, PAD, z2i) + at(PAD + top, PAD, z2r)
        + at(0, top, z2r) + at(PAD, top, z2i) + at(0, PAD + top, -z2i) + at(PAD, PAD + top, z2r)
    ).astype(BF)
    kq0 = jnp.concatenate([at(0, 0, q2r) + at(0, PAD, -q2i), at(0, 0, q2i) + at(0, PAD, q2r)], axis=0).astype(BF)
    kq2 = jnp.concatenate([at(0, 0, q2r) + at(PAD, 0, -q2i), at(0, 0, q2i) + at(PAD, 0, q2r)], axis=1).astype(BF)

    a1[:, ROWS:, :] = jnp.zeros((2, PAD * NR - ROWS, KB), F32)

    def pack(x0, x1):
        return jnp.concatenate(
            [jnp.concatenate([x0[:, :KB], x1[:, :KB]], axis=1), jnp.concatenate([x0[:, KB:], x1[:, KB:]], axis=1)], axis=0
        )

    def unpack(y, height):
        return (
            jnp.concatenate([y[:height, :KB], y[height:, :KB]], axis=1),
            jnp.concatenate([y[:height, KB:], y[height:, KB:]], axis=1),
        )

    def put(ref, k, x):
        ref[0, pl.ds(k, PAD, stride=NR), :] = x[:, :KB]
        ref[1, pl.ds(k, PAD, stride=NR), :] = x[:, KB:]

    def get(ref, k):
        return jnp.concatenate([ref[0, pl.ds(k, PAD, stride=NR), :], ref[1, pl.ds(k, PAD, stride=NR), :]], axis=1)

    def both_halves(ref):
        return jnp.concatenate([ref[0, :ROWS, :], ref[1, :ROWS, :]], axis=1).astype(BF)

    prow = sublanes((KB, 2 * KB))
    urow = sublanes((2 * KB, 2 * KB))

    def start(q, carry):
        pairs = [q * UNROLL_S + j for j in range(UNROLL_S)]
        blocks = [[jnp.concatenate([b0_ref[0, 2 * p + e], b0_ref[1, 2 * p + e]], axis=1).astype(BF) for e in range(2)] for p in pairs]
        xs = [pack(mm(b[0], lbt[...]), mm(b[1], lbt[...])) for b in blocks]
        revs = [[mm(rev[...], e) for e in b] for b in blocks]
        ys = [mm(lb[...], x.astype(BF)) for x in xs]
        ys = [jnp.concatenate([hat[0] * y[:KB] + hat[1] * y[KB:], hat[0] * y[KB:] - hat[1] * y[:KB]], axis=0).astype(BF) for y in ys]
        ds = [mm(lct[...], y) for y in ys]
        for p, x, d, rv in zip(pairs, xs, ds, revs):
            xr, xi = x[0:1], x[KB : KB + 1]
            cr, ci = (q1r * xr + q1i * xi) / KB, (q1r * xi - q1i * xr) / KB
            d = d - jnp.where(prow == 0, cr, 0.0) - jnp.where(prow == PAD, ci, 0.0)
            d0, d1 = unpack(d, PAD)
            put(f2, 2 * p, d0)
            put(f2, 2 * p + 1, d1)
            put(bx, 2 * p, rv[0])
            put(bx, 2 * p + 1, rv[1])
        return carry

    lax.fori_loop(0, NR // 2 // UNROLL_S, start, 0)
    first = mm(both_halves(f2), lc[...]) - mm(both_halves(bx), kq0)
    c_ref[...] = wf[...] * first

    def wide(ref):
        return jnp.concatenate([ref[s * NR : (s + 1) * NR, :] for s in range(SLOTS)], axis=1)

    def tallput(ref, x):
        for s in range(SLOTS):
            ref[s * NR : (s + 1) * NR, :] = x[:, s * KB : (s + 1) * KB]

    def forward(p):
        return pack(get(a1, 2 * p), get(a1, 2 * p + 1)).astype(BF)

    def middle(q, carry):
        pairs = [q * UNROLL + j for j in range(UNROLL)]
        ys = [mm(lc[...], forward(p)) for p in pairs]
        ys = [jnp.concatenate([hat[2] * y[:KB], hat[2] * y[KB:]], axis=0).astype(BF) for y in ys]
        ds = [mm(lct[...], y) for y in ys]
        for p, d in zip(pairs, ds):
            d0, d1 = unpack(d, PAD)
            put(f2, 2 * p, d0)
            put(f2, 2 * p + 1, d1)
        return carry

    def apply():
        coef = c_ref[...].astype(BF)
        full = mm(coef, lct[...])
        a1[0, :ROWS, :] = full[:, :KB]
        a1[1, :ROWS, :] = full[:, KB:]
        lax.fori_loop(0, NR // 2 // UNROLL, middle, 0)
        last = slice(top * NR, (top + 1) * NR)
        lr, li, ur, ui = a1[0, 0:NR, :], a1[1, 0:NR, :], a1[0, last, :], a1[1, last, :]
        f2[0, 0:NR, :] = f2[0, 0:NR, :] - (lr + z1r * ur - z1i * ui) / KB
        f2[1, 0:NR, :] = f2[1, 0:NR, :] - (li + z1r * ui + z1i * ur) / KB
        f2[0, last, :] = f2[0, last, :] - (z1r * lr + z1i * li) / KB
        f2[1, last, :] = f2[1, last, :] - (z1r * li - z1i * lr) / KB
        h_ref[...] = mm(both_halves(f2), lc[...]) - mm(coef, ky)
        gram = fine_nt(wide(c_ref), wide(h_ref))
        gram = 0.5 * (gram + gram.T)
        eye = sublanes((NR, NR)) == lanes((NR, NR))
        trace = jnp.sum(jnp.sum(jnp.where(eye, gram, 0.0), axis=1, keepdims=True), axis=0, keepdims=True)
        return factor(gram + jnp.where(eye, RIDGE_SHARE * trace / NR + 1e-06, 0.0), 0.0)[1]

    def step(iteration, carry):
        @pl.when(iteration > 0)
        def _():
            tallput(h_ref, fine_mm(inv_ref[:, :NR], wide(h_ref)))
            c_ref[...] = wf[...] * h_ref[...]

        inv_ref[:, :NR] = apply()
        return carry

    lax.fori_loop(0, ITERS, step, 0)
    inverse = inv_ref[:, :NR]
    f2[0, :ROWS, :] = wf[...] * h_ref[...]
    moment = fine_nt(jnp.concatenate([f2[0, s * NR : (s + 1) * NR, :] for s in range(SLOTS)], axis=1), wide(h_ref))
    moment = jnp.dot(inverse, moment, precision=HI, preferred_element_type=F32)
    mixing = nt(moment, inverse, HI)
    mixing = 0.5 * (mixing + mixing.T)
    eye = sublanes((NR, NR)) == lanes((NR, NR))
    trace = jnp.sum(jnp.sum(jnp.where(eye, mixing, 0.0), axis=1, keepdims=True), axis=0, keepdims=True)
    root = factor(mixing, 1e-6 * trace + 1e-30)[0]
    combine = jnp.dot(root, inverse, precision=HI, preferred_element_type=F32)
    tallput(c_ref, fine_mm(combine, wide(c_ref)))
    coef = c_ref[...].astype(BF)
    full = mm(jnp.concatenate([coef, coef], axis=1), lct2[...])
    a1[0, :ROWS, :] = full[:, :KB]
    a1[1, :ROWS, :] = full[:, KB:]
    c2[:ROWS, :] = c_ref[...]
    c2[ROWS:, :] = jnp.zeros((PAD * NR - ROWS, KB), F32)

    def finish(q, carry):
        pairs = [q * UNROLL_F + j for j in range(UNROLL_F)]
        xs = [pack(get(a1, 2 * p), get(a1, 2 * p + 1)) for p in pairs]
        cols = [[mm(revt[...], c2[pl.ds(2 * p + e, PAD, stride=NR), :].astype(BF)).astype(BF) for e in range(2)] for p in pairs]
        ys = [mm(lc2[...], jnp.concatenate([x, x], axis=0).astype(BF)) for x in xs]
        ys = [jnp.concatenate([hat[0] * y[:KB] - hat[1] * y[KB:], hat[0] * y[KB:] + hat[1] * y[:KB]], axis=0).astype(BF) for y in ys]
        us = [mm(lbt[...], y) + mm(lbt_lo[...], y) for y in ys]
        for p, x, u, col in zip(pairs, xs, us, cols):
            xr, xi = x[0:1], x[PAD : PAD + 1]
            cr, ci = (q1r * xr - q1i * xi) / KB, (q1r * xi + q1i * xr) / KB
            u = u - jnp.where(urow == 0, cr, 0.0) - jnp.where(urow == KB, ci, 0.0)
            pair = unpack(u, KB)
            for e in range(2):
                ub = pair[e].astype(BF)
                out_ref[2 * p + e] = (mm(ub, lb[...]) + mm(ub, lb_lo[...]) - mm(col[e], kq2)).astype(BF)
        return carry

    lax.fori_loop(0, NR // 2 // UNROLL_F, finish, 0)


def synthesize(rank, tile_slit, zernike, source_points, source_weight, start_block):
    ztab, inside = zernike_tables()
    wide = np.zeros((NZ, 96, KB), np.float32)
    wide[:, 8:89, 24:105] = ztab
    ins = np.zeros((96, KB), np.float32)
    ins[8:89, 24:105] = inside
    smem = pl.BlockSpec(memory_space=pltpu.SMEM)
    vmem = pl.BlockSpec(memory_space=pltpu.VMEM)
    tables = [jnp.asarray(t) for t in block_tables()]
    big = (2, PAD * NR, KB)
    return pl.pallas_call(
        synth_kernel,
        out_shape=jax.ShapeDtypeStruct((NR, KB, 2 * KB), BF),
        in_specs=[smem] * 3 + [vmem] * (5 + len(tables)),
        out_specs=vmem,
        scratch_shapes=[
            pltpu.VMEM((NR, KB), F32),
            pltpu.VMEM((3, KB, 2 * KB), F32),
            pltpu.VMEM(big, F32),
            pltpu.VMEM(big, F32),
            pltpu.VMEM((ROWS, KB), F32),
            pltpu.VMEM((ROWS, KB), F32),
            pltpu.VMEM((ROWS, KB), F32),
            pltpu.VMEM(big, F32),
            pltpu.VMEM((PAD * NR, KB), F32),
        ],
    )(rank.reshape(1), tile_slit, zernike, source_points.T, source_weight.reshape(1, -1), jnp.asarray(wide), jnp.asarray(ins), start_block, *tables)


def tables_of(count, period):
    t = dft(np.arange(count), np.arange(KB) - KB // 2, 1, period)
    return t.real.astype(np.float32), t.imag.astype(np.float32)


def cast(x):
    return np.ascontiguousarray(x).astype(jnp.bfloat16)


def strip_tables():
    cc, cs = tables_of(PW, PW)
    fwd = np.concatenate([cc, -cs], 1)
    strip = np.zeros((2, 5 * KB, 2 * KB), np.float32)
    strip[0, : PW - HALO] = fwd[HALO:]
    strip[0, 2 * TS + HALO :] = fwd[:HALO]
    strip[1, 2 * TS - PW + HALO : 2 * TS] = fwd[: PW - HALO]
    strip[1, 2 * TS : 2 * TS + HALO] = fwd[PW - HALO :]
    return strip


def image_tables():
    rc, rs = tables_of(TS, TS)
    cc, cs = tables_of(PW, PW)
    fwd = np.concatenate([cc, -cs], 1)
    rows = np.concatenate([rc, rs], 1)
    turn = np.stack([np.concatenate([rc[i : i + KB].T, rs[i : i + KB].T], 1) for i in (0, KB)])
    inv_t = fwd[HALO : HALO + TS].T
    adj = np.concatenate([cc, cs], 1)[HALO : HALO + TS]
    rim = np.stack([fwd[:HALO].T, fwd[PW - HALO :].T])
    return tuple(cast(x) for x in (strip_tables(), rows.T, rows, turn, inv_t, adj, rim))


def back_tables():
    rc, rs = tables_of(TS, TS)
    strip = strip_tables()[:, : 2 * TS]
    return cast(np.concatenate([rc, rs], 1)), cast(np.concatenate([strip[0].T, strip[1].T], 0))


def image_kernel(rank_ref, m0, m1, m2, m3, e0, e1, e2, e3, g0, g1, kern_ref, strip, rows_t, rows, turn, inv_t, adj, rim, keep_ref, send_ref, grad_ref, q0, q1, q2, q3, patch, goal, fields, edge):
    rank = rank_ref[0]
    t, h = lax.rem(rank, 2), lax.div(rank, 2)
    quarter = m0.shape[0]
    first = t == 0
    block_of = lambda j: pl.ds(pl.multiple_of((rank ^ j) * quarter, quarter), quarter)
    half_of = lambda e: pl.ds(pl.multiple_of(e * quarter, quarter), quarter)
    for j, (m, e) in enumerate(((m0, e0), (m1, e1), (m2, e2), (m3, e3))):
        patch[block_of(j), : 2 * TS] = m[...]
        patch[block_of(j), 2 * TS :] = e[...]
    goal[half_of(t), :] = jnp.where(first, g0[:, :TS], g0[:, TS:])
    goal[half_of(1 - t), :] = jnp.where(first, g1[:, :TS], g1[:, TS:])
    s = 1.0 / math.sqrt(TS * PW)
    columns = mm(patch[...], strip[t]).astype(BF)
    sums = mm(rows_t[...], columns)
    sr = s * (sums[:KB, :KB] + sums[KB:, KB:])
    si = s * (sums[:KB, KB:] - sums[KB:, :KB])
    mine = rows[pl.ds(pl.multiple_of(h * KB, KB), KB), :]
    inten = jnp.zeros((KB, TS), F32)
    for k in range(NR):
        kr, ki = kern_ref[k, :, :KB].astype(F32), kern_ref[k, :, KB:].astype(F32)
        wr, wi = kr * sr + ki * si, kr * si - ki * sr
        block = jnp.concatenate([jnp.concatenate([wr, wi], axis=1), jnp.concatenate([-wi, wr], axis=1)], axis=0).astype(BF)
        field = mm(mm(mine, block).astype(BF), inv_t[...])
        fields[k] = field
        inten = inten + field * field
    resist = 1.0 / (1.0 + jnp.exp(-STEEPNESS * (inten - THRESHOLD)))
    goal_f = goal[...].astype(F32)
    slope = 4.0 * (resist - goal_f) * STEEPNESS * resist * (1.0 - resist)
    goal[...] = resist.astype(BF)
    keep_ref[...] = goal[half_of(t), :]
    send_ref[...] = goal[half_of(1 - t), :]
    back = turn[h]
    gr = jnp.zeros((KB, KB), F32)
    gi = jnp.zeros((KB, KB), F32)
    for k in range(NR):
        cols = mm((fields[k] * slope).astype(BF), adj[...])
        cr, ci = cols[:, :KB], cols[:, KB:]
        block = jnp.concatenate([cols, jnp.concatenate([-ci, cr], axis=1)], axis=0).astype(BF)
        turned = mm(back, block)
        tr, ti = turned[:, :KB], turned[:, KB:]
        kr, ki = kern_ref[k, :, :KB].astype(F32), kern_ref[k, :, KB:].astype(F32)
        gr = gr + kr * tr + ki * ti
        gi = gi + ki * tr - kr * ti
    gr, gi = s * gr, s * gi
    grad = jnp.concatenate([gr, gi], axis=1)
    grad_ref[...] = grad.astype(BF)
    block = jnp.concatenate([grad, jnp.concatenate([-gi, gr], axis=1)], axis=0).astype(BF)
    edge[...] = mm(mm(rows[...], block).astype(BF), rim[t])
    for j, q in enumerate((q0, q1, q2, q3)):
        q[...] = edge[block_of(j), :].astype(BF)


def imaging(rank, masks, edges, goals, kern):
    quarter = masks[0].shape[0]
    smem = pl.BlockSpec(memory_space=pltpu.SMEM)
    vmem = pl.BlockSpec(memory_space=pltpu.VMEM)
    tables = [jnp.asarray(x) for x in image_tables()]
    return pl.pallas_call(
        image_kernel,
        out_shape=(
            jax.ShapeDtypeStruct((quarter, TS), BF),
            jax.ShapeDtypeStruct((quarter, TS), BF),
            jax.ShapeDtypeStruct((KB, 2 * KB), BF),
        ) + (jax.ShapeDtypeStruct((quarter, HALO), BF),) * 4,
        in_specs=[smem] + [vmem] * (11 + len(tables)),
        out_specs=(vmem,) * 7,
        scratch_shapes=[
            pltpu.VMEM((TS, 5 * KB), BF),
            pltpu.VMEM((2 * quarter, TS), BF),
            pltpu.VMEM((NR, 2 * quarter, TS), F32),
            pltpu.VMEM((TS, HALO), F32),
        ],
    )(rank.reshape(1), *masks, *edges, *goals, kern, *tables)


def back_kernel(rank_ref, keep, got, own, got1, got2, got3, r0, r1, r2, r3, row_tab, cols, resist_ref, grad_ref):
    rank = rank_ref[0]
    quarter, width = grad_ref.shape
    first = lax.rem(rank, 2) == 0
    resist_ref[:, :TS] = jnp.where(first, keep[...], got[...])
    resist_ref[:, TS:] = jnp.where(first, got[...], keep[...])
    mine = own[...].astype(F32) + got2[...].astype(F32)
    other = got1[...].astype(F32) + got3[...].astype(F32)
    rows = row_tab[pl.ds(pl.multiple_of(rank * quarter, quarter), quarter), :]
    parts = []
    for total in (jnp.where(first, mine, other), jnp.where(first, other, mine)):
        br, bi = total[:, :KB], total[:, KB:]
        block = jnp.concatenate([total, jnp.concatenate([-bi, br], axis=1)], axis=0).astype(BF)
        parts.append(mm(rows, block))
    result = mm(jnp.concatenate(parts, axis=1).astype(BF), cols[...])
    even = r0[...].astype(F32) + r2[...].astype(F32)
    odd = r1[...].astype(F32) + r3[...].astype(F32)
    low, high = jnp.where(first, odd, even), jnp.where(first, even, odd)
    blank = jnp.zeros((quarter, width - 2 * HALO), F32)
    grad_ref[...] = (result + jnp.concatenate([low, blank, high], axis=1)).astype(BF)


def back(rank, keep, got, grads, rims):
    quarter = keep.shape[0]
    smem = pl.BlockSpec(memory_space=pltpu.SMEM)
    vmem = pl.BlockSpec(memory_space=pltpu.VMEM)
    tables = [jnp.asarray(x) for x in back_tables()]
    whole = jax.ShapeDtypeStruct((quarter, 2 * TS), BF)
    return pl.pallas_call(
        back_kernel,
        out_shape=(whole, whole),
        in_specs=[smem] + [vmem] * (10 + len(tables)),
        out_specs=(vmem, vmem),
    )(rank.reshape(1), keep, got, *grads, *rims, *tables)


def swap(x, m, size):
    return lax.ppermute(x, "src", [(i, i ^ m) for i in range(size)])


def across(x, m, groups, size, to_left):
    pairs = []
    for g in range(groups):
        for r in range(size):
            there = g - 1 if to_left(r, r ^ m) else g + 1
            if 0 <= there < groups:
                pairs.append((r * groups + g, (r ^ m) * groups + there))
    return lax.ppermute(x, ("src", "tile"), pairs)


def on_device(mask, target, start_block, zernike, source_points, source_weight, tile_slit):
    groups = lax.axis_size("tile")
    size = lax.axis_size("src")
    rank = lax.axis_index("src").astype(jnp.int32)
    ends = jnp.concatenate([mask[:, :HALO], mask[:, -HALO:]], axis=1)
    masks = [mask] + [swap(mask, m, size) for m in (1, 2, 3)]
    edges = [across(ends, m, groups, size, lambda r, q: q % 2 == 1) for m in range(4)]
    goals = [target, swap(target, 1, size)]
    kern = synthesize(rank, tile_slit, zernike, source_points, source_weight, start_block)
    keep, send, grad, *rims = imaging(rank, masks, edges, goals, kern)
    grads = [grad] + [swap(grad, m, size) for m in (1, 2, 3)]
    arrived = [across(rims[m], m, groups, size, lambda r, q: r % 2 == 0) for m in range(4)]
    return tuple(back(rank, keep, swap(send, 1, size), grads, arrived))


def solution(mesh):
    placed = (P("src", "tile"), P("src", "tile"), P(), P(), P(), P(), P("tile"))
    return jax.shard_map(
        on_device,
        mesh=mesh,
        in_specs=placed,
        out_specs=(P("src", "tile"), P("src", "tile")),
        check_vma=False,
    )
```

```python
import math

import jax
import jax.numpy as jnp
import numpy as np
from jax import lax
from jax.experimental import pallas as pl
from jax.experimental.pallas import tpu as pltpu
from jax.sharding import PartitionSpec as P

KB = 128
NR = 24
NZ = 37
RAD = 40
SHIFT = 24
HALO = 64
ITERS = 4
TS = 256
PW = TS + 2 * HALO
GRID = 2 * SHIFT + 1
PUP = 2 * RAD + 1

STEEPNESS = 4.0
THRESHOLD = 0.5
RIDGE_SHARE = 0.001
BF = jnp.bfloat16
F32 = jnp.float32


def noll_terms(term_count):
    listing = []
    degree = 0
    while len(listing) < term_count:
        for azimuth in range(degree % 2, degree + 1, 2):
            if azimuth == 0:
                listing.append((degree, 0, 0))
            else:
                for repeat in range(2):
                    number = len(listing) + 1
                    listing.append((degree, azimuth, 2 if number % 2 == 0 else 1))
        degree += 1
    return listing[:term_count]


def radial_terms(degree, azimuth):
    powers = []
    for counter in range((degree - azimuth) // 2 + 1):
        factor = (
            (-1) ** counter
            * math.factorial(degree - counter)
            / (
                math.factorial(counter)
                * math.factorial((degree + azimuth) // 2 - counter)
                * math.factorial((degree - azimuth) // 2 - counter)
            )
        )
        powers.append((degree - 2 * counter, factor))
    return powers


def zernike_tables():
    coords = np.arange(PUP) - RAD
    row, col = np.meshgrid(coords, coords, indexing="ij")
    radius = np.sqrt(row * row + col * col) / RAD
    angle = np.arctan2(col * 1.0, row * 1.0)
    out = []
    for degree, azimuth, parity in noll_terms(NZ):
        radial = sum(factor * radius**power for power, factor in radial_terms(degree, azimuth))
        if azimuth == 0:
            out.append(math.sqrt(degree + 1.0) * radial)
        elif parity == 2:
            out.append(math.sqrt(2.0 * degree + 2.0) * radial * np.cos(azimuth * angle))
        else:
            out.append(math.sqrt(2.0 * degree + 2.0) * radial * np.sin(azimuth * angle))
    inside = row * row + col * col <= RAD * RAD
    return np.stack(out) * inside, inside.astype(np.float32)


def dft(rows, cols, sign, period=KB):
    return np.exp(sign * 2j * np.pi * np.mod(np.outer(rows, cols), period) / period)


def cmul(a, b):
    return (a[0] * b[0] - a[1] * b[1], a[0] * b[1] + a[1] * b[0])


SLOTS = 50
ROWS = SLOTS * NR
PAD = 64
HI = lax.Precision.HIGHEST
UNROLL = 6
UNROLL_S = 4
UNROLL_F = 4
UNROLL_I = 4


def real_form(table):
    return np.block([[table.real, -table.imag], [table.imag, table.real]])


def split(table):
    high = table.astype(np.float32).astype(jnp.bfloat16)
    low = (table - high.astype(np.float64)).astype(jnp.bfloat16)
    return high, low


def block_tables():
    freq = np.arange(KB)
    big = real_form(dft(freq, np.arange(KB) - KB // 2, -1))
    offs = np.zeros((KB, PAD), np.complex128)
    offs[:, :GRID] = dft(freq, np.arange(GRID) - SHIFT, 1)
    small = real_form(offs)
    rev = np.zeros((PAD, KB), np.float32)
    for spot in range(GRID):
        rev[spot, KB // 2 + SHIFT - spot] = 1.0
    lb, lb_lo = split(big)
    lbt, lbt_lo = split(big.T.copy())
    lc, lc_lo = split(small)
    lct, lct_lo = split(small.T.copy())
    wide = lambda a, b: np.concatenate([a, b], axis=1)
    tall = lambda a, b: np.concatenate([a, b], axis=0)
    return (lb, lbt, lc, lct, tall(lct, lct_lo), wide(lc, lc_lo), lbt_lo, lb_lo, rev.astype(jnp.bfloat16), rev.T.copy().astype(jnp.bfloat16))


def mm(a, b):
    return jnp.dot(a, b, preferred_element_type=F32)


def nt(a, b, precision=None):
    return lax.dot_general(a, b, (((1,), (1,)), ((), ())), precision=precision, preferred_element_type=F32)


def lanes(shape):
    return lax.broadcasted_iota(jnp.int32, shape, 1)


def sublanes(shape):
    return lax.broadcasted_iota(jnp.int32, shape, 0)


def halves(x):
    high = x.astype(BF)
    return high, (x - high.astype(F32)).astype(BF)


def fine_nt(a, b):
    ah, al = halves(a)
    bh, bl = halves(b)
    return nt(ah, bh) + nt(ah, bl) + nt(al, bh)


def fine_mm(a, b):
    ah, al = (x.astype(F32) for x in halves(a))
    bh, bl = (x.astype(F32) for x in halves(b))
    return mm(jnp.concatenate([ah, al, ah], axis=1).astype(BF), jnp.concatenate([bh, bh, bl], axis=0).astype(BF))


def factor(gram, floor):
    tile, blocks = 8, NR // 8
    rows = [slice(b * tile, (b + 1) * tile) for b in range(blocks)]
    wide_eye = (sublanes((NR, PAD)) == lanes((NR, PAD))).astype(F32)
    start = jnp.concatenate([gram, jnp.zeros((NR, PAD - NR), F32), wide_eye], axis=1)
    work = [start[x] for x in rows]
    col = [[jnp.broadcast_to(gram[x, j : j + 1], (tile, KB)) for x in rows] for j in range(NR)]
    row_no = sublanes((tile, KB))
    diag = [jnp.zeros((tile, KB), F32) for _ in rows]
    for k in range(NR):
        b0, r0 = divmod(k, tile)
        pick = lambda x: jnp.broadcast_to(x[r0 : r0 + 1, :], (tile, KB))
        pivot = jnp.maximum(pick(col[k][b0]), floor)
        diag[b0] = jnp.where(row_no == r0, pivot, diag[b0])
        inv = 1.0 / pivot
        ratio = [c * inv for c in col[k]]
        lead = pick(work[b0])
        for j in range(k + 1, NR):
            entry = pick(col[j][b0])
            for b in range(b0, blocks):
                col[j][b] = col[j][b] - ratio[b] * entry
        for b in range(b0, blocks):
            part = ratio[b] if b > b0 else jnp.where(row_no > r0, ratio[b], 0.0)
            work[b] = work[b] - part * lead
    done = jnp.concatenate([w * lax.rsqrt(d) for w, d in zip(work, diag)], axis=0)
    return done[:, :NR], done[:, PAD : PAD + NR]


def synth_kernel(rank_ref, slit_ref, zern_ref, sp_ref, sw_ref, zt_ref, ins_ref, b0_ref, lb, lbt, lc, lct, lct2, lc2, lbt_lo, lb_lo, rev, revt, out_ref, inv_ref, hat, a1, f2, c_ref, h_ref, wf, bx, c2):
    slit = jnp.maximum(slit_ref[rank_ref[0]], 0)
    turns = jnp.zeros((96, KB), F32)
    for z in range(NZ):
        turns = turns + zern_ref[slit, z] * zt_ref[z]
    turns = turns - jnp.floor(turns + 0.5)
    half = math.pi * turns
    sq = half * half
    sine = jnp.full_like(half, 1.0 / math.factorial(15))
    for n in (13, 11, 9, 7, 5, 3, 1):
        sine = 1.0 / math.factorial(n) - sine * sq
    sine = sine * half
    cosine = jnp.full_like(half, 1.0 / math.factorial(14))
    for n in (12, 10, 8, 6, 4, 2, 0):
        cosine = 1.0 / math.factorial(n) - cosine * sq
    pr = ins_ref[...] * (1.0 - 2.0 * sine * sine)
    pi = ins_ref[...] * (2.0 * sine * cosine)
    spot = lambda a, i, j: a[i : i + 1, j : j + 1]
    q1r, q1i = spot(pr, 88, 64), spot(pi, 88, 64)
    m1r, m1i = spot(pr, 8, 64), spot(pi, 8, 64)
    q2r, q2i = spot(pr, 48, 104), spot(pi, 48, 104)
    m2r, m2i = spot(pr, 48, 24), spot(pi, 48, 24)
    z1r, z1i = q1r * m1r + q1i * m1i, q1r * m1i - q1i * m1r
    z2r, z2i = q2r * m2r + q2i * m2i, q2r * m2i - q2i * m2r
    edge = jnp.zeros((16, 2 * KB), F32)
    both = jnp.concatenate([edge, jnp.concatenate([pr, pi], axis=1), edge], axis=0).astype(BF)
    ph = mm(both, lbt[...])
    stacked = jnp.concatenate([ph[:, :KB], ph[:, KB:]], axis=0).astype(BF)
    ph = mm(lb[...], stacked)
    hr, hi = ph[:KB], ph[KB:]
    hat[0] = jnp.concatenate([hr, hr], axis=1) / (KB * KB)
    hat[1] = jnp.concatenate([hi, hi], axis=1) / (KB * KB)
    power = (hr * hr + hi * hi) / (KB * KB)
    power = jnp.concatenate([power, power], axis=1)
    hat[2] = power

    weights = sw_ref[...]
    weights = weights / (math.pi * RAD * RAD * jnp.sum(weights, axis=1, keepdims=True))
    count = sp_ref.shape[1]
    offset = sublanes((KB, count))
    hot_x = jnp.where(offset - SHIFT == sp_ref[0:1, :], weights, 0.0)
    hot_y = (jnp.where(offset >= PAD, offset - PAD, offset) - SHIFT == sp_ref[1:2, :]).astype(F32).astype(BF)
    high, low = halves(hot_x)
    wmap = nt(high, hot_y) + nt(low, hot_y)
    for s in range(SLOTS):
        wf[s * NR : (s + 1) * NR, :] = jnp.broadcast_to(wmap[s : s + 1, :], (NR, KB))

    rs, cs = sublanes((KB, KB)), lanes((KB, KB))
    at = lambda i, j, v: jnp.where((rs == i) & (cs == j), v, 0.0)
    one = jnp.ones((1, 1), F32)
    top = 2 * SHIFT
    ky = (
        at(0, 0, one) + at(PAD, PAD, one)
        + at(top, 0, z2r) + at(PAD + top, 0, -z2i) + at(top, PAD, z2i) + at(PAD + top, PAD, z2r)
        + at(0, top, z2r) + at(PAD, top, z2i) + at(0, PAD + top, -z2i) + at(PAD, PAD + top, z2r)
    ).astype(BF)
    kq0 = jnp.concatenate([at(0, 0, q2r) + at(0, PAD, -q2i), at(0, 0, q2i) + at(0, PAD, q2r)], axis=0).astype(BF)
    kq2 = jnp.concatenate([at(0, 0, q2r) + at(PAD, 0, -q2i), at(0, 0, q2i) + at(PAD, 0, q2r)], axis=1).astype(BF)

    a1[:, ROWS:, :] = jnp.zeros((2, PAD * NR - ROWS, KB), F32)

    def pack(x0, x1):
        return jnp.concatenate(
            [jnp.concatenate([x0[:, :KB], x1[:, :KB]], axis=1), jnp.concatenate([x0[:, KB:], x1[:, KB:]], axis=1)], axis=0
        )

    def unpack(y, height):
        return (
            jnp.concatenate([y[:height, :KB], y[height:, :KB]], axis=1),
            jnp.concatenate([y[:height, KB:], y[height:, KB:]], axis=1),
        )

    def put(ref, k, x):
        ref[0, pl.ds(k, PAD, stride=NR), :] = x[:, :KB]
        ref[1, pl.ds(k, PAD, stride=NR), :] = x[:, KB:]

    def get(ref, k):
        return jnp.concatenate([ref[0, pl.ds(k, PAD, stride=NR), :], ref[1, pl.ds(k, PAD, stride=NR), :]], axis=1)

    def both_halves(ref):
        return jnp.concatenate([ref[0, :ROWS, :], ref[1, :ROWS, :]], axis=1).astype(BF)

    prow = sublanes((KB, 2 * KB))
    urow = sublanes((2 * KB, 2 * KB))

    def start(q, carry):
        pairs = [q * UNROLL_S + j for j in range(UNROLL_S)]
        blocks = [[jnp.concatenate([b0_ref[0, 2 * p + e], b0_ref[1, 2 * p + e]], axis=1).astype(BF) for e in range(2)] for p in pairs]
        xs = [pack(mm(b[0], lbt[...]), mm(b[1], lbt[...])) for b in blocks]
        revs = [[mm(rev[...], e) for e in b] for b in blocks]
        ys = [mm(lb[...], x.astype(BF)) for x in xs]
        ys = [jnp.concatenate([hat[0] * y[:KB] + hat[1] * y[KB:], hat[0] * y[KB:] - hat[1] * y[:KB]], axis=0).astype(BF) for y in ys]
        ds = [mm(lct[...], y) for y in ys]
        for p, x, d, rv in zip(pairs, xs, ds, revs):
            xr, xi = x[0:1], x[KB : KB + 1]
            cr, ci = (q1r * xr + q1i * xi) / KB, (q1r * xi - q1i * xr) / KB
            d = d - jnp.where(prow == 0, cr, 0.0) - jnp.where(prow == PAD, ci, 0.0)
            d0, d1 = unpack(d, PAD)
            put(f2, 2 * p, d0)
            put(f2, 2 * p + 1, d1)
            put(bx, 2 * p, rv[0])
            put(bx, 2 * p + 1, rv[1])
        return carry

    lax.fori_loop(0, NR // 2 // UNROLL_S, start, 0)
    first = mm(both_halves(f2), lc[...]) - mm(both_halves(bx), kq0)
    c_ref[...] = wf[...] * first

    def wide(ref):
        return jnp.concatenate([ref[s * NR : (s + 1) * NR, :] for s in range(SLOTS)], axis=1)

    def tallput(ref, x):
        for s in range(SLOTS):
            ref[s * NR : (s + 1) * NR, :] = x[:, s * KB : (s + 1) * KB]

    def forward(p):
        return pack(get(a1, 2 * p), get(a1, 2 * p + 1)).astype(BF)

    def middle(q, carry):
        pairs = [q * UNROLL + j for j in range(UNROLL)]
        ys = [mm(lc[...], forward(p)) for p in pairs]
        ys = [jnp.concatenate([hat[2] * y[:KB], hat[2] * y[KB:]], axis=0).astype(BF) for y in ys]
        ds = [mm(lct[...], y) for y in ys]
        for p, d in zip(pairs, ds):
            d0, d1 = unpack(d, PAD)
            put(f2, 2 * p, d0)
            put(f2, 2 * p + 1, d1)
        return carry

    def apply():
        coef = c_ref[...].astype(BF)
        full = mm(coef, lct[...])
        a1[0, :ROWS, :] = full[:, :KB]
        a1[1, :ROWS, :] = full[:, KB:]
        lax.fori_loop(0, NR // 2 // UNROLL, middle, 0)
        last = slice(top * NR, (top + 1) * NR)
        lr, li, ur, ui = a1[0, 0:NR, :], a1[1, 0:NR, :], a1[0, last, :], a1[1, last, :]
        f2[0, 0:NR, :] = f2[0, 0:NR, :] - (lr + z1r * ur - z1i * ui) / KB
        f2[1, 0:NR, :] = f2[1, 0:NR, :] - (li + z1r * ui + z1i * ur) / KB
        f2[0, last, :] = f2[0, last, :] - (z1r * lr + z1i * li) / KB
        f2[1, last, :] = f2[1, last, :] - (z1r * li - z1i * lr) / KB
        h_ref[...] = mm(both_halves(f2), lc[...]) - mm(coef, ky)
        gram = fine_nt(wide(c_ref), wide(h_ref))
        gram = 0.5 * (gram + gram.T)
        eye = sublanes((NR, NR)) == lanes((NR, NR))
        trace = jnp.sum(jnp.sum(jnp.where(eye, gram, 0.0), axis=1, keepdims=True), axis=0, keepdims=True)
        return factor(gram + jnp.where(eye, RIDGE_SHARE * trace / NR + 1e-06, 0.0), 0.0)[1]

    def step(iteration, carry):
        @pl.when(iteration > 0)
        def _():
            tallput(h_ref, fine_mm(inv_ref[:, :NR], wide(h_ref)))
            c_ref[...] = wf[...] * h_ref[...]

        inv_ref[:, :NR] = apply()
        return carry

    lax.fori_loop(0, ITERS, step, 0)
    inverse = inv_ref[:, :NR]
    f2[0, :ROWS, :] = wf[...] * h_ref[...]
    moment = fine_nt(jnp.concatenate([f2[0, s * NR : (s + 1) * NR, :] for s in range(SLOTS)], axis=1), wide(h_ref))
    moment = jnp.dot(inverse, moment, precision=HI, preferred_element_type=F32)
    mixing = nt(moment, inverse, HI)
    mixing = 0.5 * (mixing + mixing.T)
    eye = sublanes((NR, NR)) == lanes((NR, NR))
    trace = jnp.sum(jnp.sum(jnp.where(eye, mixing, 0.0), axis=1, keepdims=True), axis=0, keepdims=True)
    root = factor(mixing, 1e-6 * trace + 1e-30)[0]
    combine = jnp.dot(root, inverse, precision=HI, preferred_element_type=F32)
    tallput(c_ref, fine_mm(combine, wide(c_ref)))
    coef = c_ref[...].astype(BF)
    full = mm(jnp.concatenate([coef, coef], axis=1), lct2[...])
    a1[0, :ROWS, :] = full[:, :KB]
    a1[1, :ROWS, :] = full[:, KB:]
    c2[:ROWS, :] = c_ref[...]
    c2[ROWS:, :] = jnp.zeros((PAD * NR - ROWS, KB), F32)

    def finish(q, carry):
        pairs = [q * UNROLL_F + j for j in range(UNROLL_F)]
        xs = [pack(get(a1, 2 * p), get(a1, 2 * p + 1)) for p in pairs]
        cols = [[mm(revt[...], c2[pl.ds(2 * p + e, PAD, stride=NR), :].astype(BF)).astype(BF) for e in range(2)] for p in pairs]
        ys = [mm(lc2[...], jnp.concatenate([x, x], axis=0).astype(BF)) for x in xs]
        ys = [jnp.concatenate([hat[0] * y[:KB] - hat[1] * y[KB:], hat[0] * y[KB:] + hat[1] * y[:KB]], axis=0).astype(BF) for y in ys]
        us = [mm(lbt[...], y) + mm(lbt_lo[...], y) for y in ys]
        for p, x, u, col in zip(pairs, xs, us, cols):
            xr, xi = x[0:1], x[PAD : PAD + 1]
            cr, ci = (q1r * xr - q1i * xi) / KB, (q1r * xi + q1i * xr) / KB
            u = u - jnp.where(urow == 0, cr, 0.0) - jnp.where(urow == KB, ci, 0.0)
            pair = unpack(u, KB)
            for e in range(2):
                ub = pair[e].astype(BF)
                out_ref[2 * p + e] = (mm(ub, lb[...]) + mm(ub, lb_lo[...]) - mm(col[e], kq2)).astype(BF)
        return carry

    lax.fori_loop(0, NR // 2 // UNROLL_F, finish, 0)


def synthesize(rank, tile_slit, zernike, source_points, source_weight, start_block):
    ztab, inside = zernike_tables()
    wide = np.zeros((NZ, 96, KB), np.float32)
    wide[:, 8:89, 24:105] = ztab
    ins = np.zeros((96, KB), np.float32)
    ins[8:89, 24:105] = inside
    smem = pl.BlockSpec(memory_space=pltpu.SMEM)
    vmem = pl.BlockSpec(memory_space=pltpu.VMEM)
    tables = [jnp.asarray(t) for t in block_tables()]
    big = (2, PAD * NR, KB)
    return pl.pallas_call(
        synth_kernel,
        out_shape=jax.ShapeDtypeStruct((NR, KB, 2 * KB), BF),
        in_specs=[smem] * 3 + [vmem] * (5 + len(tables)),
        out_specs=vmem,
        scratch_shapes=[
            pltpu.VMEM((NR, KB), F32),
            pltpu.VMEM((3, KB, 2 * KB), F32),
            pltpu.VMEM(big, F32),
            pltpu.VMEM(big, F32),
            pltpu.VMEM((ROWS, KB), F32),
            pltpu.VMEM((ROWS, KB), F32),
            pltpu.VMEM((ROWS, KB), F32),
            pltpu.VMEM(big, F32),
            pltpu.VMEM((PAD * NR, KB), F32),
        ],
    )(rank.reshape(1), tile_slit, zernike, source_points.T, source_weight.reshape(1, -1), jnp.asarray(wide), jnp.asarray(ins), start_block, *tables)


SIDE = TS + PW
PACK = 4 * TS + 2 * SIDE


def tables_of(count, period):
    t = dft(np.arange(count), np.arange(KB) - KB // 2, 1, period)
    return t.real.astype(np.float32), t.imag.astype(np.float32)


def cast(x):
    return np.ascontiguousarray(x).astype(jnp.bfloat16)


def column_table():
    cc, cs = tables_of(PW, PW)
    out = np.zeros((5 * TS, 2 * KB), np.float32)
    out[2 * TS - HALO : 2 * TS - HALO + PW] = np.concatenate([cc, -cs], 1)
    return cast(out)


def row_table():
    rc, rs = tables_of(TS, TS)
    return np.concatenate([rc, rs], 1)


def image_tables():
    rc, rs = tables_of(TS, TS)
    cc, cs = tables_of(PW, PW)
    turn = np.concatenate([rc.T, rs.T], 1)
    inv_t = np.concatenate([cc, -cs], 1)[HALO : HALO + TS].T
    adj = np.concatenate([cc, cs], 1)[HALO : HALO + TS]
    rows = row_table()
    return (column_table(),) + tuple(cast(x) for x in (rows.T, rows, turn, inv_t, adj))


def tile_columns(ref, tile):
    return ref[pl.ds(pl.multiple_of(TS * (3 - tile), TS), 2 * TS), :]


def image_kernel(rank_ref, slit_ref, m0, m1, m2, m3, kern_ref, fwd, rows_t, rows, turn, inv_t, adj, o0, o1, o2, o3, patch, goal, fields, inten, gsum, spec):
    rank = rank_ref[0]
    quarter = m0.shape[0]
    left, outer = rank < 2, (rank == 0) | (rank == 3)
    block_of = lambda j: pl.ds(pl.multiple_of((rank ^ j) * quarter, quarter), quarter)
    keep = lanes((quarter, PW)) < PW - HALO
    for j, m in enumerate((m0, m1, m2, m3)):
        side = jnp.where(left, m[:, 4 * TS : 4 * TS + SIDE], m[:, 4 * TS + SIDE :])
        own = jnp.where(left, m[:, 2 * TS : 3 * TS], m[:, 3 * TS : 4 * TS])
        patch[block_of(j), : 2 * TS] = m[:, : 2 * TS]
        patch[block_of(j), 2 * TS :] = jnp.where(keep, side[:, TS:].astype(F32), 0.0).astype(BF)
        goal[block_of(j), :] = jnp.where(outer, side[:, :TS], own).astype(F32)
    s = 1.0 / math.sqrt(TS * PW)
    start = jnp.where(rank < 2, 2 * TS - HALO - rank * TS, 3 * TS - (rank - 2) * TS)
    side_table = fwd[pl.ds(pl.multiple_of(start, HALO), PW), :]
    table = jnp.concatenate([tile_columns(fwd, rank), side_table], axis=0)
    columns = mm(patch[...], table).astype(BF)
    sums = mm(rows_t[...], columns)
    spec[0] = s * (sums[:KB, :KB] + sums[KB:, KB:])
    spec[1] = s * (sums[:KB, KB:] - sums[KB:, :KB])
    inten[...] = jnp.zeros((TS, TS), F32)
    gsum[...] = jnp.zeros((KB, 2 * KB), F32)

    def forward(q, carry):
        ks = [q * UNROLL_I + e for e in range(UNROLL_I)]
        sr, si = spec[0], spec[1]
        blocks = []
        for k in ks:
            kr, ki = kern_ref[k, :, :KB].astype(F32), kern_ref[k, :, KB:].astype(F32)
            wr, wi = kr * sr + ki * si, kr * si - ki * sr
            blocks.append(jnp.concatenate([jnp.concatenate([wr, wi], axis=1), jnp.concatenate([-wi, wr], axis=1)], axis=0).astype(BF))
        waves = [mm(rows[...], b).astype(BF) for b in blocks]
        total = inten[...]
        for k, w in zip(ks, waves):
            field = mm(w, inv_t[...])
            fields[k] = field
            total = total + field * field
        inten[...] = total
        return carry

    lax.fori_loop(0, NR // UNROLL_I, forward, 0)
    resist = 1.0 / (1.0 + jnp.exp(-STEEPNESS * (inten[...] - THRESHOLD)))
    inten[...] = 4.0 * (resist - goal[...]) * STEEPNESS * resist * (1.0 - resist)
    goal[...] = resist

    def backward(q, carry):
        ks = [q * UNROLL_I + e for e in range(UNROLL_I)]
        cols = [mm((fields[k] * inten[...]).astype(BF), adj[...]) for k in ks]
        blocks = [jnp.concatenate([c, jnp.concatenate([-c[:, KB:], c[:, :KB]], axis=1)], axis=0).astype(BF) for c in cols]
        turned = [mm(turn[...], b) for b in blocks]
        gr, gi = gsum[:, :KB], gsum[:, KB:]
        for k, y in zip(ks, turned):
            kr, ki = kern_ref[k, :, :KB].astype(F32), kern_ref[k, :, KB:].astype(F32)
            gr = gr + kr * y[:, :KB] + ki * y[:, KB:]
            gi = gi + ki * y[:, :KB] - kr * y[:, KB:]
        gsum[:, :KB] = gr
        gsum[:, KB:] = gi
        return carry

    lax.fori_loop(0, NR // UNROLL_I, backward, 0)
    grad = jnp.where(slit_ref[rank] >= 0, s * gsum[...], 0.0).astype(BF)
    for j, o in enumerate((o0, o1, o2, o3)):
        o[:KB, :] = grad
        o[KB:, :] = goal[block_of(j), :].astype(BF)


def imaging(rank, slits, packs, kern):
    quarter = packs[0].shape[0]
    smem = pl.BlockSpec(memory_space=pltpu.SMEM)
    vmem = pl.BlockSpec(memory_space=pltpu.VMEM)
    tables = [jnp.asarray(x) for x in image_tables()]
    return pl.pallas_call(
        image_kernel,
        out_shape=(jax.ShapeDtypeStruct((KB + quarter, TS), BF),) * 4,
        in_specs=[smem] * 2 + [vmem] * (5 + len(tables)),
        out_specs=(vmem,) * 4,
        scratch_shapes=[
            pltpu.VMEM((TS, 2 * TS + PW), BF),
            pltpu.VMEM((TS, TS), F32),
            pltpu.VMEM((NR, TS, TS), F32),
            pltpu.VMEM((TS, TS), F32),
            pltpu.VMEM((KB, 2 * KB), F32),
            pltpu.VMEM((2, KB, KB), F32),
        ],
    )(rank.reshape(1), slits, *packs, kern, *tables)


def back_kernel(rank_ref, n0, n1, n2, n3, row_tab, fwd, resist_ref, grad_ref, held):
    rank = rank_ref[0]
    quarter, width = grad_ref.shape
    for j, n in enumerate((n0, n1, n2, n3)):
        held[rank ^ j] = n[...]
    resist_ref[:, :TS] = held[1, KB:, :]
    resist_ref[:, TS:] = held[2, KB:, :]
    rows = row_tab[pl.ds(pl.multiple_of(rank * quarter, quarter), quarter), :]
    parts, tables = [], []
    for tile in range(4):
        total = held[tile, :KB, :].astype(F32)
        br, bi = total[:, :KB], total[:, KB:]
        block = jnp.concatenate([total, jnp.concatenate([-bi, br], axis=1)], axis=0).astype(BF)
        parts.append(nt(mm(rows, block).astype(BF), fwd[TS * (3 - tile) : TS * (5 - tile), :]))
    grad_ref[...] = (parts[0] + parts[1] + parts[2] + parts[3]).astype(BF)


def back(rank, notes):
    quarter = notes[0].shape[0] - KB
    smem = pl.BlockSpec(memory_space=pltpu.SMEM)
    vmem = pl.BlockSpec(memory_space=pltpu.VMEM)
    whole = jax.ShapeDtypeStruct((quarter, 2 * TS), BF)
    return pl.pallas_call(
        back_kernel,
        out_shape=(whole, whole),
        in_specs=[smem] + [vmem] * 6,
        out_specs=(vmem, vmem),
        scratch_shapes=[pltpu.VMEM((4, KB + quarter, TS), BF)],
    )(rank.reshape(1), *notes, jnp.asarray(cast(row_table())), jnp.asarray(column_table()))


def swap(x, m, size):
    return lax.ppermute(x, "src", [(i, i ^ m) for i in range(size)])


def shift(x, step, count):
    pairs = [(i, i + step) for i in range(count) if 0 <= i + step < count]
    return lax.ppermute(x, "tile", pairs)


def on_device(mask, target, start_block, zernike, source_points, source_weight, tile_slit):
    groups = lax.axis_size("tile")
    size = lax.axis_size("src")
    rank = lax.axis_index("src").astype(jnp.int32)
    quarter = mask.shape[0]
    mark = lambda e: jnp.broadcast_to((tile_slit[e] + 1).astype(BF), (quarter, HALO))
    reach = PW - HALO
    rightward = jnp.concatenate([target[:, TS:], mask[:, 2 * TS - reach :], mark(1)], axis=1)
    leftward = jnp.concatenate([target[:, :TS], mask[:, :reach], mark(0)], axis=1)
    from_left = shift(rightward, 1, groups)
    from_right = shift(leftward, -1, groups)
    pack = jnp.concatenate([mask, target, from_left, from_right], axis=1)
    ends = [x[0, SIDE - HALO : SIDE - HALO + 1].astype(jnp.int32) - 1 for x in (from_left, from_right)]
    slits = jnp.concatenate([ends[0], tile_slit, ends[1]])
    packs = [pack] + [swap(pack, m, size) for m in (1, 2, 3)]
    kern = synthesize(rank, slits, zernike, source_points, source_weight, start_block)
    notes = imaging(rank, slits, packs, kern)
    return tuple(back(rank, [notes[0]] + [swap(notes[m], m, size) for m in (1, 2, 3)]))


def solution(mesh):
    placed = (P("src", "tile"), P("src", "tile"), P(), P(), P(), P(), P("tile"))
    return jax.shard_map(
        on_device,
        mesh=mesh,
        in_specs=placed,
        out_specs=(P("src", "tile"), P("src", "tile")),
        check_vma=False,
    )
```

```python
import math

import jax
import jax.numpy as jnp
import numpy as np
from jax import lax
from jax.experimental import pallas as pl
from jax.experimental.pallas import tpu as pltpu
from jax.sharding import PartitionSpec as P

KB = 128
NR = 24
NZ = 37
RAD = 40
SHIFT = 24
HALO = 64
ITERS = 4
TS = 256
PW = TS + 2 * HALO
GRID = 2 * SHIFT + 1
PUP = 2 * RAD + 1

STEEPNESS = 4.0
THRESHOLD = 0.5
RIDGE_SHARE = 0.001
BF = jnp.bfloat16
F32 = jnp.float32


def noll_terms(term_count):
    listing = []
    degree = 0
    while len(listing) < term_count:
        for azimuth in range(degree % 2, degree + 1, 2):
            if azimuth == 0:
                listing.append((degree, 0, 0))
            else:
                for repeat in range(2):
                    number = len(listing) + 1
                    listing.append((degree, azimuth, 2 if number % 2 == 0 else 1))
        degree += 1
    return listing[:term_count]


def radial_terms(degree, azimuth):
    powers = []
    for counter in range((degree - azimuth) // 2 + 1):
        factor = (
            (-1) ** counter
            * math.factorial(degree - counter)
            / (
                math.factorial(counter)
                * math.factorial((degree + azimuth) // 2 - counter)
                * math.factorial((degree - azimuth) // 2 - counter)
            )
        )
        powers.append((degree - 2 * counter, factor))
    return powers


def zernike_tables():
    coords = np.arange(PUP) - RAD
    row, col = np.meshgrid(coords, coords, indexing="ij")
    radius = np.sqrt(row * row + col * col) / RAD
    angle = np.arctan2(col * 1.0, row * 1.0)
    out = []
    for degree, azimuth, parity in noll_terms(NZ):
        radial = sum(factor * radius**power for power, factor in radial_terms(degree, azimuth))
        if azimuth == 0:
            out.append(math.sqrt(degree + 1.0) * radial)
        elif parity == 2:
            out.append(math.sqrt(2.0 * degree + 2.0) * radial * np.cos(azimuth * angle))
        else:
            out.append(math.sqrt(2.0 * degree + 2.0) * radial * np.sin(azimuth * angle))
    inside = row * row + col * col <= RAD * RAD
    return np.stack(out) * inside, inside.astype(np.float32)


def dft(rows, cols, sign, period=KB):
    return np.exp(sign * 2j * np.pi * np.mod(np.outer(rows, cols), period) / period)


def cmul(a, b):
    return (a[0] * b[0] - a[1] * b[1], a[0] * b[1] + a[1] * b[0])


SLOTS = 50
SIDE = TS + PW
ROWS = SLOTS * NR
PAD = 64
HI = lax.Precision.HIGHEST
UNROLL = 6
UNROLL_S = 4
UNROLL_F = 4
UNROLL_I = 4


def real_form(table):
    return np.block([[table.real, -table.imag], [table.imag, table.real]])


def split(table):
    high = table.astype(np.float32).astype(jnp.bfloat16)
    low = (table - high.astype(np.float64)).astype(jnp.bfloat16)
    return high, low


def block_tables():
    freq = np.arange(KB)
    big = real_form(dft(freq, np.arange(KB) - KB // 2, -1))
    offs = np.zeros((KB, PAD), np.complex128)
    offs[:, :GRID] = dft(freq, np.arange(GRID) - SHIFT, 1)
    small = real_form(offs)
    rev = np.zeros((PAD, KB), np.float32)
    for spot in range(GRID):
        rev[spot, KB // 2 + SHIFT - spot] = 1.0
    lb, lb_lo = split(big)
    lbt, lbt_lo = split(big.T.copy())
    lc, lc_lo = split(small)
    lct, lct_lo = split(small.T.copy())
    wide = lambda a, b: np.concatenate([a, b], axis=1)
    tall = lambda a, b: np.concatenate([a, b], axis=0)
    return (lb, lbt, lc, lct, tall(lct, lct_lo), wide(lc, lc_lo), lbt_lo, lb_lo, rev.astype(jnp.bfloat16), rev.T.copy().astype(jnp.bfloat16))


def mm(a, b):
    return jnp.dot(a, b, preferred_element_type=F32)


def nt(a, b, precision=None):
    return lax.dot_general(a, b, (((1,), (1,)), ((), ())), precision=precision, preferred_element_type=F32)


def lanes(shape):
    return lax.broadcasted_iota(jnp.int32, shape, 1)


def sublanes(shape):
    return lax.broadcasted_iota(jnp.int32, shape, 0)


def halves(x):
    high = x.astype(BF)
    return high, (x - high.astype(F32)).astype(BF)


def stack_halves(x):
    return jnp.concatenate([part.astype(F32) for part in halves(x)], axis=0).astype(BF)


def fine_nt(a, b):
    full = nt(stack_halves(a), stack_halves(b))
    return full[:NR, :NR] + full[:NR, NR:] + full[NR:, :NR]


def fine_mm(a, b):
    ah, al = (x.astype(F32) for x in halves(a))
    bh, bl = (x.astype(F32) for x in halves(b))
    return mm(jnp.concatenate([ah, al, ah], axis=1).astype(BF), jnp.concatenate([bh, bh, bl], axis=0).astype(BF))


def factor(gram, floor):
    tile, blocks = 8, NR // 8
    rows = [slice(b * tile, (b + 1) * tile) for b in range(blocks)]
    wide_eye = (sublanes((NR, PAD)) == lanes((NR, PAD))).astype(F32)
    start = jnp.concatenate([gram, jnp.zeros((NR, PAD - NR), F32), wide_eye], axis=1)
    work = [start[x] for x in rows]
    col = [[jnp.broadcast_to(gram[x, j : j + 1], (tile, KB)) for x in rows] for j in range(NR)]
    row_no = sublanes((tile, KB))
    diag = [jnp.zeros((tile, KB), F32) for _ in rows]
    for k in range(NR):
        b0, r0 = divmod(k, tile)
        pick = lambda x: jnp.broadcast_to(x[r0 : r0 + 1, :], (tile, KB))
        pivot = jnp.maximum(pick(col[k][b0]), floor)
        diag[b0] = jnp.where(row_no == r0, pivot, diag[b0])
        inv = 1.0 / pivot
        ratio = [c * inv for c in col[k]]
        lead = pick(work[b0])
        for j in range(k + 1, NR):
            entry = pick(col[j][b0])
            for b in range(b0, blocks):
                col[j][b] = col[j][b] - ratio[b] * entry
        for b in range(b0, blocks):
            part = ratio[b] if b > b0 else jnp.where(row_no > r0, ratio[b], 0.0)
            work[b] = work[b] - part * lead
    done = jnp.concatenate([w * lax.rsqrt(d) for w, d in zip(work, diag)], axis=0)
    return done[:, :NR], done[:, PAD : PAD + NR]


def neighbour_marks(left_ref, right_ref):
    low = left_ref[0:16, TS : TS + KB].astype(F32)[0:1, 0:1]
    high = right_ref[0:16, SIDE - KB : SIDE].astype(F32)[0:1, KB - 1 : KB]
    return low, high


def synth_kernel(rank_ref, slit_ref, left_ref, right_ref, zern_ref, sp_ref, sw_ref, zt_ref, ins_ref, b0_ref, lb, lbt, lc, lct, lct2, lc2, lbt_lo, lb_lo, rev, revt, out_ref, inv_ref, hat, a1, f2, c_ref, h_ref, wf, bx, c2):
    rank = rank_ref[0]
    low_end, high_end = neighbour_marks(left_ref, right_ref)
    slit = slit_ref[jnp.clip(rank - 1, 0, 1)].astype(F32)
    slit = jnp.where(rank == 0, low_end - 1.0, jnp.where(rank == 3, high_end - 1.0, slit))
    chosen = sublanes((zern_ref.shape[0], 1)).astype(F32) == jnp.maximum(slit, 0.0)
    coefs = jnp.sum(jnp.where(chosen, zern_ref[...], 0.0), axis=0, keepdims=True)
    turns = jnp.zeros((96, KB), F32)
    for z in range(NZ):
        turns = turns + coefs[:, z : z + 1] * zt_ref[z]
    turns = turns - jnp.floor(turns + 0.5)
    half = math.pi * turns
    sq = half * half
    sine = jnp.full_like(half, 1.0 / math.factorial(15))
    for n in (13, 11, 9, 7, 5, 3, 1):
        sine = 1.0 / math.factorial(n) - sine * sq
    sine = sine * half
    cosine = jnp.full_like(half, 1.0 / math.factorial(14))
    for n in (12, 10, 8, 6, 4, 2, 0):
        cosine = 1.0 / math.factorial(n) - cosine * sq
    pr = ins_ref[...] * (1.0 - 2.0 * sine * sine)
    pi = ins_ref[...] * (2.0 * sine * cosine)
    spot = lambda a, i, j: a[i : i + 1, j : j + 1]
    q1r, q1i = spot(pr, 88, 64), spot(pi, 88, 64)
    m1r, m1i = spot(pr, 8, 64), spot(pi, 8, 64)
    q2r, q2i = spot(pr, 48, 104), spot(pi, 48, 104)
    m2r, m2i = spot(pr, 48, 24), spot(pi, 48, 24)
    z1r, z1i = q1r * m1r + q1i * m1i, q1r * m1i - q1i * m1r
    z2r, z2i = q2r * m2r + q2i * m2i, q2r * m2i - q2i * m2r
    edge = jnp.zeros((16, 2 * KB), F32)
    both = jnp.concatenate([edge, jnp.concatenate([pr, pi], axis=1), edge], axis=0).astype(BF)
    ph = mm(both, lbt[...])
    stacked = jnp.concatenate([ph[:, :KB], ph[:, KB:]], axis=0).astype(BF)
    ph = mm(lb[...], stacked)
    hr, hi = ph[:KB], ph[KB:]
    hat[0] = jnp.concatenate([hr, hr], axis=1) / (KB * KB)
    hat[1] = jnp.concatenate([hi, hi], axis=1) / (KB * KB)
    power = (hr * hr + hi * hi) / (KB * KB)
    power = jnp.concatenate([power, power], axis=1)
    hat[2] = power

    weights = sw_ref[...]
    weights = weights / (math.pi * RAD * RAD * jnp.sum(weights, axis=1, keepdims=True))
    count = sp_ref.shape[1]
    offset = sublanes((KB, count))
    hot_x = jnp.where(offset - SHIFT == sp_ref[0:1, :], weights, 0.0)
    hot_y = (jnp.where(offset >= PAD, offset - PAD, offset) - SHIFT == sp_ref[1:2, :]).astype(F32).astype(BF)
    high, low = halves(hot_x)
    wmap = nt(high, hot_y) + nt(low, hot_y)
    for s in range(SLOTS):
        wf[s * NR : (s + 1) * NR, :] = jnp.broadcast_to(wmap[s : s + 1, :], (NR, KB))

    rs, cs = sublanes((KB, KB)), lanes((KB, KB))
    at = lambda i, j, v: jnp.where((rs == i) & (cs == j), v, 0.0)
    one = jnp.ones((1, 1), F32)
    top = 2 * SHIFT
    ky = (
        at(0, 0, one) + at(PAD, PAD, one)
        + at(top, 0, z2r) + at(PAD + top, 0, -z2i) + at(top, PAD, z2i) + at(PAD + top, PAD, z2r)
        + at(0, top, z2r) + at(PAD, top, z2i) + at(0, PAD + top, -z2i) + at(PAD, PAD + top, z2r)
    ).astype(BF)
    kq0 = jnp.concatenate([at(0, 0, q2r) + at(0, PAD, -q2i), at(0, 0, q2i) + at(0, PAD, q2r)], axis=0).astype(BF)
    kq2 = jnp.concatenate([at(0, 0, q2r) + at(PAD, 0, -q2i), at(0, 0, q2i) + at(PAD, 0, q2r)], axis=1).astype(BF)

    a1[:, ROWS:, :] = jnp.zeros((2, PAD * NR - ROWS, KB), F32)

    def pack(x0, x1):
        return jnp.concatenate(
            [jnp.concatenate([x0[:, :KB], x1[:, :KB]], axis=1), jnp.concatenate([x0[:, KB:], x1[:, KB:]], axis=1)], axis=0
        )

    def unpack(y, height):
        return (
            jnp.concatenate([y[:height, :KB], y[height:, :KB]], axis=1),
            jnp.concatenate([y[:height, KB:], y[height:, KB:]], axis=1),
        )

    def put(ref, k, x):
        ref[0, pl.ds(k, PAD, stride=NR), :] = x[:, :KB]
        ref[1, pl.ds(k, PAD, stride=NR), :] = x[:, KB:]

    def get(ref, k):
        return jnp.concatenate([ref[0, pl.ds(k, PAD, stride=NR), :], ref[1, pl.ds(k, PAD, stride=NR), :]], axis=1)

    def both_halves(ref):
        return jnp.concatenate([ref[0, :ROWS, :], ref[1, :ROWS, :]], axis=1).astype(BF)

    prow = sublanes((KB, 2 * KB))
    urow = sublanes((2 * KB, 2 * KB))

    def start(q, carry):
        pairs = [q * UNROLL_S + j for j in range(UNROLL_S)]
        blocks = [[jnp.concatenate([b0_ref[0, 2 * p + e], b0_ref[1, 2 * p + e]], axis=1).astype(BF) for e in range(2)] for p in pairs]
        xs = [pack(mm(b[0], lbt[...]), mm(b[1], lbt[...])) for b in blocks]
        revs = [[mm(rev[...], e) for e in b] for b in blocks]
        ys = [mm(lb[...], x.astype(BF)) for x in xs]
        ys = [jnp.concatenate([hat[0] * y[:KB] + hat[1] * y[KB:], hat[0] * y[KB:] - hat[1] * y[:KB]], axis=0).astype(BF) for y in ys]
        ds = [mm(lct[...], y) for y in ys]
        for p, x, d, rv in zip(pairs, xs, ds, revs):
            xr, xi = x[0:1], x[KB : KB + 1]
            cr, ci = (q1r * xr + q1i * xi) / KB, (q1r * xi - q1i * xr) / KB
            d = d - jnp.where(prow == 0, cr, 0.0) - jnp.where(prow == PAD, ci, 0.0)
            d0, d1 = unpack(d, PAD)
            put(f2, 2 * p, d0)
            put(f2, 2 * p + 1, d1)
            put(bx, 2 * p, rv[0])
            put(bx, 2 * p + 1, rv[1])
        return carry

    lax.fori_loop(0, NR // 2 // UNROLL_S, start, 0)
    first = mm(both_halves(f2), lc[...]) - mm(both_halves(bx), kq0)
    c_ref[...] = wf[...] * first

    def wide(ref):
        return jnp.concatenate([ref[s * NR : (s + 1) * NR, :] for s in range(SLOTS)], axis=1)

    def tallput(ref, x):
        for s in range(SLOTS):
            ref[s * NR : (s + 1) * NR, :] = x[:, s * KB : (s + 1) * KB]

    def forward(p):
        return pack(get(a1, 2 * p), get(a1, 2 * p + 1)).astype(BF)

    def middle(q, carry):
        pairs = [q * UNROLL + j for j in range(UNROLL)]
        ys = [mm(lc[...], forward(p)) for p in pairs]
        ys = [jnp.concatenate([hat[2] * y[:KB], hat[2] * y[KB:]], axis=0).astype(BF) for y in ys]
        ds = [mm(lct[...], y) for y in ys]
        for p, d in zip(pairs, ds):
            d0, d1 = unpack(d, PAD)
            put(f2, 2 * p, d0)
            put(f2, 2 * p + 1, d1)
        return carry

    def apply():
        coef = c_ref[...].astype(BF)
        full = mm(coef, lct[...])
        a1[0, :ROWS, :] = full[:, :KB]
        a1[1, :ROWS, :] = full[:, KB:]
        lax.fori_loop(0, NR // 2 // UNROLL, middle, 0)
        last = slice(top * NR, (top + 1) * NR)
        lr, li, ur, ui = a1[0, 0:NR, :], a1[1, 0:NR, :], a1[0, last, :], a1[1, last, :]
        f2[0, 0:NR, :] = f2[0, 0:NR, :] - (lr + z1r * ur - z1i * ui) / KB
        f2[1, 0:NR, :] = f2[1, 0:NR, :] - (li + z1r * ui + z1i * ur) / KB
        f2[0, last, :] = f2[0, last, :] - (z1r * lr + z1i * li) / KB
        f2[1, last, :] = f2[1, last, :] - (z1r * li - z1i * lr) / KB
        h_ref[...] = mm(both_halves(f2), lc[...]) - mm(coef, ky)
        gram = fine_nt(wide(c_ref), wide(h_ref))
        gram = 0.5 * (gram + gram.T)
        eye = sublanes((NR, NR)) == lanes((NR, NR))
        trace = jnp.sum(jnp.sum(jnp.where(eye, gram, 0.0), axis=1, keepdims=True), axis=0, keepdims=True)
        return factor(gram + jnp.where(eye, RIDGE_SHARE * trace / NR + 1e-06, 0.0), 0.0)[1]

    def step(iteration, carry):
        @pl.when(iteration > 0)
        def _():
            tallput(h_ref, fine_mm(inv_ref[:, :NR], wide(h_ref)))
            c_ref[...] = wf[...] * h_ref[...]

        inv_ref[:, :NR] = apply()
        return carry

    lax.fori_loop(0, ITERS, step, 0)
    inverse = inv_ref[:, :NR]
    f2[0, :ROWS, :] = wf[...] * h_ref[...]
    moment = fine_nt(jnp.concatenate([f2[0, s * NR : (s + 1) * NR, :] for s in range(SLOTS)], axis=1), wide(h_ref))
    moment = jnp.dot(inverse, moment, precision=HI, preferred_element_type=F32)
    mixing = nt(moment, inverse, HI)
    mixing = 0.5 * (mixing + mixing.T)
    eye = sublanes((NR, NR)) == lanes((NR, NR))
    trace = jnp.sum(jnp.sum(jnp.where(eye, mixing, 0.0), axis=1, keepdims=True), axis=0, keepdims=True)
    root = factor(mixing, 1e-6 * trace + 1e-30)[0]
    combine = jnp.dot(root, inverse, precision=HI, preferred_element_type=F32)
    tallput(c_ref, fine_mm(combine, wide(c_ref)))
    coef = c_ref[...].astype(BF)
    full = mm(jnp.concatenate([coef, coef], axis=1), lct2[...])
    a1[0, :ROWS, :] = full[:, :KB]
    a1[1, :ROWS, :] = full[:, KB:]
    c2[:ROWS, :] = c_ref[...]
    c2[ROWS:, :] = jnp.zeros((PAD * NR - ROWS, KB), F32)

    def finish(q, carry):
        pairs = [q * UNROLL_F + j for j in range(UNROLL_F)]
        xs = [pack(get(a1, 2 * p), get(a1, 2 * p + 1)) for p in pairs]
        cols = [[mm(revt[...], c2[pl.ds(2 * p + e, PAD, stride=NR), :].astype(BF)).astype(BF) for e in range(2)] for p in pairs]
        ys = [mm(lc2[...], jnp.concatenate([x, x], axis=0).astype(BF)) for x in xs]
        ys = [jnp.concatenate([hat[0] * y[:KB] - hat[1] * y[KB:], hat[0] * y[KB:] + hat[1] * y[:KB]], axis=0).astype(BF) for y in ys]
        us = [mm(lbt[...], y) + mm(lbt_lo[...], y) for y in ys]
        for p, x, u, col in zip(pairs, xs, us, cols):
            xr, xi = x[0:1], x[PAD : PAD + 1]
            cr, ci = (q1r * xr - q1i * xi) / KB, (q1r * xi + q1i * xr) / KB
            u = u - jnp.where(urow == 0, cr, 0.0) - jnp.where(urow == KB, ci, 0.0)
            pair = unpack(u, KB)
            for e in range(2):
                ub = pair[e].astype(BF)
                out_ref[2 * p + e] = (mm(ub, lb[...]) + mm(ub, lb_lo[...]) - mm(col[e], kq2)).astype(BF)
        return carry

    lax.fori_loop(0, NR // 2 // UNROLL_F, finish, 0)


def synthesize(rank, tile_slit, sides, zernike, source_points, source_weight, start_block):
    ztab, inside = zernike_tables()
    wide = np.zeros((NZ, 96, KB), np.float32)
    wide[:, 8:89, 24:105] = ztab
    ins = np.zeros((96, KB), np.float32)
    ins[8:89, 24:105] = inside
    smem = pl.BlockSpec(memory_space=pltpu.SMEM)
    vmem = pl.BlockSpec(memory_space=pltpu.VMEM)
    tables = [jnp.asarray(t) for t in block_tables()]
    big = (2, PAD * NR, KB)
    return pl.pallas_call(
        synth_kernel,
        out_shape=jax.ShapeDtypeStruct((NR, KB, 2 * KB), BF),
        in_specs=[smem] * 2 + [vmem] * (8 + len(tables)),
        out_specs=vmem,
        scratch_shapes=[
            pltpu.VMEM((NR, KB), F32),
            pltpu.VMEM((3, KB, 2 * KB), F32),
            pltpu.VMEM(big, F32),
            pltpu.VMEM(big, F32),
            pltpu.VMEM((ROWS, KB), F32),
            pltpu.VMEM((ROWS, KB), F32),
            pltpu.VMEM((ROWS, KB), F32),
            pltpu.VMEM(big, F32),
            pltpu.VMEM((PAD * NR, KB), F32),
        ],
    )(rank.reshape(1), tile_slit, *sides, zernike, source_points.T, source_weight.reshape(1, -1), jnp.asarray(wide), jnp.asarray(ins), start_block, *tables)


def tables_of(count, period):
    t = dft(np.arange(count), np.arange(KB) - KB // 2, 1, period)
    return t.real.astype(np.float32), t.imag.astype(np.float32)


def cast(x):
    return np.ascontiguousarray(x).astype(jnp.bfloat16)


def column_table():
    cc, cs = tables_of(PW, PW)
    out = np.zeros((5 * TS, 2 * KB), np.float32)
    out[2 * TS - HALO : 2 * TS - HALO + PW] = np.concatenate([cc, -cs], 1)
    return cast(out)


def row_table():
    rc, rs = tables_of(TS, TS)
    return np.concatenate([rc, rs], 1)


def image_tables():
    rc, rs = tables_of(TS, TS)
    cc, cs = tables_of(PW, PW)
    turn = np.concatenate([rc.T, rs.T], 1)
    inv_t = np.concatenate([cc, -cs], 1)[HALO : HALO + TS].T
    adj = np.concatenate([cc, cs], 1)[HALO : HALO + TS]
    rows = row_table()
    return (column_table(),) + tuple(cast(x) for x in (rows.T, rows, turn, inv_t, adj))


def tile_columns(ref, tile):
    return ref[pl.ds(pl.multiple_of(TS * (3 - tile), TS), 2 * TS), :]


def image_kernel(rank_ref, m0, m1, m2, m3, kern_ref, fwd, rows_t, rows, turn, inv_t, adj, o0, o1, o2, o3, patch, goal, fields, inten, gsum, spec):
    rank = rank_ref[0]
    quarter = m0.shape[0]
    left, outer = rank < 2, (rank == 0) | (rank == 3)
    block_of = lambda j: pl.ds(pl.multiple_of((rank ^ j) * quarter, quarter), quarter)
    low_end, high_end = neighbour_marks(m0.at[:, 4 * TS : 4 * TS + SIDE], m0.at[:, 4 * TS + SIDE :])
    present = jnp.where(rank == 0, low_end, jnp.where(rank == 3, high_end, 1.0)) > 0.5
    for j, m in enumerate((m0, m1, m2, m3)):
        side = jnp.where(left, m[:, 4 * TS : 4 * TS + SIDE], m[:, 4 * TS + SIDE :])
        own = jnp.where(left, m[:, 2 * TS : 3 * TS], m[:, 3 * TS : 4 * TS])
        patch[block_of(j), : 2 * TS] = m[:, : 2 * TS]
        patch[block_of(j), 2 * TS :] = side[:, TS:]
        goal[block_of(j), :] = jnp.where(outer, side[:, :TS], own).astype(F32)
    s = 1.0 / math.sqrt(TS * PW)
    start = jnp.where(rank < 2, PW - rank * TS, 3 * TS - (rank - 2) * TS)
    side_table = fwd[pl.ds(pl.multiple_of(start, HALO), PW), :]
    table = jnp.concatenate([tile_columns(fwd, rank), side_table], axis=0)
    columns = mm(patch[...], table).astype(BF)
    sums = mm(rows_t[...], columns)
    spec[0] = s * (sums[:KB, :KB] + sums[KB:, KB:])
    spec[1] = s * (sums[:KB, KB:] - sums[KB:, :KB])
    inten[...] = jnp.zeros((TS, TS), F32)
    gsum[...] = jnp.zeros((KB, 2 * KB), F32)

    def forward(q, carry):
        ks = [q * UNROLL_I + e for e in range(UNROLL_I)]
        sr, si = spec[0], spec[1]
        blocks = []
        for k in ks:
            kr, ki = kern_ref[k, :, :KB].astype(F32), kern_ref[k, :, KB:].astype(F32)
            wr, wi = kr * sr + ki * si, kr * si - ki * sr
            blocks.append(jnp.concatenate([jnp.concatenate([wr, wi], axis=1), jnp.concatenate([-wi, wr], axis=1)], axis=0).astype(BF))
        waves = [mm(rows[...], b).astype(BF) for b in blocks]
        total = inten[...]
        for k, w in zip(ks, waves):
            field = mm(w, inv_t[...])
            fields[k] = field
            total = total + field * field
        inten[...] = total
        return carry

    lax.fori_loop(0, NR // UNROLL_I, forward, 0)
    resist = 1.0 / (1.0 + jnp.exp(-STEEPNESS * (inten[...] - THRESHOLD)))
    inten[...] = 4.0 * (resist - goal[...]) * STEEPNESS * resist * (1.0 - resist)
    goal[...] = resist

    def backward(q, carry):
        ks = [q * UNROLL_I + e for e in range(UNROLL_I)]
        cols = [mm((fields[k] * inten[...]).astype(BF), adj[...]) for k in ks]
        blocks = [jnp.concatenate([c, jnp.concatenate([-c[:, KB:], c[:, :KB]], axis=1)], axis=0).astype(BF) for c in cols]
        turned = [mm(turn[...], b) for b in blocks]
        gr, gi = gsum[:, :KB], gsum[:, KB:]
        for k, y in zip(ks, turned):
            kr, ki = kern_ref[k, :, :KB].astype(F32), kern_ref[k, :, KB:].astype(F32)
            gr = gr + kr * y[:, :KB] + ki * y[:, KB:]
            gi = gi + ki * y[:, :KB] - kr * y[:, KB:]
        gsum[:, :KB] = gr
        gsum[:, KB:] = gi
        return carry

    lax.fori_loop(0, NR // UNROLL_I, backward, 0)
    grad = jnp.where(present, s * gsum[...], 0.0)
    block = jnp.concatenate([grad, jnp.concatenate([-grad[:, KB:], grad[:, :KB]], axis=1)], axis=0).astype(BF)
    inten[...] = mm(rows[...], block)
    for j, o in enumerate((o0, o1, o2, o3)):
        o[:quarter, :] = inten[block_of(j), :].astype(BF)
        o[quarter:, :] = goal[block_of(j), :].astype(BF)


def imaging(rank, packs, kern):
    quarter = packs[0].shape[0]
    smem = pl.BlockSpec(memory_space=pltpu.SMEM)
    vmem = pl.BlockSpec(memory_space=pltpu.VMEM)
    tables = [jnp.asarray(x) for x in image_tables()]
    return pl.pallas_call(
        image_kernel,
        out_shape=(jax.ShapeDtypeStruct((2 * quarter, TS), BF),) * 4,
        in_specs=[smem] + [vmem] * (5 + len(tables)),
        out_specs=(vmem,) * 4,
        scratch_shapes=[
            pltpu.VMEM((TS, 2 * TS + PW), BF),
            pltpu.VMEM((TS, TS), F32),
            pltpu.VMEM((NR, TS, TS), F32),
            pltpu.VMEM((TS, TS), F32),
            pltpu.VMEM((KB, 2 * KB), F32),
            pltpu.VMEM((2, KB, KB), F32),
        ],
    )(rank.reshape(1), *packs, kern, *tables)


def back_kernel(rank_ref, n0, n1, n2, n3, fwd, resist_ref, grad_ref, held):
    rank = rank_ref[0]
    quarter, width = grad_ref.shape
    for j, n in enumerate((n0, n1, n2, n3)):
        held[rank ^ j] = n[...]
    resist_ref[:, :TS] = held[1, quarter:, :]
    resist_ref[:, TS:] = held[2, quarter:, :]
    parts = []
    for tile in range(4):
        parts.append(nt(held[tile, :quarter, :], fwd[TS * (3 - tile) : TS * (5 - tile), :]))
    grad_ref[...] = (parts[0] + parts[1] + parts[2] + parts[3]).astype(BF)


def back(rank, notes):
    quarter = notes[0].shape[0] // 2
    smem = pl.BlockSpec(memory_space=pltpu.SMEM)
    vmem = pl.BlockSpec(memory_space=pltpu.VMEM)
    whole = jax.ShapeDtypeStruct((quarter, 2 * TS), BF)
    return pl.pallas_call(
        back_kernel,
        out_shape=(whole, whole),
        in_specs=[smem] + [vmem] * 5,
        out_specs=(vmem, vmem),
        scratch_shapes=[pltpu.VMEM((4, 2 * quarter, TS), BF)],
    )(rank.reshape(1), *notes, jnp.asarray(column_table()))


def prep_kernel(slit_ref, mask, goal, right_ref, left_ref):
    quarter = mask.shape[0]
    lane = lanes((quarter, PW))
    right_ref[:, :TS] = goal[:, TS:]
    left_ref[:, :TS] = goal[:, :TS]
    first, second = (slit_ref[0] + 1).astype(F32), (slit_ref[1] + 1).astype(F32)
    right_ref[:, TS:] = jnp.where(lane < HALO, second, mask[:, 2 * TS - PW :].astype(F32)).astype(BF)
    left_ref[:, TS:] = jnp.where(lane >= PW - HALO, first, mask[:, :PW].astype(F32)).astype(BF)


def messages(tile_slit, mask, target):
    smem = pl.BlockSpec(memory_space=pltpu.SMEM)
    vmem = pl.BlockSpec(memory_space=pltpu.VMEM)
    return pl.pallas_call(
        prep_kernel,
        out_shape=(jax.ShapeDtypeStruct((mask.shape[0], SIDE), BF),) * 2,
        in_specs=[smem, vmem, vmem],
        out_specs=(vmem, vmem),
    )(tile_slit, mask, target)


def swap(x, m, size):
    return lax.ppermute(x, "src", [(i, i ^ m) for i in range(size)])


def shift(x, step, count):
    pairs = [(i, i + step) for i in range(count) if 0 <= i + step < count]
    return lax.ppermute(x, "tile", pairs)


def on_device(mask, target, start_block, zernike, source_points, source_weight, tile_slit):
    groups = lax.axis_size("tile")
    size = lax.axis_size("src")
    rank = lax.axis_index("src").astype(jnp.int32)
    rightward, leftward = messages(tile_slit, mask, target)
    from_left = shift(rightward, 1, groups)
    from_right = shift(leftward, -1, groups)
    pack = jnp.concatenate([mask, target, from_left, from_right], axis=1)
    packs = [pack] + [swap(pack, m, size) for m in (1, 2, 3)]
    kern = synthesize(rank, tile_slit, (from_left, from_right), zernike, source_points, source_weight, start_block)
    notes = imaging(rank, packs, kern)
    return tuple(back(rank, [notes[0]] + [swap(notes[m], m, size) for m in (1, 2, 3)]))


def solution(mesh):
    placed = (P("src", "tile"), P("src", "tile"), P(), P(), P(), P(), P("tile"))
    return jax.shard_map(
        on_device,
        mesh=mesh,
        in_specs=placed,
        out_specs=(P("src", "tile"), P("src", "tile")),
        check_vma=False,
    )
```

```python
import math

import jax
import jax.numpy as jnp
import numpy as np
from jax import lax
from jax.experimental import pallas as pl
from jax.experimental.pallas import tpu as pltpu
from jax.sharding import PartitionSpec as P

KB = 128
NR = 24
NZ = 37
RAD = 40
SHIFT = 24
HALO = 64
ITERS = 4
TS = 256
PW = TS + 2 * HALO
GRID = 2 * SHIFT + 1
PUP = 2 * RAD + 1

STEEPNESS = 4.0
THRESHOLD = 0.5
RIDGE_SHARE = 0.001
BF = jnp.bfloat16
F32 = jnp.float32


def noll_terms(term_count):
    listing = []
    degree = 0
    while len(listing) < term_count:
        for azimuth in range(degree % 2, degree + 1, 2):
            if azimuth == 0:
                listing.append((degree, 0, 0))
            else:
                for repeat in range(2):
                    number = len(listing) + 1
                    listing.append((degree, azimuth, 2 if number % 2 == 0 else 1))
        degree += 1
    return listing[:term_count]


def radial_terms(degree, azimuth):
    powers = []
    for counter in range((degree - azimuth) // 2 + 1):
        factor = (
            (-1) ** counter
            * math.factorial(degree - counter)
            / (
                math.factorial(counter)
                * math.factorial((degree + azimuth) // 2 - counter)
                * math.factorial((degree - azimuth) // 2 - counter)
            )
        )
        powers.append((degree - 2 * counter, factor))
    return powers


def zernike_tables():
    coords = np.arange(PUP) - RAD
    row, col = np.meshgrid(coords, coords, indexing="ij")
    radius = np.sqrt(row * row + col * col) / RAD
    angle = np.arctan2(col * 1.0, row * 1.0)
    out = []
    for degree, azimuth, parity in noll_terms(NZ):
        radial = sum(factor * radius**power for power, factor in radial_terms(degree, azimuth))
        if azimuth == 0:
            out.append(math.sqrt(degree + 1.0) * radial)
        elif parity == 2:
            out.append(math.sqrt(2.0 * degree + 2.0) * radial * np.cos(azimuth * angle))
        else:
            out.append(math.sqrt(2.0 * degree + 2.0) * radial * np.sin(azimuth * angle))
    inside = row * row + col * col <= RAD * RAD
    return np.stack(out) * inside, inside.astype(np.float32)


def dft(rows, cols, sign, period=KB):
    return np.exp(sign * 2j * np.pi * np.mod(np.outer(rows, cols), period) / period)


def cmul(a, b):
    return (a[0] * b[0] - a[1] * b[1], a[0] * b[1] + a[1] * b[0])


SLOTS = 50
SIDE = TS + PW
ROWS = SLOTS * NR
PAD = 64
HI = lax.Precision.HIGHEST
UNROLL = 6
UNROLL_S = 4
UNROLL_F = 4
UNROLL_I = 8


def real_form(table):
    return np.block([[table.real, -table.imag], [table.imag, table.real]])


def split(table):
    high = table.astype(np.float32).astype(jnp.bfloat16)
    low = (table - high.astype(np.float64)).astype(jnp.bfloat16)
    return high, low


def block_tables():
    freq = np.arange(KB)
    big = real_form(dft(freq, np.arange(KB) - KB // 2, -1))
    offs = np.zeros((KB, PAD), np.complex128)
    offs[:, :GRID] = dft(freq, np.arange(GRID) - SHIFT, 1)
    small = real_form(offs)
    rev = np.zeros((PAD, KB), np.float32)
    for spot in range(GRID):
        rev[spot, KB // 2 + SHIFT - spot] = 1.0
    lb, lb_lo = split(big)
    lbt, lbt_lo = split(big.T.copy())
    lc, lc_lo = split(small)
    lct, lct_lo = split(small.T.copy())
    wide = lambda a, b: np.concatenate([a, b], axis=1)
    tall = lambda a, b: np.concatenate([a, b], axis=0)
    return (lb, lbt, lc, lct, tall(lct, lct_lo), wide(lc, lc_lo), lbt_lo, lb_lo, rev.astype(jnp.bfloat16), rev.T.copy().astype(jnp.bfloat16))


def mm(a, b):
    return jnp.dot(a, b, preferred_element_type=F32)


def nt(a, b, precision=None):
    return lax.dot_general(a, b, (((1,), (1,)), ((), ())), precision=precision, preferred_element_type=F32)


def lanes(shape):
    return lax.broadcasted_iota(jnp.int32, shape, 1)


def sublanes(shape):
    return lax.broadcasted_iota(jnp.int32, shape, 0)


def halves(x):
    high = x.astype(BF)
    return high, (x - high.astype(F32)).astype(BF)


def stack_halves(x):
    return jnp.concatenate([part.astype(F32) for part in halves(x)], axis=0).astype(BF)


def fine_nt(a, b):
    full = nt(stack_halves(a), stack_halves(b))
    return full[:NR, :NR] + full[:NR, NR:] + full[NR:, :NR]


def fine_mm(a, b):
    ah, al = (x.astype(F32) for x in halves(a))
    bh, bl = (x.astype(F32) for x in halves(b))
    return mm(jnp.concatenate([ah, al, ah], axis=1).astype(BF), jnp.concatenate([bh, bh, bl], axis=0).astype(BF))


def factor(gram, floor):
    tile, blocks = 8, NR // 8
    rows = [slice(b * tile, (b + 1) * tile) for b in range(blocks)]
    wide_eye = (sublanes((NR, PAD)) == lanes((NR, PAD))).astype(F32)
    start = jnp.concatenate([gram, jnp.zeros((NR, PAD - NR), F32), wide_eye], axis=1)
    work = [start[x] for x in rows]
    col = [[jnp.broadcast_to(gram[x, j : j + 1], (tile, KB)) for x in rows] for j in range(NR)]
    row_no = sublanes((tile, KB))
    diag = [jnp.zeros((tile, KB), F32) for _ in rows]
    for k in range(NR):
        b0, r0 = divmod(k, tile)
        pick = lambda x: jnp.broadcast_to(x[r0 : r0 + 1, :], (tile, KB))
        pivot = jnp.maximum(pick(col[k][b0]), floor)
        diag[b0] = jnp.where(row_no == r0, pivot, diag[b0])
        inv = 1.0 / pivot
        ratio = [c * inv for c in col[k]]
        lead = pick(work[b0])
        for j in range(k + 1, NR):
            entry = pick(col[j][b0])
            for b in range(b0, blocks):
                col[j][b] = col[j][b] - ratio[b] * entry
        for b in range(b0, blocks):
            part = ratio[b] if b > b0 else jnp.where(row_no > r0, ratio[b], 0.0)
            work[b] = work[b] - part * lead
    done = jnp.concatenate([w * lax.rsqrt(d) for w, d in zip(work, diag)], axis=0)
    return done[:, :NR], done[:, PAD : PAD + NR]


def neighbour_marks(left_ref, right_ref):
    low = left_ref[0:16, TS : TS + KB].astype(F32)[0:1, 0:1]
    high = right_ref[0:16, SIDE - KB : SIDE].astype(F32)[0:1, KB - 1 : KB]
    return low, high


def pack(x0, x1):
    return jnp.concatenate(
        [jnp.concatenate([x0[:, :KB], x1[:, :KB]], axis=1), jnp.concatenate([x0[:, KB:], x1[:, KB:]], axis=1)], axis=0
    )


def put(ref, k, x):
    ref[0, pl.ds(k, PAD, stride=NR), :] = x[:, :KB]
    ref[1, pl.ds(k, PAD, stride=NR), :] = x[:, KB:]

def ground_kernel(order_ref, sp_ref, sw_ref, b0_ref, lb, lbt, rev, yb_ref, row_ref, edge_ref, wmap, bx):
    weights = sw_ref[...]
    weights = weights / (math.pi * RAD * RAD * jnp.sum(weights, axis=1, keepdims=True))
    count = sp_ref.shape[1]
    offset = sublanes((KB, count))
    hot_x = jnp.where(offset - SHIFT == sp_ref[0:1, :], weights, 0.0)
    hot_y = (jnp.where(offset >= PAD, offset - PAD, offset) - SHIFT == sp_ref[1:2, :]).astype(F32).astype(BF)
    high, low = halves(hot_x)
    wmap[...] = nt(high, hot_y) + nt(low, hot_y)

    def start(q, carry):
        pairs = [q * UNROLL_S + j for j in range(UNROLL_S)]
        blocks = [[jnp.concatenate([b0_ref[0, 2 * p + e], b0_ref[1, 2 * p + e]], axis=1).astype(BF) for e in range(2)] for p in pairs]
        xs = [pack(mm(b[0], lbt[...]), mm(b[1], lbt[...])) for b in blocks]
        revs = [[mm(rev[...], e) for e in b] for b in blocks]
        ys = [mm(lb[...], x.astype(BF)).astype(BF) for x in xs]
        for p, x, y, rv in zip(pairs, xs, ys, revs):
            yb_ref[p] = y
            row_ref[p, 0:1, :] = x[0:1]
            row_ref[p, 1:2, :] = x[KB : KB + 1]
            put(bx, 2 * p, rv[0])
            put(bx, 2 * p + 1, rv[1])
        return carry

    lax.fori_loop(0, NR // 2 // UNROLL_S, start, 0)
    lane = lanes((ROWS, KB))
    turned = pltpu.roll(bx[1, :ROWS, :], PAD, 1)
    edge_ref[...] = jnp.where(lane == 0, bx[0, :ROWS, :], jnp.where(lane == PAD, turned, 0.0)).astype(BF)


def ground(order, source_points, source_weight, start_block):
    vmem = pl.BlockSpec(memory_space=pltpu.VMEM)
    tables = block_tables()
    return pl.pallas_call(
        ground_kernel,
        out_shape=(
            jax.ShapeDtypeStruct((NR // 2, 2 * KB, 2 * KB), BF),
            jax.ShapeDtypeStruct((NR // 2, 2, 2 * KB), F32),
            jax.ShapeDtypeStruct((ROWS, KB), BF),
            jax.ShapeDtypeStruct((KB, KB), F32),
        ),
        in_specs=[pl.BlockSpec(memory_space=pl.ANY)] + [vmem] * 6,
        out_specs=(vmem,) * 4,
        scratch_shapes=[pltpu.VMEM((2, PAD * NR, KB), F32)],
    )(order, source_points.T, source_weight.reshape(1, -1), start_block, *[jnp.asarray(tables[i]) for i in (0, 1, 8)])


def synth_kernel(rank_ref, slit_ref, left_ref, right_ref, zern_ref, zt_ref, ins_ref, yb_ref, row_ref, edge_ref, wmap, lb, lbt, lc, lct, lct2, lc2, revt, out_ref, inv_ref, hat, a1, f2, c_ref, h_ref, wf):
    rank = rank_ref[0]
    low_end, high_end = neighbour_marks(left_ref, right_ref)
    slit = slit_ref[jnp.clip(rank - 1, 0, 1)].astype(F32)
    slit = jnp.where(rank == 0, low_end - 1.0, jnp.where(rank == 3, high_end - 1.0, slit))
    chosen = sublanes((zern_ref.shape[0], 1)).astype(F32) == jnp.maximum(slit, 0.0)
    coefs = jnp.sum(jnp.where(chosen, zern_ref[...], 0.0), axis=0, keepdims=True)
    turns = jnp.zeros((96, KB), F32)
    for z in range(NZ):
        turns = turns + coefs[:, z : z + 1] * zt_ref[z]
    turns = turns - jnp.floor(turns + 0.5)
    half = math.pi * turns
    sq = half * half
    sine = jnp.full_like(half, 1.0 / math.factorial(15))
    for n in (13, 11, 9, 7, 5, 3, 1):
        sine = 1.0 / math.factorial(n) - sine * sq
    sine = sine * half
    cosine = jnp.full_like(half, 1.0 / math.factorial(14))
    for n in (12, 10, 8, 6, 4, 2, 0):
        cosine = 1.0 / math.factorial(n) - cosine * sq
    pr = ins_ref[...] * (1.0 - 2.0 * sine * sine)
    pi = ins_ref[...] * (2.0 * sine * cosine)
    spot = lambda a, i, j: a[i : i + 1, j : j + 1]
    q1r, q1i = spot(pr, 88, 64), spot(pi, 88, 64)
    m1r, m1i = spot(pr, 8, 64), spot(pi, 8, 64)
    q2r, q2i = spot(pr, 48, 104), spot(pi, 48, 104)
    m2r, m2i = spot(pr, 48, 24), spot(pi, 48, 24)
    z1r, z1i = q1r * m1r + q1i * m1i, q1r * m1i - q1i * m1r
    z2r, z2i = q2r * m2r + q2i * m2i, q2r * m2i - q2i * m2r
    edge = jnp.zeros((16, 2 * KB), F32)
    both = jnp.concatenate([edge, jnp.concatenate([pr, pi], axis=1), edge], axis=0).astype(BF)
    ph = mm(both, lbt[...])
    stacked = jnp.concatenate([ph[:, :KB], ph[:, KB:]], axis=0).astype(BF)
    ph = mm(lb[...], stacked)
    hr, hi = ph[:KB], ph[KB:]
    hat[0] = jnp.concatenate([hr, hr], axis=1) / (KB * KB)
    hat[1] = jnp.concatenate([hi, hi], axis=1) / (KB * KB)
    power = (hr * hr + hi * hi) / (KB * KB)
    power = jnp.concatenate([power, power], axis=1)
    hat[2] = power

    for s in range(SLOTS):
        wf[s * NR : (s + 1) * NR, :] = jnp.broadcast_to(wmap[s : s + 1, :], (NR, KB))

    rs, cs = sublanes((KB, KB)), lanes((KB, KB))
    at = lambda i, j, v: jnp.where((rs == i) & (cs == j), v, 0.0)
    one = jnp.ones((1, 1), F32)
    top = 2 * SHIFT
    ky = (
        at(0, 0, one) + at(PAD, PAD, one)
        + at(top, 0, z2r) + at(PAD + top, 0, -z2i) + at(top, PAD, z2i) + at(PAD + top, PAD, z2r)
        + at(0, top, z2r) + at(PAD, top, z2i) + at(0, PAD + top, -z2i) + at(PAD, PAD + top, z2r)
    ).astype(BF)
    kq0 = (at(0, 0, q2r) + at(0, PAD, -q2i) + at(PAD, 0, q2i) + at(PAD, PAD, q2r)).astype(BF)
    kq2 = jnp.concatenate([at(0, 0, q2r) + at(PAD, 0, -q2i), at(0, 0, q2i) + at(PAD, 0, q2r)], axis=1).astype(BF)

    a1[:, ROWS:, :] = jnp.zeros((2, PAD * NR - ROWS, KB), F32)

    def unpack(y, height):
        return (
            jnp.concatenate([y[:height, :KB], y[height:, :KB]], axis=1),
            jnp.concatenate([y[:height, KB:], y[height:, KB:]], axis=1),
        )

    def get(ref, k):
        return jnp.concatenate([ref[0, pl.ds(k, PAD, stride=NR), :], ref[1, pl.ds(k, PAD, stride=NR), :]], axis=1)

    def both_halves(ref):
        return jnp.concatenate([ref[0, :ROWS, :], ref[1, :ROWS, :]], axis=1).astype(BF)

    prow = sublanes((KB, 2 * KB))
    urow = sublanes((2 * KB, 2 * KB))

    def start(q, carry):
        pairs = [q * UNROLL_S + j for j in range(UNROLL_S)]
        ys = [yb_ref[p].astype(F32) for p in pairs]
        ys = [jnp.concatenate([hat[0] * y[:KB] + hat[1] * y[KB:], hat[0] * y[KB:] - hat[1] * y[:KB]], axis=0).astype(BF) for y in ys]
        ds = [mm(lct[...], y) for y in ys]
        for p, d in zip(pairs, ds):
            xr, xi = row_ref[p, 0:1, :], row_ref[p, 1:2, :]
            cr, ci = (q1r * xr + q1i * xi) / KB, (q1r * xi - q1i * xr) / KB
            d = d - jnp.where(prow == 0, cr, 0.0) - jnp.where(prow == PAD, ci, 0.0)
            d0, d1 = unpack(d, PAD)
            put(f2, 2 * p, d0)
            put(f2, 2 * p + 1, d1)
        return carry

    lax.fori_loop(0, NR // 2 // UNROLL_S, start, 0)
    first = mm(both_halves(f2), lc[...]) - mm(edge_ref[...], kq0)
    c_ref[...] = wf[...] * first

    def wide(ref):
        return jnp.concatenate([ref[s * NR : (s + 1) * NR, :] for s in range(SLOTS)], axis=1)

    def tallput(ref, x):
        for s in range(SLOTS):
            ref[s * NR : (s + 1) * NR, :] = x[:, s * KB : (s + 1) * KB]

    def forward(p):
        return pack(get(a1, 2 * p), get(a1, 2 * p + 1)).astype(BF)

    def middle(q, carry):
        pairs = [q * UNROLL + j for j in range(UNROLL)]
        ys = [mm(lc[...], forward(p)) for p in pairs]
        ys = [jnp.concatenate([hat[2] * y[:KB], hat[2] * y[KB:]], axis=0).astype(BF) for y in ys]
        ds = [mm(lct[...], y) for y in ys]
        for p, d in zip(pairs, ds):
            d0, d1 = unpack(d, PAD)
            put(f2, 2 * p, d0)
            put(f2, 2 * p + 1, d1)
        return carry

    def apply():
        coef = c_ref[...].astype(BF)
        full = mm(coef, lct[...])
        a1[0, :ROWS, :] = full[:, :KB]
        a1[1, :ROWS, :] = full[:, KB:]
        lax.fori_loop(0, NR // 2 // UNROLL, middle, 0)
        last = slice(top * NR, (top + 1) * NR)
        lr, li, ur, ui = a1[0, 0:NR, :], a1[1, 0:NR, :], a1[0, last, :], a1[1, last, :]
        f2[0, 0:NR, :] = f2[0, 0:NR, :] - (lr + z1r * ur - z1i * ui) / KB
        f2[1, 0:NR, :] = f2[1, 0:NR, :] - (li + z1r * ui + z1i * ur) / KB
        f2[0, last, :] = f2[0, last, :] - (z1r * lr + z1i * li) / KB
        f2[1, last, :] = f2[1, last, :] - (z1r * li - z1i * lr) / KB
        h_ref[...] = mm(both_halves(f2), lc[...]) - mm(coef, ky)
        gram = fine_nt(wide(c_ref), wide(h_ref))
        gram = 0.5 * (gram + gram.T)
        eye = sublanes((NR, NR)) == lanes((NR, NR))
        trace = jnp.sum(jnp.sum(jnp.where(eye, gram, 0.0), axis=1, keepdims=True), axis=0, keepdims=True)
        return factor(gram + jnp.where(eye, RIDGE_SHARE * trace / NR + 1e-06, 0.0), 0.0)[1]

    def step(iteration, carry):
        @pl.when(iteration > 0)
        def _():
            tallput(h_ref, fine_mm(inv_ref[:, :NR], wide(h_ref)))
            c_ref[...] = wf[...] * h_ref[...]

        inv_ref[:, :NR] = apply()
        return carry

    lax.fori_loop(0, ITERS, step, 0)
    inverse = inv_ref[:, :NR]
    f2[0, :ROWS, :] = wf[...] * h_ref[...]
    moment = fine_nt(jnp.concatenate([f2[0, s * NR : (s + 1) * NR, :] for s in range(SLOTS)], axis=1), wide(h_ref))
    moment = jnp.dot(inverse, moment, precision=HI, preferred_element_type=F32)
    mixing = nt(moment, inverse, HI)
    mixing = 0.5 * (mixing + mixing.T)
    eye = sublanes((NR, NR)) == lanes((NR, NR))
    trace = jnp.sum(jnp.sum(jnp.where(eye, mixing, 0.0), axis=1, keepdims=True), axis=0, keepdims=True)
    root = factor(mixing, 1e-6 * trace + 1e-30)[0]
    combine = jnp.dot(root, inverse, precision=HI, preferred_element_type=F32)
    tallput(c_ref, fine_mm(combine, wide(c_ref)))
    coef = c_ref[...].astype(BF)
    full = mm(jnp.concatenate([coef, coef], axis=1), lct2[...])
    a1[0, :ROWS, :] = full[:, :KB]
    a1[1, :ROWS, :] = full[:, KB:]
    shifted = mm(coef, kq2)
    f2[0, :ROWS, :] = shifted[:, :KB]
    f2[1, :ROWS, :] = shifted[:, KB:]
    f2[:, ROWS:, :] = jnp.zeros((2, PAD * NR - ROWS, KB), F32)

    def finish(q, carry):
        pairs = [q * UNROLL_F + j for j in range(UNROLL_F)]
        xs = [pack(get(a1, 2 * p), get(a1, 2 * p + 1)) for p in pairs]
        cols = [[mm(revt[...], get(f2, 2 * p + e).astype(BF)) for e in range(2)] for p in pairs]
        ys = [mm(lc2[...], jnp.concatenate([x, x], axis=0).astype(BF)) for x in xs]
        ys = [jnp.concatenate([hat[0] * y[:KB] - hat[1] * y[KB:], hat[0] * y[KB:] + hat[1] * y[:KB]], axis=0).astype(BF) for y in ys]
        us = [mm(lbt[...], y) for y in ys]
        for p, x, u, col in zip(pairs, xs, us, cols):
            xr, xi = x[0:1], x[PAD : PAD + 1]
            cr, ci = (q1r * xr - q1i * xi) / KB, (q1r * xi + q1i * xr) / KB
            u = u - jnp.where(urow == 0, cr, 0.0) - jnp.where(urow == KB, ci, 0.0)
            pair = unpack(u, KB)
            for e in range(2):
                ub = pair[e].astype(BF)
                out_ref[2 * p + e] = (mm(ub, lb[...]) - col[e]).astype(BF)
        return carry

    lax.fori_loop(0, NR // 2 // UNROLL_F, finish, 0)


def synthesize(rank, tile_slit, sides, zernike, base):
    ztab, inside = zernike_tables()
    wide = np.zeros((NZ, 96, KB), np.float32)
    wide[:, 8:89, 24:105] = ztab
    ins = np.zeros((96, KB), np.float32)
    ins[8:89, 24:105] = inside
    smem = pl.BlockSpec(memory_space=pltpu.SMEM)
    vmem = pl.BlockSpec(memory_space=pltpu.VMEM)
    tables = block_tables()
    tables = [jnp.asarray(tables[i]) for i in (0, 1, 2, 3, 4, 5, 9)]
    big = (2, PAD * NR, KB)
    return pl.pallas_call(
        synth_kernel,
        out_shape=jax.ShapeDtypeStruct((NR, KB, 2 * KB), BF),
        in_specs=[smem] * 2 + [vmem] * (9 + len(tables)),
        out_specs=vmem,
        scratch_shapes=[
            pltpu.VMEM((NR, KB), F32),
            pltpu.VMEM((3, KB, 2 * KB), F32),
            pltpu.VMEM(big, F32),
            pltpu.VMEM(big, F32),
            pltpu.VMEM((ROWS, KB), F32),
            pltpu.VMEM((ROWS, KB), F32),
            pltpu.VMEM((ROWS, KB), F32),
        ],
    )(rank.reshape(1), tile_slit, *sides, zernike, jnp.asarray(wide), jnp.asarray(ins), *base, *tables)


def tables_of(count, period):
    t = dft(np.arange(count), np.arange(KB) - KB // 2, 1, period)
    return t.real.astype(np.float32), t.imag.astype(np.float32)


def cast(x):
    return np.ascontiguousarray(x).astype(jnp.bfloat16)


def column_table():
    cc, cs = tables_of(PW, PW)
    out = np.zeros((5 * TS, 2 * KB), np.float32)
    out[2 * TS - HALO : 2 * TS - HALO + PW] = np.concatenate([cc, -cs], 1)
    return cast(out)


def row_table():
    rc, rs = tables_of(TS, TS)
    return np.concatenate([rc, rs], 1)


def image_tables():
    rc, rs = tables_of(TS, TS)
    cc, cs = tables_of(PW, PW)
    turn = np.concatenate([rc.T, rs.T], 1)
    inv_t = np.concatenate([cc, -cs], 1)[HALO : HALO + TS].T
    adj = np.concatenate([cc, cs], 1)[HALO : HALO + TS]
    rows = row_table()
    return (column_table(),) + tuple(cast(x) for x in (rows.T, rows, turn, inv_t, adj))


def tile_columns(ref, tile):
    return ref[pl.ds(pl.multiple_of(TS * (3 - tile), TS), 2 * TS), :]


def image_kernel(rank_ref, m0, m1, m2, m3, kern_ref, fwd, rows_t, rows, turn, inv_t, adj, o0, o1, o2, o3, patch, goal, fields, inten, gsum, spec):
    rank = rank_ref[0]
    quarter = m0.shape[0]
    left, outer = rank < 2, (rank == 0) | (rank == 3)
    block_of = lambda j: pl.ds(pl.multiple_of((rank ^ j) * quarter, quarter), quarter)
    low_end, high_end = neighbour_marks(m0.at[:, 4 * TS : 4 * TS + SIDE], m0.at[:, 4 * TS + SIDE :])
    present = jnp.where(rank == 0, low_end, jnp.where(rank == 3, high_end, 1.0)) > 0.5
    for j, m in enumerate((m0, m1, m2, m3)):
        side = jnp.where(left, m[:, 4 * TS : 4 * TS + SIDE], m[:, 4 * TS + SIDE :])
        own = jnp.where(left, m[:, 2 * TS : 3 * TS], m[:, 3 * TS : 4 * TS])
        patch[block_of(j), : 2 * TS] = m[:, : 2 * TS]
        patch[block_of(j), 2 * TS :] = side[:, TS:]
        goal[block_of(j), :] = jnp.where(outer, side[:, :TS], own).astype(F32)
    s = 1.0 / math.sqrt(TS * PW)
    start = jnp.where(rank < 2, PW - rank * TS, 3 * TS - (rank - 2) * TS)
    side_table = fwd[pl.ds(pl.multiple_of(start, HALO), PW), :]
    table = jnp.concatenate([tile_columns(fwd, rank), side_table], axis=0)
    columns = mm(patch[...], table).astype(BF)
    sums = mm(rows_t[...], columns)
    spec[0] = s * (sums[:KB, :KB] + sums[KB:, KB:])
    spec[1] = s * (sums[:KB, KB:] - sums[KB:, :KB])
    inten[...] = jnp.zeros((TS, TS), F32)
    gsum[...] = jnp.zeros((KB, 2 * KB), F32)

    def forward(q, carry):
        ks = [q * UNROLL_I + e for e in range(UNROLL_I)]
        sr, si = spec[0], spec[1]
        blocks = []
        for k in ks:
            kr, ki = kern_ref[k, :, :KB].astype(F32), kern_ref[k, :, KB:].astype(F32)
            wr, wi = kr * sr + ki * si, kr * si - ki * sr
            blocks.append(jnp.concatenate([jnp.concatenate([wr, wi], axis=1), jnp.concatenate([-wi, wr], axis=1)], axis=0).astype(BF))
        waves = [mm(rows[...], b).astype(BF) for b in blocks]
        total = inten[...]
        for k, w in zip(ks, waves):
            field = mm(w, inv_t[...])
            fields[k] = field
            total = total + field * field
        inten[...] = total
        return carry

    lax.fori_loop(0, NR // UNROLL_I, forward, 0)
    resist = 1.0 / (1.0 + jnp.exp(-STEEPNESS * (inten[...] - THRESHOLD)))
    inten[...] = 4.0 * (resist - goal[...]) * STEEPNESS * resist * (1.0 - resist)
    goal[...] = resist

    def backward(q, carry):
        ks = [q * UNROLL_I + e for e in range(UNROLL_I)]
        cols = [mm((fields[k] * inten[...]).astype(BF), adj[...]) for k in ks]
        blocks = [jnp.concatenate([c, jnp.concatenate([-c[:, KB:], c[:, :KB]], axis=1)], axis=0).astype(BF) for c in cols]
        turned = [mm(turn[...], b) for b in blocks]
        gr, gi = gsum[:, :KB], gsum[:, KB:]
        for k, y in zip(ks, turned):
            kr, ki = kern_ref[k, :, :KB].astype(F32), kern_ref[k, :, KB:].astype(F32)
            gr = gr + kr * y[:, :KB] + ki * y[:, KB:]
            gi = gi + ki * y[:, :KB] - kr * y[:, KB:]
        gsum[:, :KB] = gr
        gsum[:, KB:] = gi
        return carry

    lax.fori_loop(0, NR // UNROLL_I, backward, 0)
    grad = jnp.where(present, s * gsum[...], 0.0)
    block = jnp.concatenate([grad, jnp.concatenate([-grad[:, KB:], grad[:, :KB]], axis=1)], axis=0).astype(BF)
    inten[...] = mm(rows[...], block)
    for j, o in enumerate((o0, o1, o2, o3)):
        o[:quarter, :] = inten[block_of(j), :].astype(BF)
        o[quarter:, :] = goal[block_of(j), :].astype(BF)


def imaging(rank, packs, kern):
    quarter = packs[0].shape[0]
    smem = pl.BlockSpec(memory_space=pltpu.SMEM)
    vmem = pl.BlockSpec(memory_space=pltpu.VMEM)
    tables = [jnp.asarray(x) for x in image_tables()]
    return pl.pallas_call(
        image_kernel,
        out_shape=(jax.ShapeDtypeStruct((2 * quarter, TS), BF),) * 4,
        in_specs=[smem] + [vmem] * (5 + len(tables)),
        out_specs=(vmem,) * 4,
        scratch_shapes=[
            pltpu.VMEM((TS, 2 * TS + PW), BF),
            pltpu.VMEM((TS, TS), F32),
            pltpu.VMEM((NR, TS, TS), F32),
            pltpu.VMEM((TS, TS), F32),
            pltpu.VMEM((KB, 2 * KB), F32),
            pltpu.VMEM((2, KB, KB), F32),
        ],
    )(rank.reshape(1), *packs, kern, *tables)


def back_kernel(rank_ref, n0, n1, n2, n3, fwd, resist_ref, grad_ref, held):
    rank = rank_ref[0]
    quarter, width = grad_ref.shape
    for j, n in enumerate((n0, n1, n2, n3)):
        held[rank ^ j] = n[...]
    resist_ref[:, :TS] = held[1, quarter:, :]
    resist_ref[:, TS:] = held[2, quarter:, :]
    parts = []
    for tile in range(4):
        parts.append(nt(held[tile, :quarter, :], fwd[TS * (3 - tile) : TS * (5 - tile), :]))
    grad_ref[...] = (parts[0] + parts[1] + parts[2] + parts[3]).astype(BF)


def back(rank, notes):
    quarter = notes[0].shape[0] // 2
    smem = pl.BlockSpec(memory_space=pltpu.SMEM)
    vmem = pl.BlockSpec(memory_space=pltpu.VMEM)
    whole = jax.ShapeDtypeStruct((quarter, 2 * TS), BF)
    return pl.pallas_call(
        back_kernel,
        out_shape=(whole, whole),
        in_specs=[smem] + [vmem] * 5,
        out_specs=(vmem, vmem),
        scratch_shapes=[pltpu.VMEM((4, 2 * quarter, TS), BF)],
    )(rank.reshape(1), *notes, jnp.asarray(column_table()))


def prep_kernel(slit_ref, mask, goal, right_ref, left_ref):
    quarter = mask.shape[0]
    lane = lanes((quarter, PW))
    right_ref[:, :TS] = goal[:, TS:]
    left_ref[:, :TS] = goal[:, :TS]
    first, second = (slit_ref[0] + 1).astype(F32), (slit_ref[1] + 1).astype(F32)
    right_ref[:, TS:] = jnp.where(lane < HALO, second, mask[:, 2 * TS - PW :].astype(F32)).astype(BF)
    left_ref[:, TS:] = jnp.where(lane >= PW - HALO, first, mask[:, :PW].astype(F32)).astype(BF)


def messages(tile_slit, mask, target):
    smem = pl.BlockSpec(memory_space=pltpu.SMEM)
    vmem = pl.BlockSpec(memory_space=pltpu.VMEM)
    return pl.pallas_call(
        prep_kernel,
        out_shape=(jax.ShapeDtypeStruct((mask.shape[0], SIDE), BF),) * 2,
        in_specs=[smem, vmem, vmem],
        out_specs=(vmem, vmem),
    )(tile_slit, mask, target)


def swap(x, m, size):
    return lax.ppermute(x, "src", [(i, i ^ m) for i in range(size)])


def shift(x, step, count):
    pairs = [(i, i + step) for i in range(count) if 0 <= i + step < count]
    return lax.ppermute(x, "tile", pairs)


def on_device(mask, target, start_block, zernike, source_points, source_weight, tile_slit):
    groups = lax.axis_size("tile")
    size = lax.axis_size("src")
    rank = lax.axis_index("src").astype(jnp.int32)
    rightward, leftward = messages(tile_slit, mask, target)
    from_left = shift(rightward, 1, groups)
    from_right = shift(leftward, -1, groups)
    base = ground(rightward, source_points, source_weight, start_block)
    from_left, from_right, *base = lax.optimization_barrier((from_left, from_right, *base))
    pack = jnp.concatenate([mask, target, from_left, from_right], axis=1)
    packs = [pack] + [swap(pack, m, size) for m in (1, 2, 3)]
    kern = synthesize(rank, tile_slit, (from_left, from_right), zernike, base)
    notes = imaging(rank, packs, kern)
    return tuple(back(rank, [notes[0]] + [swap(notes[m], m, size) for m in (1, 2, 3)]))


def solution(mesh):
    placed = (P("src", "tile"), P("src", "tile"), P(), P(), P(), P(), P("tile"))
    return jax.shard_map(
        on_device,
        mesh=mesh,
        in_specs=placed,
        out_specs=(P("src", "tile"), P("src", "tile")),
        check_vma=False,
    )
```

```python
import math

import jax
import jax.numpy as jnp
import numpy as np
from jax import lax
from jax.experimental import pallas as pl
from jax.experimental.pallas import tpu as pltpu
from jax.sharding import PartitionSpec as P

KB = 128
NR = 24
NZ = 37
RAD = 40
SHIFT = 24
HALO = 64
ITERS = 4
TS = 256
PW = TS + 2 * HALO
GRID = 2 * SHIFT + 1
PUP = 2 * RAD + 1

STEEPNESS = 4.0
THRESHOLD = 0.5
RIDGE_SHARE = 0.001
BF = jnp.bfloat16
F32 = jnp.float32


def noll_terms(term_count):
    listing = []
    degree = 0
    while len(listing) < term_count:
        for azimuth in range(degree % 2, degree + 1, 2):
            if azimuth == 0:
                listing.append((degree, 0, 0))
            else:
                for repeat in range(2):
                    number = len(listing) + 1
                    listing.append((degree, azimuth, 2 if number % 2 == 0 else 1))
        degree += 1
    return listing[:term_count]


def radial_terms(degree, azimuth):
    powers = []
    for counter in range((degree - azimuth) // 2 + 1):
        factor = (
            (-1) ** counter
            * math.factorial(degree - counter)
            / (
                math.factorial(counter)
                * math.factorial((degree + azimuth) // 2 - counter)
                * math.factorial((degree - azimuth) // 2 - counter)
            )
        )
        powers.append((degree - 2 * counter, factor))
    return powers


def zernike_tables():
    coords = np.arange(PUP) - RAD
    row, col = np.meshgrid(coords, coords, indexing="ij")
    radius = np.sqrt(row * row + col * col) / RAD
    angle = np.arctan2(col * 1.0, row * 1.0)
    out = []
    for degree, azimuth, parity in noll_terms(NZ):
        radial = sum(factor * radius**power for power, factor in radial_terms(degree, azimuth))
        if azimuth == 0:
            out.append(math.sqrt(degree + 1.0) * radial)
        elif parity == 2:
            out.append(math.sqrt(2.0 * degree + 2.0) * radial * np.cos(azimuth * angle))
        else:
            out.append(math.sqrt(2.0 * degree + 2.0) * radial * np.sin(azimuth * angle))
    inside = row * row + col * col <= RAD * RAD
    return np.stack(out) * inside, inside.astype(np.float32)


def dft(rows, cols, sign, period=KB):
    return np.exp(sign * 2j * np.pi * np.mod(np.outer(rows, cols), period) / period)


def cmul(a, b):
    return (a[0] * b[0] - a[1] * b[1], a[0] * b[1] + a[1] * b[0])


SLOTS = 50
VMEM_CAP = 32 << 20
SIDE = TS + PW
ROWS = SLOTS * NR
PAD = 64
HI = lax.Precision.HIGHEST
UNROLL = 6
UNROLL_S = 4
UNROLL_F = 4
UNROLL_I = 8


def real_form(table):
    return np.block([[table.real, -table.imag], [table.imag, table.real]])


def split(table):
    high = table.astype(np.float32).astype(jnp.bfloat16)
    low = (table - high.astype(np.float64)).astype(jnp.bfloat16)
    return high, low


def block_tables():
    freq = np.arange(KB)
    big = real_form(dft(freq, np.arange(KB) - KB // 2, -1))
    offs = np.zeros((KB, PAD), np.complex128)
    offs[:, :GRID] = dft(freq, np.arange(GRID) - SHIFT, 1)
    small = real_form(offs)
    rev = np.zeros((PAD, KB), np.float32)
    for spot in range(GRID):
        rev[spot, KB // 2 + SHIFT - spot] = 1.0
    lb, lb_lo = split(big)
    lbt, lbt_lo = split(big.T.copy())
    lc, lc_lo = split(small)
    lct, lct_lo = split(small.T.copy())
    wide = lambda a, b: np.concatenate([a, b], axis=1)
    tall = lambda a, b: np.concatenate([a, b], axis=0)
    return (lb, lbt, lc, lct, tall(lct, lct_lo), wide(lc, lc_lo), lbt_lo, lb_lo, rev.astype(jnp.bfloat16), rev.T.copy().astype(jnp.bfloat16))


def near(*arrays):
    return tuple(pltpu.with_memory_space_constraint(x, pltpu.VMEM) for x in arrays)


def far(*arrays):
    return tuple(pltpu.with_memory_space_constraint(x, pltpu.HBM) for x in arrays)


def mm(a, b):
    return jnp.dot(a, b, preferred_element_type=F32)


def nt(a, b, precision=None):
    return lax.dot_general(a, b, (((1,), (1,)), ((), ())), precision=precision, preferred_element_type=F32)


def lanes(shape):
    return lax.broadcasted_iota(jnp.int32, shape, 1)


def sublanes(shape):
    return lax.broadcasted_iota(jnp.int32, shape, 0)


def halves(x):
    high = x.astype(BF)
    return high, (x - high.astype(F32)).astype(BF)


def stack_halves(x):
    return jnp.concatenate([part.astype(F32) for part in halves(x)], axis=0).astype(BF)


def fine_nt(a, b):
    full = nt(stack_halves(a), stack_halves(b))
    return full[:NR, :NR] + full[:NR, NR:] + full[NR:, :NR]


def fine_mm(a, b):
    ah, al = (x.astype(F32) for x in halves(a))
    bh, bl = (x.astype(F32) for x in halves(b))
    return mm(jnp.concatenate([ah, al, ah], axis=1).astype(BF), jnp.concatenate([bh, bh, bl], axis=0).astype(BF))


def factor(gram, floor):
    tile, blocks = 8, NR // 8
    rows = [slice(b * tile, (b + 1) * tile) for b in range(blocks)]
    wide_eye = (sublanes((NR, PAD)) == lanes((NR, PAD))).astype(F32)
    start = jnp.concatenate([gram, jnp.zeros((NR, PAD - NR), F32), wide_eye], axis=1)
    work = [start[x] for x in rows]
    col = [[jnp.broadcast_to(gram[x, j : j + 1], (tile, KB)) for x in rows] for j in range(NR)]
    row_no = sublanes((tile, KB))
    diag = [jnp.zeros((tile, KB), F32) for _ in rows]
    for k in range(NR):
        b0, r0 = divmod(k, tile)
        pick = lambda x: jnp.broadcast_to(x[r0 : r0 + 1, :], (tile, KB))
        pivot = jnp.maximum(pick(col[k][b0]), floor)
        diag[b0] = jnp.where(row_no == r0, pivot, diag[b0])
        inv = 1.0 / pivot
        ratio = [c * inv for c in col[k]]
        lead = pick(work[b0])
        for j in range(k + 1, NR):
            entry = pick(col[j][b0])
            for b in range(b0, blocks):
                col[j][b] = col[j][b] - ratio[b] * entry
        for b in range(b0, blocks):
            part = ratio[b] if b > b0 else jnp.where(row_no > r0, ratio[b], 0.0)
            work[b] = work[b] - part * lead
    done = jnp.concatenate([w * lax.rsqrt(d) for w, d in zip(work, diag)], axis=0)
    return done[:, :NR], done[:, PAD : PAD + NR]


def neighbour_marks(left_ref, right_ref):
    low = left_ref[0:16, TS : TS + KB].astype(F32)[0:1, 0:1]
    high = right_ref[0:16, SIDE - KB : SIDE].astype(F32)[0:1, KB - 1 : KB]
    return low, high


def synth_kernel(rank_ref, slit_ref, left_ref, right_ref, zern_ref, sp_ref, sw_ref, ins_ref, lb, lbt, lc, lct, lct2, lc2, rev, revt, zt_far, b0_far, out_ref, inv_ref, hat, a1, f2, c_ref, h_ref, wf, bx, zt_ref, b0_ref, sems):
    zt_copy = pltpu.make_async_copy(zt_far, zt_ref, sems.at[0])
    b0_copy = pltpu.make_async_copy(b0_far, b0_ref, sems.at[1])
    zt_copy.start()
    b0_copy.start()
    weights = sw_ref[...]
    weights = weights / (math.pi * RAD * RAD * jnp.sum(weights, axis=1, keepdims=True))
    count = sp_ref.shape[1]
    offset = sublanes((KB, count))
    hot_x = jnp.where(offset - SHIFT == sp_ref[0:1, :], weights, 0.0)
    hot_y = (jnp.where(offset >= PAD, offset - PAD, offset) - SHIFT == sp_ref[1:2, :]).astype(F32).astype(BF)
    high, low = halves(hot_x)
    wmap = nt(high, hot_y) + nt(low, hot_y)
    for s in range(SLOTS):
        wf[s * NR : (s + 1) * NR, :] = jnp.broadcast_to(wmap[s : s + 1, :], (NR, KB))

    rank = rank_ref[0]
    low_end, high_end = neighbour_marks(left_ref, right_ref)
    slit = slit_ref[jnp.clip(rank - 1, 0, 1)].astype(F32)
    slit = jnp.where(rank == 0, low_end - 1.0, jnp.where(rank == 3, high_end - 1.0, slit))
    chosen = sublanes((zern_ref.shape[0], 1)).astype(F32) == jnp.maximum(slit, 0.0)
    coefs = jnp.sum(jnp.where(chosen, zern_ref[...], 0.0), axis=0, keepdims=True)
    zt_copy.wait()
    turns = jnp.zeros((96, KB), F32)
    for z in range(NZ):
        turns = turns + coefs[:, z : z + 1] * zt_ref[z]
    turns = turns - jnp.floor(turns + 0.5)
    half = math.pi * turns
    sq = half * half
    sine = jnp.full_like(half, 1.0 / math.factorial(15))
    for n in (13, 11, 9, 7, 5, 3, 1):
        sine = 1.0 / math.factorial(n) - sine * sq
    sine = sine * half
    cosine = jnp.full_like(half, 1.0 / math.factorial(14))
    for n in (12, 10, 8, 6, 4, 2, 0):
        cosine = 1.0 / math.factorial(n) - cosine * sq
    pr = ins_ref[...] * (1.0 - 2.0 * sine * sine)
    pi = ins_ref[...] * (2.0 * sine * cosine)
    spot = lambda a, i, j: a[i : i + 1, j : j + 1]
    q1r, q1i = spot(pr, 88, 64), spot(pi, 88, 64)
    m1r, m1i = spot(pr, 8, 64), spot(pi, 8, 64)
    q2r, q2i = spot(pr, 48, 104), spot(pi, 48, 104)
    m2r, m2i = spot(pr, 48, 24), spot(pi, 48, 24)
    z1r, z1i = q1r * m1r + q1i * m1i, q1r * m1i - q1i * m1r
    z2r, z2i = q2r * m2r + q2i * m2i, q2r * m2i - q2i * m2r
    edge = jnp.zeros((16, 2 * KB), F32)
    both = jnp.concatenate([edge, jnp.concatenate([pr, pi], axis=1), edge], axis=0).astype(BF)
    ph = mm(both, lbt[...])
    stacked = jnp.concatenate([ph[:, :KB], ph[:, KB:]], axis=0).astype(BF)
    ph = mm(lb[...], stacked)
    hr, hi = ph[:KB], ph[KB:]
    hat[0] = jnp.concatenate([hr, hr], axis=1) / (KB * KB)
    hat[1] = jnp.concatenate([hi, hi], axis=1) / (KB * KB)
    power = (hr * hr + hi * hi) / (KB * KB)
    power = jnp.concatenate([power, power], axis=1)
    hat[2] = power

    rs, cs = sublanes((KB, KB)), lanes((KB, KB))
    at = lambda i, j, v: jnp.where((rs == i) & (cs == j), v, 0.0)
    one = jnp.ones((1, 1), F32)
    top = 2 * SHIFT
    ky = (
        at(0, 0, one) + at(PAD, PAD, one)
        + at(top, 0, z2r) + at(PAD + top, 0, -z2i) + at(top, PAD, z2i) + at(PAD + top, PAD, z2r)
        + at(0, top, z2r) + at(PAD, top, z2i) + at(0, PAD + top, -z2i) + at(PAD, PAD + top, z2r)
    ).astype(BF)
    kq0 = jnp.concatenate([at(0, 0, q2r) + at(0, PAD, -q2i), at(0, 0, q2i) + at(0, PAD, q2r)], axis=0).astype(BF)
    kq2 = jnp.concatenate([at(0, 0, q2r) + at(PAD, 0, -q2i), at(0, 0, q2i) + at(PAD, 0, q2r)], axis=1).astype(BF)

    a1[:, ROWS:, :] = jnp.zeros((2, PAD * NR - ROWS, KB), F32)

    def pack(x0, x1):
        return jnp.concatenate(
            [jnp.concatenate([x0[:, :KB], x1[:, :KB]], axis=1), jnp.concatenate([x0[:, KB:], x1[:, KB:]], axis=1)], axis=0
        )

    def unpack(y, height):
        return (
            jnp.concatenate([y[:height, :KB], y[height:, :KB]], axis=1),
            jnp.concatenate([y[:height, KB:], y[height:, KB:]], axis=1),
        )

    def put(ref, k, x):
        ref[0, pl.ds(k, PAD, stride=NR), :] = x[:, :KB]
        ref[1, pl.ds(k, PAD, stride=NR), :] = x[:, KB:]

    def get(ref, k):
        return jnp.concatenate([ref[0, pl.ds(k, PAD, stride=NR), :], ref[1, pl.ds(k, PAD, stride=NR), :]], axis=1)

    def both_halves(ref):
        return jnp.concatenate([ref[0, :ROWS, :], ref[1, :ROWS, :]], axis=1).astype(BF)

    prow = sublanes((KB, 2 * KB))
    urow = sublanes((2 * KB, 2 * KB))

    def start(q, carry):
        pairs = [q * UNROLL_S + j for j in range(UNROLL_S)]
        blocks = [[jnp.concatenate([b0_ref[0, 2 * p + e], b0_ref[1, 2 * p + e]], axis=1).astype(BF) for e in range(2)] for p in pairs]
        xs = [pack(mm(b[0], lbt[...]), mm(b[1], lbt[...])) for b in blocks]
        revs = [[mm(rev[...], e) for e in b] for b in blocks]
        ys = [mm(lb[...], x.astype(BF)) for x in xs]
        ys = [jnp.concatenate([hat[0] * y[:KB] + hat[1] * y[KB:], hat[0] * y[KB:] - hat[1] * y[:KB]], axis=0).astype(BF) for y in ys]
        ds = [mm(lct[...], y) for y in ys]
        for p, x, d, rv in zip(pairs, xs, ds, revs):
            xr, xi = x[0:1], x[KB : KB + 1]
            cr, ci = (q1r * xr + q1i * xi) / KB, (q1r * xi - q1i * xr) / KB
            d = d - jnp.where(prow == 0, cr, 0.0) - jnp.where(prow == PAD, ci, 0.0)
            d0, d1 = unpack(d, PAD)
            put(f2, 2 * p, d0)
            put(f2, 2 * p + 1, d1)
            put(bx, 2 * p, rv[0])
            put(bx, 2 * p + 1, rv[1])
        return carry

    b0_copy.wait()
    lax.fori_loop(0, NR // 2 // UNROLL_S, start, 0)
    first = mm(both_halves(f2), lc[...]) - mm(both_halves(bx), kq0)
    c_ref[...] = wf[...] * first

    def wide(ref):
        return jnp.concatenate([ref[s * NR : (s + 1) * NR, :] for s in range(SLOTS)], axis=1)

    def tallput(ref, x):
        for s in range(SLOTS):
            ref[s * NR : (s + 1) * NR, :] = x[:, s * KB : (s + 1) * KB]

    def forward(p):
        return pack(get(a1, 2 * p), get(a1, 2 * p + 1)).astype(BF)

    def middle(q, carry):
        pairs = [q * UNROLL + j for j in range(UNROLL)]
        ys = [mm(lc[...], forward(p)) for p in pairs]
        ys = [jnp.concatenate([hat[2] * y[:KB], hat[2] * y[KB:]], axis=0).astype(BF) for y in ys]
        ds = [mm(lct[...], y) for y in ys]
        for p, d in zip(pairs, ds):
            d0, d1 = unpack(d, PAD)
            put(f2, 2 * p, d0)
            put(f2, 2 * p + 1, d1)
        return carry

    def apply():
        coef = c_ref[...].astype(BF)
        full = mm(coef, lct[...])
        a1[0, :ROWS, :] = full[:, :KB]
        a1[1, :ROWS, :] = full[:, KB:]
        lax.fori_loop(0, NR // 2 // UNROLL, middle, 0)
        last = slice(top * NR, (top + 1) * NR)
        lr, li, ur, ui = a1[0, 0:NR, :], a1[1, 0:NR, :], a1[0, last, :], a1[1, last, :]
        f2[0, 0:NR, :] = f2[0, 0:NR, :] - (lr + z1r * ur - z1i * ui) / KB
        f2[1, 0:NR, :] = f2[1, 0:NR, :] - (li + z1r * ui + z1i * ur) / KB
        f2[0, last, :] = f2[0, last, :] - (z1r * lr + z1i * li) / KB
        f2[1, last, :] = f2[1, last, :] - (z1r * li - z1i * lr) / KB
        h_ref[...] = mm(both_halves(f2), lc[...]) - mm(coef, ky)
        gram = fine_nt(wide(c_ref), wide(h_ref))
        gram = 0.5 * (gram + gram.T)
        eye = sublanes((NR, NR)) == lanes((NR, NR))
        trace = jnp.sum(jnp.sum(jnp.where(eye, gram, 0.0), axis=1, keepdims=True), axis=0, keepdims=True)
        return factor(gram + jnp.where(eye, RIDGE_SHARE * trace / NR + 1e-06, 0.0), 0.0)[1]

    def step(iteration, carry):
        @pl.when(iteration > 0)
        def _():
            tallput(h_ref, fine_mm(inv_ref[:, :NR], wide(h_ref)))
            c_ref[...] = wf[...] * h_ref[...]

        inv_ref[:, :NR] = apply()
        return carry

    lax.fori_loop(0, ITERS, step, 0)
    inverse = inv_ref[:, :NR]
    f2[0, :ROWS, :] = wf[...] * h_ref[...]
    moment = fine_nt(jnp.concatenate([f2[0, s * NR : (s + 1) * NR, :] for s in range(SLOTS)], axis=1), wide(h_ref))
    moment = jnp.dot(inverse, moment, precision=HI, preferred_element_type=F32)
    mixing = nt(moment, inverse, HI)
    mixing = 0.5 * (mixing + mixing.T)
    eye = sublanes((NR, NR)) == lanes((NR, NR))
    trace = jnp.sum(jnp.sum(jnp.where(eye, mixing, 0.0), axis=1, keepdims=True), axis=0, keepdims=True)
    root = factor(mixing, 1e-6 * trace + 1e-30)[0]
    combine = jnp.dot(root, inverse, precision=HI, preferred_element_type=F32)
    tallput(c_ref, fine_mm(combine, wide(c_ref)))
    coef = c_ref[...].astype(BF)
    full = mm(jnp.concatenate([coef, coef], axis=1), lct2[...])
    a1[0, :ROWS, :] = full[:, :KB]
    a1[1, :ROWS, :] = full[:, KB:]
    shifted = mm(coef, kq2)
    f2[0, :ROWS, :] = shifted[:, :KB]
    f2[1, :ROWS, :] = shifted[:, KB:]
    f2[:, ROWS:, :] = jnp.zeros((2, PAD * NR - ROWS, KB), F32)

    def finish(q, carry):
        pairs = [q * UNROLL_F + j for j in range(UNROLL_F)]
        xs = [pack(get(a1, 2 * p), get(a1, 2 * p + 1)) for p in pairs]
        cols = [[mm(revt[...], get(f2, 2 * p + e).astype(BF)) for e in range(2)] for p in pairs]
        ys = [mm(lc2[...], jnp.concatenate([x, x], axis=0).astype(BF)) for x in xs]
        ys = [jnp.concatenate([hat[0] * y[:KB] - hat[1] * y[KB:], hat[0] * y[KB:] + hat[1] * y[:KB]], axis=0).astype(BF) for y in ys]
        us = [mm(lbt[...], y) for y in ys]
        for p, x, u, col in zip(pairs, xs, us, cols):
            xr, xi = x[0:1], x[PAD : PAD + 1]
            cr, ci = (q1r * xr - q1i * xi) / KB, (q1r * xi + q1i * xr) / KB
            u = u - jnp.where(urow == 0, cr, 0.0) - jnp.where(urow == KB, ci, 0.0)
            pair = unpack(u, KB)
            for e in range(2):
                ub = pair[e].astype(BF)
                out_ref[2 * p + e] = (mm(ub, lb[...]) - col[e]).astype(BF)
        return carry

    lax.fori_loop(0, NR // 2 // UNROLL_F, finish, 0)


def synthesize(rank, tile_slit, sides, zernike, source_points, source_weight, start_block):
    ztab, inside = zernike_tables()
    wide = np.zeros((NZ, 96, KB), np.float32)
    wide[:, 8:89, 24:105] = ztab
    ins = np.zeros((96, KB), np.float32)
    ins[8:89, 24:105] = inside
    smem = pl.BlockSpec(memory_space=pltpu.SMEM)
    vmem = pl.BlockSpec(memory_space=pltpu.VMEM)
    tables = block_tables()
    tables = [jnp.asarray(tables[i]) for i in (0, 1, 2, 3, 4, 5, 8, 9)]
    big = (2, PAD * NR, KB)
    return pl.pallas_call(
        synth_kernel,
        out_shape=jax.ShapeDtypeStruct((NR, KB, 2 * KB), BF),
        in_specs=[smem] * 2 + [vmem] * (6 + len(tables)) + [pl.BlockSpec(memory_space=pl.ANY)] * 2,
        out_specs=vmem,
        compiler_params=pltpu.CompilerParams(vmem_limit_bytes=VMEM_CAP),
        scratch_shapes=[
            pltpu.VMEM((NR, KB), F32),
            pltpu.VMEM((3, KB, 2 * KB), F32),
            pltpu.VMEM(big, F32),
            pltpu.VMEM(big, F32),
            pltpu.VMEM((ROWS, KB), F32),
            pltpu.VMEM((ROWS, KB), F32),
            pltpu.VMEM((ROWS, KB), F32),
            pltpu.VMEM(big, F32),
            pltpu.VMEM((NZ, 96, KB), F32),
            pltpu.VMEM(start_block.shape, F32),
            pltpu.SemaphoreType.DMA((2,)),
        ],
    )(rank.reshape(1), *far(tile_slit), *sides, *far(zernike, source_points.T, source_weight.reshape(1, -1), jnp.asarray(ins), *tables, jnp.asarray(wide), start_block))


def tables_of(count, period):
    t = dft(np.arange(count), np.arange(KB) - KB // 2, 1, period)
    return t.real.astype(np.float32), t.imag.astype(np.float32)


def cast(x):
    return np.ascontiguousarray(x).astype(jnp.bfloat16)


def column_table():
    cc, cs = tables_of(PW, PW)
    out = np.zeros((5 * TS, 2 * KB), np.float32)
    out[2 * TS - HALO : 2 * TS - HALO + PW] = np.concatenate([cc, -cs], 1)
    return cast(out)


def row_table():
    rc, rs = tables_of(TS, TS)
    return np.concatenate([rc, rs], 1)


def image_tables():
    rc, rs = tables_of(TS, TS)
    cc, cs = tables_of(PW, PW)
    turn = np.concatenate([rc.T, rs.T], 1)
    inv_t = np.concatenate([cc, -cs], 1)[HALO : HALO + TS].T
    adj = np.concatenate([cc, cs], 1)[HALO : HALO + TS]
    rows = row_table()
    return (column_table(),) + tuple(cast(x) for x in (rows.T, rows, turn, inv_t, adj))


def tile_columns(ref, tile):
    return ref[pl.ds(pl.multiple_of(TS * (3 - tile), TS), 2 * TS), :]


def image_kernel(rank_ref, m0, m1, m2, m3, kern_ref, fwd, rows_t, rows, turn, inv_t, adj, o0, o1, o2, o3, patch, goal, fields, inten, gsum, spec):
    rank = rank_ref[0]
    quarter = m0.shape[0]
    left, outer = rank < 2, (rank == 0) | (rank == 3)
    block_of = lambda j: pl.ds(pl.multiple_of((rank ^ j) * quarter, quarter), quarter)
    low_end, high_end = neighbour_marks(m0.at[:, 4 * TS : 4 * TS + SIDE], m0.at[:, 4 * TS + SIDE :])
    present = jnp.where(rank == 0, low_end, jnp.where(rank == 3, high_end, 1.0)) > 0.5
    for j, m in enumerate((m0, m1, m2, m3)):
        side = jnp.where(left, m[:, 4 * TS : 4 * TS + SIDE], m[:, 4 * TS + SIDE :])
        own = jnp.where(left, m[:, 2 * TS : 3 * TS], m[:, 3 * TS : 4 * TS])
        patch[block_of(j), : 2 * TS] = m[:, : 2 * TS]
        patch[block_of(j), 2 * TS :] = side[:, TS:]
        goal[block_of(j), :] = jnp.where(outer, side[:, :TS], own).astype(F32)
    s = 1.0 / math.sqrt(TS * PW)
    start = jnp.where(rank < 2, PW - rank * TS, 3 * TS - (rank - 2) * TS)
    side_table = fwd[pl.ds(pl.multiple_of(start, HALO), PW), :]
    table = jnp.concatenate([tile_columns(fwd, rank), side_table], axis=0)
    columns = mm(patch[...], table).astype(BF)
    sums = mm(rows_t[...], columns)
    spec[0] = s * (sums[:KB, :KB] + sums[KB:, KB:])
    spec[1] = s * (sums[:KB, KB:] - sums[KB:, :KB])
    inten[...] = jnp.zeros((TS, TS), F32)
    gsum[...] = jnp.zeros((KB, 2 * KB), F32)

    def forward(q, carry):
        ks = [q * UNROLL_I + e for e in range(UNROLL_I)]
        sr, si = spec[0], spec[1]
        blocks = []
        for k in ks:
            kr, ki = kern_ref[k, :, :KB].astype(F32), kern_ref[k, :, KB:].astype(F32)
            wr, wi = kr * sr + ki * si, kr * si - ki * sr
            blocks.append(jnp.concatenate([jnp.concatenate([wr, wi], axis=1), jnp.concatenate([-wi, wr], axis=1)], axis=0).astype(BF))
        waves = [mm(rows[...], b).astype(BF) for b in blocks]
        total = inten[...]
        for k, w in zip(ks, waves):
            field = mm(w, inv_t[...])
            fields[k] = field
            total = total + field * field
        inten[...] = total
        return carry

    lax.fori_loop(0, NR // UNROLL_I, forward, 0)
    resist = 1.0 / (1.0 + jnp.exp(-STEEPNESS * (inten[...] - THRESHOLD)))
    inten[...] = 4.0 * (resist - goal[...]) * STEEPNESS * resist * (1.0 - resist)
    goal[...] = resist

    def backward(q, carry):
        ks = [q * UNROLL_I + e for e in range(UNROLL_I)]
        cols = [mm((fields[k] * inten[...]).astype(BF), adj[...]) for k in ks]
        blocks = [jnp.concatenate([c, jnp.concatenate([-c[:, KB:], c[:, :KB]], axis=1)], axis=0).astype(BF) for c in cols]
        turned = [mm(turn[...], b) for b in blocks]
        gr, gi = gsum[:, :KB], gsum[:, KB:]
        for k, y in zip(ks, turned):
            kr, ki = kern_ref[k, :, :KB].astype(F32), kern_ref[k, :, KB:].astype(F32)
            gr = gr + kr * y[:, :KB] + ki * y[:, KB:]
            gi = gi + ki * y[:, :KB] - kr * y[:, KB:]
        gsum[:, :KB] = gr
        gsum[:, KB:] = gi
        return carry

    lax.fori_loop(0, NR // UNROLL_I, backward, 0)
    grad = jnp.where(present, s * gsum[...], 0.0)
    block = jnp.concatenate([grad, jnp.concatenate([-grad[:, KB:], grad[:, :KB]], axis=1)], axis=0).astype(BF)
    inten[...] = mm(rows[...], block)
    for j, o in enumerate((o0, o1, o2, o3)):
        o[:quarter, :] = inten[block_of(j), :].astype(BF)
        o[quarter:, :] = goal[block_of(j), :].astype(BF)


def imaging(rank, packs, kern):
    quarter = packs[0].shape[0]
    smem = pl.BlockSpec(memory_space=pltpu.SMEM)
    vmem = pl.BlockSpec(memory_space=pltpu.VMEM)
    tables = [jnp.asarray(x) for x in image_tables()]
    return pl.pallas_call(
        image_kernel,
        out_shape=(jax.ShapeDtypeStruct((2 * quarter, TS), BF),) * 4,
        in_specs=[smem] + [vmem] * (5 + len(tables)),
        out_specs=(vmem,) * 4,
        compiler_params=pltpu.CompilerParams(vmem_limit_bytes=VMEM_CAP),
        scratch_shapes=[
            pltpu.VMEM((TS, 2 * TS + PW), BF),
            pltpu.VMEM((TS, TS), F32),
            pltpu.VMEM((NR, TS, TS), F32),
            pltpu.VMEM((TS, TS), F32),
            pltpu.VMEM((KB, 2 * KB), F32),
            pltpu.VMEM((2, KB, KB), F32),
        ],
    )(rank.reshape(1), *near(*packs, kern, *tables))


def back_kernel(rank_ref, n0, n1, n2, n3, fwd, resist_ref, grad_ref, held):
    rank = rank_ref[0]
    quarter, width = grad_ref.shape
    for j, n in enumerate((n0, n1, n2, n3)):
        held[rank ^ j] = n[...]
    resist_ref[:, :TS] = held[1, quarter:, :]
    resist_ref[:, TS:] = held[2, quarter:, :]
    parts = []
    for tile in range(4):
        parts.append(nt(held[tile, :quarter, :], fwd[TS * (3 - tile) : TS * (5 - tile), :]))
    grad_ref[...] = (parts[0] + parts[1] + parts[2] + parts[3]).astype(BF)


def back(rank, notes):
    quarter = notes[0].shape[0] // 2
    smem = pl.BlockSpec(memory_space=pltpu.SMEM)
    vmem = pl.BlockSpec(memory_space=pltpu.VMEM)
    whole = jax.ShapeDtypeStruct((quarter, 2 * TS), BF)
    return pl.pallas_call(
        back_kernel,
        out_shape=(whole, whole),
        in_specs=[smem] + [vmem] * 5,
        out_specs=(vmem, vmem),
        compiler_params=pltpu.CompilerParams(vmem_limit_bytes=VMEM_CAP),
        scratch_shapes=[pltpu.VMEM((4, 2 * quarter, TS), BF)],
    )(rank.reshape(1), *near(*notes, jnp.asarray(column_table())))


def prep_kernel(slit_ref, mask, goal, right_ref, left_ref):
    quarter = mask.shape[0]
    lane = lanes((quarter, PW))
    right_ref[:, :TS] = goal[:, TS:]
    left_ref[:, :TS] = goal[:, :TS]
    first, second = (slit_ref[0] + 1).astype(F32), (slit_ref[1] + 1).astype(F32)
    right_ref[:, TS:] = jnp.where(lane < HALO, second, mask[:, 2 * TS - PW :].astype(F32)).astype(BF)
    left_ref[:, TS:] = jnp.where(lane >= PW - HALO, first, mask[:, :PW].astype(F32)).astype(BF)


def messages(tile_slit, mask, target):
    smem = pl.BlockSpec(memory_space=pltpu.SMEM)
    vmem = pl.BlockSpec(memory_space=pltpu.VMEM)
    return pl.pallas_call(
        prep_kernel,
        out_shape=(jax.ShapeDtypeStruct((mask.shape[0], SIDE), BF),) * 2,
        compiler_params=pltpu.CompilerParams(vmem_limit_bytes=VMEM_CAP),
        in_specs=[smem, vmem, vmem],
        out_specs=(vmem, vmem),
    )(*far(tile_slit, mask, target))


def swap(x, m, size):
    return lax.ppermute(x, "src", [(i, i ^ m) for i in range(size)])


def shift(x, step, count):
    pairs = [(i, i + step) for i in range(count) if 0 <= i + step < count]
    return lax.ppermute(x, "tile", pairs)


def on_device(mask, target, start_block, zernike, source_points, source_weight, tile_slit):
    groups = lax.axis_size("tile")
    size = lax.axis_size("src")
    rank = lax.axis_index("src").astype(jnp.int32)
    rightward, leftward = messages(tile_slit, mask, target)
    from_left = shift(rightward, 1, groups)
    from_right = shift(leftward, -1, groups)
    pack = jnp.concatenate([mask, target, from_left, from_right], axis=1)
    packs = [pack] + [swap(pack, m, size) for m in (1, 2, 3)]
    kern = synthesize(rank, tile_slit, (from_left, from_right), zernike, source_points, source_weight, start_block)
    notes = imaging(rank, packs, kern)
    return tuple(back(rank, [notes[0]] + [swap(notes[m], m, size) for m in (1, 2, 3)]))


def solution(mesh):
    placed = (P("src", "tile"), P("src", "tile"), P(), P(), P(), P(), P("tile"))
    return jax.shard_map(
        on_device,
        mesh=mesh,
        in_specs=placed,
        out_specs=(P("src", "tile"), P("src", "tile")),
        check_vma=False,
    )
```

```python
import math

import jax
import jax.numpy as jnp
import numpy as np
from jax import lax
from jax.experimental import pallas as pl
from jax.experimental.pallas import tpu as pltpu
from jax.sharding import PartitionSpec as P

KB = 128
NR = 24
NZ = 37
RAD = 40
SHIFT = 24
HALO = 64
ITERS = 4
TS = 256
PW = TS + 2 * HALO
GRID = 2 * SHIFT + 1
PUP = 2 * RAD + 1

STEEPNESS = 4.0
THRESHOLD = 0.5
RIDGE_SHARE = 0.001
BF = jnp.bfloat16
F32 = jnp.float32


def noll_terms(term_count):
    listing = []
    degree = 0
    while len(listing) < term_count:
        for azimuth in range(degree % 2, degree + 1, 2):
            if azimuth == 0:
                listing.append((degree, 0, 0))
            else:
                for repeat in range(2):
                    number = len(listing) + 1
                    listing.append((degree, azimuth, 2 if number % 2 == 0 else 1))
        degree += 1
    return listing[:term_count]


def radial_terms(degree, azimuth):
    powers = []
    for counter in range((degree - azimuth) // 2 + 1):
        factor = (
            (-1) ** counter
            * math.factorial(degree - counter)
            / (
                math.factorial(counter)
                * math.factorial((degree + azimuth) // 2 - counter)
                * math.factorial((degree - azimuth) // 2 - counter)
            )
        )
        powers.append((degree - 2 * counter, factor))
    return powers


def dft(rows, cols, sign, period=KB):
    return np.exp(sign * 2j * np.pi * np.mod(np.outer(rows, cols), period) / period)


def cmul(a, b):
    return (a[0] * b[0] - a[1] * b[1], a[0] * b[1] + a[1] * b[0])


SLOTS = 50
VMEM_CAP = 32 << 20
SIDE = TS + PW
ROWS = SLOTS * NR
PAD = 64
HI = lax.Precision.HIGHEST
UNROLL = 6
UNROLL_S = 4
UNROLL_F = 4
UNROLL_I = 8


ORDER = 9


def times(a, b):
    out = np.zeros((ORDER, ORDER), np.complex128)
    for i, j in zip(*np.nonzero(a)):
        for k, l in zip(*np.nonzero(b)):
            out[i + k, j + l] += a[i, j] * b[k, l]
    return out


def zernike_polynomials():
    one, step, square = (np.zeros((ORDER, ORDER), np.complex128) for _ in range(3))
    one[0, 0] = 1.0
    step[1, 0], step[0, 1] = 1.0, 1j
    square[2, 0] = square[0, 2] = 1.0
    lane = (np.arange(KB) - KB // 2) / RAD
    powers = lane[None, :] ** np.arange(ORDER)[:, None]
    out = np.zeros((NZ, 16, KB), np.float32)
    for number, (degree, azimuth, parity) in enumerate(noll_terms(NZ)):
        total = np.zeros((ORDER, ORDER))
        for power, scale in radial_terms(degree, azimuth):
            term = one
            for _ in range(azimuth):
                term = times(term, step)
            for _ in range((power - azimuth) // 2):
                term = times(term, square)
            total = total + scale * (term.real if azimuth == 0 or parity == 2 else term.imag)
        total = total * math.sqrt((1.0 if azimuth == 0 else 2.0) * (degree + 1.0))
        out[number, :ORDER] = total @ powers
    return out


def real_form(table):
    return np.block([[table.real, -table.imag], [table.imag, table.real]])


def split(table):
    high = table.astype(np.float32).astype(jnp.bfloat16)
    low = (table - high.astype(np.float64)).astype(jnp.bfloat16)
    return high, low


def block_tables():
    freq = np.arange(KB)
    big = real_form(dft(freq, np.arange(KB) - KB // 2, -1))
    offs = np.zeros((KB, PAD), np.complex128)
    offs[:, :GRID] = dft(freq, np.arange(GRID) - SHIFT, 1)
    small = real_form(offs)
    rev = np.zeros((PAD, KB), np.float32)
    for spot in range(GRID):
        rev[spot, KB // 2 + SHIFT - spot] = 1.0
    lb, lb_lo = split(big)
    lbt, lbt_lo = split(big.T.copy())
    lc, lc_lo = split(small)
    lct, lct_lo = split(small.T.copy())
    wide = lambda a, b: np.concatenate([a, b], axis=1)
    tall = lambda a, b: np.concatenate([a, b], axis=0)
    return (lb, lbt, lc, lct, tall(lct, lct_lo), wide(lc, lc_lo), lbt_lo, lb_lo, rev.astype(jnp.bfloat16), rev.T.copy().astype(jnp.bfloat16))


def near(*arrays):
    return tuple(pltpu.with_memory_space_constraint(x, pltpu.VMEM) for x in arrays)


def far(*arrays):
    return tuple(pltpu.with_memory_space_constraint(x, pltpu.HBM) for x in arrays)


def mm(a, b):
    return jnp.dot(a, b, preferred_element_type=F32)


def nt(a, b, precision=None):
    return lax.dot_general(a, b, (((1,), (1,)), ((), ())), precision=precision, preferred_element_type=F32)


def lanes(shape):
    return lax.broadcasted_iota(jnp.int32, shape, 1)


def sublanes(shape):
    return lax.broadcasted_iota(jnp.int32, shape, 0)


def halves(x):
    high = x.astype(BF)
    return high, (x - high.astype(F32)).astype(BF)


def stack_halves(x):
    return jnp.concatenate([part.astype(F32) for part in halves(x)], axis=0).astype(BF)


def fine_nt(a, b):
    full = nt(stack_halves(a), stack_halves(b))
    return full[:NR, :NR] + full[:NR, NR:] + full[NR:, :NR]


def fine_mm(a, b):
    ah, al = (x.astype(F32) for x in halves(a))
    bh, bl = (x.astype(F32) for x in halves(b))
    return mm(jnp.concatenate([ah, al, ah], axis=1).astype(BF), jnp.concatenate([bh, bh, bl], axis=0).astype(BF))


def factor(gram, floor):
    tile, blocks = 8, NR // 8
    rows = [slice(b * tile, (b + 1) * tile) for b in range(blocks)]
    wide_eye = (sublanes((NR, PAD)) == lanes((NR, PAD))).astype(F32)
    start = jnp.concatenate([gram, jnp.zeros((NR, PAD - NR), F32), wide_eye], axis=1)
    work = [start[x] for x in rows]
    col = [[jnp.broadcast_to(gram[x, j : j + 1], (tile, KB)) for x in rows] for j in range(NR)]
    row_no = sublanes((tile, KB))
    diag = [jnp.zeros((tile, KB), F32) for _ in rows]
    for k in range(NR):
        b0, r0 = divmod(k, tile)
        pick = lambda x: jnp.broadcast_to(x[r0 : r0 + 1, :], (tile, KB))
        pivot = jnp.maximum(pick(col[k][b0]), floor)
        diag[b0] = jnp.where(row_no == r0, pivot, diag[b0])
        inv = 1.0 / pivot
        ratio = [c * inv for c in col[k]]
        lead = pick(work[b0])
        for j in range(k + 1, NR):
            entry = pick(col[j][b0])
            for b in range(b0, blocks):
                col[j][b] = col[j][b] - ratio[b] * entry
        for b in range(b0, blocks):
            part = ratio[b] if b > b0 else jnp.where(row_no > r0, ratio[b], 0.0)
            work[b] = work[b] - part * lead
    done = jnp.concatenate([w * lax.rsqrt(d) for w, d in zip(work, diag)], axis=0)
    return done[:, :NR], done[:, PAD : PAD + NR]


def neighbour_marks(left_ref, right_ref):
    low = left_ref[0:16, TS : TS + KB].astype(F32)[0:1, 0:1]
    high = right_ref[0:16, SIDE - KB : SIDE].astype(F32)[0:1, KB - 1 : KB]
    return low, high


def synth_kernel(rank_ref, slit_ref, left_ref, right_ref, zern_ref, sp_ref, sw_ref, zt_ref, lb, lbt, lc, lct, lct2, lc2, rev, revt, b0_far, out_ref, inv_ref, hat, a1, f2, c_ref, h_ref, wf, bx, b0_ref, sem):
    b0_copy = pltpu.make_async_copy(b0_far, b0_ref, sem)
    b0_copy.start()
    weights = sw_ref[...]
    weights = weights / (math.pi * RAD * RAD * jnp.sum(weights, axis=1, keepdims=True))
    count = sp_ref.shape[1]
    offset = sublanes((KB, count))
    hot_x = jnp.where(offset - SHIFT == sp_ref[0:1, :], weights, 0.0)
    hot_y = (jnp.where(offset >= PAD, offset - PAD, offset) - SHIFT == sp_ref[1:2, :]).astype(F32).astype(BF)
    high, low = halves(hot_x)
    wmap = nt(high, hot_y) + nt(low, hot_y)
    for s in range(SLOTS):
        wf[s * NR : (s + 1) * NR, :] = jnp.broadcast_to(wmap[s : s + 1, :], (NR, KB))

    rank = rank_ref[0]
    low_end, high_end = neighbour_marks(left_ref, right_ref)
    slit = slit_ref[jnp.clip(rank - 1, 0, 1)].astype(F32)
    slit = jnp.where(rank == 0, low_end - 1.0, jnp.where(rank == 3, high_end - 1.0, slit))
    chosen = sublanes((zern_ref.shape[0], 1)).astype(F32) == jnp.maximum(slit, 0.0)
    coefs = jnp.sum(jnp.where(chosen, zern_ref[...], 0.0), axis=0, keepdims=True)
    by_row = jnp.zeros((16, KB), F32)
    for z in range(NZ):
        by_row = by_row + coefs[:, z : z + 1] * zt_ref[z]
    row_at, col_at = sublanes((96, KB)) - 48, lanes((96, KB)) - KB // 2
    scaled = row_at.astype(F32) / RAD
    turns = jnp.zeros((96, KB), F32)
    for power in range(ORDER - 1, -1, -1):
        turns = turns * scaled + by_row[power : power + 1, :]
    inside = (row_at * row_at + col_at * col_at <= RAD * RAD).astype(F32)
    turns = turns - jnp.floor(turns + 0.5)
    half = math.pi * turns
    sq = half * half
    sine = jnp.full_like(half, 1.0 / math.factorial(15))
    for n in (13, 11, 9, 7, 5, 3, 1):
        sine = 1.0 / math.factorial(n) - sine * sq
    sine = sine * half
    cosine = jnp.full_like(half, 1.0 / math.factorial(14))
    for n in (12, 10, 8, 6, 4, 2, 0):
        cosine = 1.0 / math.factorial(n) - cosine * sq
    pr = inside * (1.0 - 2.0 * sine * sine)
    pi = inside * (2.0 * sine * cosine)
    spot = lambda a, i, j: a[i : i + 1, j : j + 1]
    q1r, q1i = spot(pr, 88, 64), spot(pi, 88, 64)
    m1r, m1i = spot(pr, 8, 64), spot(pi, 8, 64)
    q2r, q2i = spot(pr, 48, 104), spot(pi, 48, 104)
    m2r, m2i = spot(pr, 48, 24), spot(pi, 48, 24)
    z1r, z1i = q1r * m1r + q1i * m1i, q1r * m1i - q1i * m1r
    z2r, z2i = q2r * m2r + q2i * m2i, q2r * m2i - q2i * m2r
    edge = jnp.zeros((16, 2 * KB), F32)
    both = jnp.concatenate([edge, jnp.concatenate([pr, pi], axis=1), edge], axis=0).astype(BF)
    ph = mm(both, lbt[...])
    stacked = jnp.concatenate([ph[:, :KB], ph[:, KB:]], axis=0).astype(BF)
    ph = mm(lb[...], stacked)
    hr, hi = ph[:KB], ph[KB:]
    hat[0] = jnp.concatenate([hr, hr], axis=1) / (KB * KB)
    hat[1] = jnp.concatenate([hi, hi], axis=1) / (KB * KB)
    power = (hr * hr + hi * hi) / (KB * KB)
    power = jnp.concatenate([power, power], axis=1)
    hat[2] = power

    rs, cs = sublanes((KB, KB)), lanes((KB, KB))
    at = lambda i, j, v: jnp.where((rs == i) & (cs == j), v, 0.0)
    one = jnp.ones((1, 1), F32)
    top = 2 * SHIFT
    ky = (
        at(0, 0, one) + at(PAD, PAD, one)
        + at(top, 0, z2r) + at(PAD + top, 0, -z2i) + at(top, PAD, z2i) + at(PAD + top, PAD, z2r)
        + at(0, top, z2r) + at(PAD, top, z2i) + at(0, PAD + top, -z2i) + at(PAD, PAD + top, z2r)
    ).astype(BF)
    none = jnp.zeros((KB, KB), BF)
    ky = jnp.concatenate([jnp.concatenate([ky, none], axis=1), jnp.concatenate([none, ky], axis=1)], axis=0)
    kq0 = jnp.concatenate([at(0, 0, q2r) + at(0, PAD, -q2i), at(0, 0, q2i) + at(0, PAD, q2r)], axis=0).astype(BF)
    kq2 = jnp.concatenate([at(0, 0, q2r) + at(PAD, 0, -q2i), at(0, 0, q2i) + at(PAD, 0, q2r)], axis=1).astype(BF)

    a1[:, ROWS:, :] = jnp.zeros((2, PAD * NR - ROWS, KB), F32)

    def pack(x0, x1):
        return jnp.concatenate(
            [jnp.concatenate([x0[:, :KB], x1[:, :KB]], axis=1), jnp.concatenate([x0[:, KB:], x1[:, KB:]], axis=1)], axis=0
        )

    def unpack(y, height):
        return (
            jnp.concatenate([y[:height, :KB], y[height:, :KB]], axis=1),
            jnp.concatenate([y[:height, KB:], y[height:, KB:]], axis=1),
        )

    def put(ref, k, x):
        ref[0, pl.ds(k, PAD, stride=NR), :] = x[:, :KB]
        ref[1, pl.ds(k, PAD, stride=NR), :] = x[:, KB:]

    def get(ref, k):
        return jnp.concatenate([ref[0, pl.ds(k, PAD, stride=NR), :], ref[1, pl.ds(k, PAD, stride=NR), :]], axis=1)

    def both_halves(ref):
        return jnp.concatenate([ref[0, :ROWS, :], ref[1, :ROWS, :]], axis=1).astype(BF)

    prow = sublanes((KB, 2 * KB))
    urow = sublanes((2 * KB, 2 * KB))

    def start(q, carry):
        pairs = [q * UNROLL_S + j for j in range(UNROLL_S)]
        blocks = [[jnp.concatenate([b0_ref[0, 2 * p + e], b0_ref[1, 2 * p + e]], axis=1).astype(BF) for e in range(2)] for p in pairs]
        xs = [pack(mm(b[0], lbt[...]), mm(b[1], lbt[...])) for b in blocks]
        revs = [[mm(rev[...], e) for e in b] for b in blocks]
        ys = [mm(lb[...], x.astype(BF)) for x in xs]
        ys = [jnp.concatenate([hat[0] * y[:KB] + hat[1] * y[KB:], hat[0] * y[KB:] - hat[1] * y[:KB]], axis=0).astype(BF) for y in ys]
        ds = [mm(lct[...], y) for y in ys]
        for p, x, d, rv in zip(pairs, xs, ds, revs):
            xr, xi = x[0:1], x[KB : KB + 1]
            cr, ci = (q1r * xr + q1i * xi) / KB, (q1r * xi - q1i * xr) / KB
            d = d - jnp.where(prow == 0, cr, 0.0) - jnp.where(prow == PAD, ci, 0.0)
            d0, d1 = unpack(d, PAD)
            put(f2, 2 * p, d0)
            put(f2, 2 * p + 1, d1)
            put(bx, 2 * p, rv[0])
            put(bx, 2 * p + 1, rv[1])
        return carry

    b0_copy.wait()
    lax.fori_loop(0, NR // 2 // UNROLL_S, start, 0)
    first = mm(both_halves(f2), lc[...]) - mm(both_halves(bx), kq0)
    c_ref[...] = wf[...] * first

    def wide(ref):
        return jnp.concatenate([ref[s * NR : (s + 1) * NR, :] for s in range(SLOTS)], axis=1)

    def tallput(ref, x):
        for s in range(SLOTS):
            ref[s * NR : (s + 1) * NR, :] = x[:, s * KB : (s + 1) * KB]

    def forward(p):
        return pack(get(a1, 2 * p), get(a1, 2 * p + 1)).astype(BF)

    def middle(q, carry):
        pairs = [q * UNROLL + j for j in range(UNROLL)]
        ys = [mm(lc[...], forward(p)) for p in pairs]
        ys = [jnp.concatenate([hat[2] * y[:KB], hat[2] * y[KB:]], axis=0).astype(BF) for y in ys]
        ds = [mm(lct[...], y) for y in ys]
        for p, d in zip(pairs, ds):
            d0, d1 = unpack(d, PAD)
            put(f2, 2 * p, d0)
            put(f2, 2 * p + 1, d1)
        return carry

    def apply():
        coef = c_ref[...].astype(BF)
        full = mm(coef, lct[...])
        a1[0, :ROWS, :] = full[:, :KB]
        a1[1, :ROWS, :] = full[:, KB:]
        lax.fori_loop(0, NR // 2 // UNROLL, middle, 0)
        last = slice(top * NR, (top + 1) * NR)
        lr, li, ur, ui = a1[0, 0:NR, :], a1[1, 0:NR, :], a1[0, last, :], a1[1, last, :]
        f2[0, 0:NR, :] = f2[0, 0:NR, :] - (lr + z1r * ur - z1i * ui) / KB
        f2[1, 0:NR, :] = f2[1, 0:NR, :] - (li + z1r * ui + z1i * ur) / KB
        f2[0, last, :] = f2[0, last, :] - (z1r * lr + z1i * li) / KB
        f2[1, last, :] = f2[1, last, :] - (z1r * li - z1i * lr) / KB
        corr = mm(jnp.concatenate([c_ref[: ROWS // 2, :], c_ref[ROWS // 2 :, :]], axis=1).astype(BF), ky)
        h_ref[...] = mm(both_halves(f2), lc[...]) - jnp.concatenate([corr[:, :KB], corr[:, KB:]], axis=0)
        gram = fine_nt(wide(c_ref), wide(h_ref))
        gram = 0.5 * (gram + gram.T)
        eye = sublanes((NR, NR)) == lanes((NR, NR))
        trace = jnp.sum(jnp.sum(jnp.where(eye, gram, 0.0), axis=1, keepdims=True), axis=0, keepdims=True)
        return factor(gram + jnp.where(eye, RIDGE_SHARE * trace / NR + 1e-06, 0.0), 0.0)[1]

    def step(iteration, carry):
        @pl.when(iteration > 0)
        def _():
            tallput(h_ref, fine_mm(inv_ref[:, :NR], wide(h_ref)))
            c_ref[...] = wf[...] * h_ref[...]

        inv_ref[:, :NR] = apply()
        return carry

    lax.fori_loop(0, ITERS, step, 0)
    inverse = inv_ref[:, :NR]
    f2[0, :ROWS, :] = wf[...] * h_ref[...]
    moment = fine_nt(jnp.concatenate([f2[0, s * NR : (s + 1) * NR, :] for s in range(SLOTS)], axis=1), wide(h_ref))
    moment = jnp.dot(inverse, moment, precision=HI, preferred_element_type=F32)
    mixing = nt(moment, inverse, HI)
    mixing = 0.5 * (mixing + mixing.T)
    eye = sublanes((NR, NR)) == lanes((NR, NR))
    trace = jnp.sum(jnp.sum(jnp.where(eye, mixing, 0.0), axis=1, keepdims=True), axis=0, keepdims=True)
    root = factor(mixing, 1e-6 * trace + 1e-30)[0]
    combine = jnp.dot(root, inverse, precision=HI, preferred_element_type=F32)
    tallput(c_ref, fine_mm(combine, wide(c_ref)))
    coef = c_ref[...].astype(BF)
    full = mm(jnp.concatenate([coef, coef], axis=1), lct2[...])
    a1[0, :ROWS, :] = full[:, :KB]
    a1[1, :ROWS, :] = full[:, KB:]
    shifted = mm(coef, kq2)
    f2[0, :ROWS, :] = shifted[:, :KB]
    f2[1, :ROWS, :] = shifted[:, KB:]
    f2[:, ROWS:, :] = jnp.zeros((2, PAD * NR - ROWS, KB), F32)

    def finish(q, carry):
        pairs = [q * UNROLL_F + j for j in range(UNROLL_F)]
        xs = [pack(get(a1, 2 * p), get(a1, 2 * p + 1)) for p in pairs]
        cols = [[mm(revt[...], get(f2, 2 * p + e).astype(BF)) for e in range(2)] for p in pairs]
        ys = [mm(lc2[...], jnp.concatenate([x, x], axis=0).astype(BF)) for x in xs]
        ys = [jnp.concatenate([hat[0] * y[:KB] - hat[1] * y[KB:], hat[0] * y[KB:] + hat[1] * y[:KB]], axis=0).astype(BF) for y in ys]
        us = [mm(lbt[...], y) for y in ys]
        for p, x, u, col in zip(pairs, xs, us, cols):
            xr, xi = x[0:1], x[PAD : PAD + 1]
            cr, ci = (q1r * xr - q1i * xi) / KB, (q1r * xi + q1i * xr) / KB
            u = u - jnp.where(urow == 0, cr, 0.0) - jnp.where(urow == KB, ci, 0.0)
            pair = unpack(u, KB)
            for e in range(2):
                ub = pair[e].astype(BF)
                out_ref[2 * p + e] = (mm(ub, lb[...]) - col[e]).astype(BF)
        return carry

    lax.fori_loop(0, NR // 2 // UNROLL_F, finish, 0)


def synthesize(rank, tile_slit, sides, zernike, source_points, source_weight, start_block):
    smem = pl.BlockSpec(memory_space=pltpu.SMEM)
    vmem = pl.BlockSpec(memory_space=pltpu.VMEM)
    tables = block_tables()
    tables = [jnp.asarray(tables[i]) for i in (0, 1, 2, 3, 4, 5, 8, 9)]
    big = (2, PAD * NR, KB)
    return pl.pallas_call(
        synth_kernel,
        out_shape=jax.ShapeDtypeStruct((NR, KB, 2 * KB), BF),
        in_specs=[smem] * 2 + [vmem] * (6 + len(tables)) + [pl.BlockSpec(memory_space=pl.ANY)],
        out_specs=vmem,
        compiler_params=pltpu.CompilerParams(vmem_limit_bytes=VMEM_CAP),
        scratch_shapes=[
            pltpu.VMEM((NR, KB), F32),
            pltpu.VMEM((3, KB, 2 * KB), F32),
            pltpu.VMEM(big, F32),
            pltpu.VMEM(big, F32),
            pltpu.VMEM((ROWS, KB), F32),
            pltpu.VMEM((ROWS, KB), F32),
            pltpu.VMEM((ROWS, KB), F32),
            pltpu.VMEM(big, F32),
            pltpu.VMEM(start_block.shape, F32),
            pltpu.SemaphoreType.DMA,
        ],
    )(rank.reshape(1), *far(tile_slit), *sides, *far(zernike, source_points.T, source_weight.reshape(1, -1), jnp.asarray(zernike_polynomials()), *tables, start_block))


def tables_of(count, period):
    t = dft(np.arange(count), np.arange(KB) - KB // 2, 1, period)
    return t.real.astype(np.float32), t.imag.astype(np.float32)


def cast(x):
    return np.ascontiguousarray(x).astype(jnp.bfloat16)


def column_table():
    cc, cs = tables_of(PW, PW)
    out = np.zeros((5 * TS, 2 * KB), np.float32)
    out[2 * TS - HALO : 2 * TS - HALO + PW] = np.concatenate([cc, -cs], 1)
    return cast(out)


def row_table():
    rc, rs = tables_of(TS, TS)
    return np.concatenate([rc, rs], 1)


def image_tables():
    rc, rs = tables_of(TS, TS)
    cc, cs = tables_of(PW, PW)
    turn = np.concatenate([rc.T, rs.T], 1)
    inv_t = np.concatenate([cc, -cs], 1)[HALO : HALO + TS].T
    adj = np.concatenate([cc, cs], 1)[HALO : HALO + TS]
    rows = row_table()
    return (column_table(),) + tuple(cast(x) for x in (rows.T, rows, turn, inv_t, adj))


def tile_columns(ref, tile):
    return ref[pl.ds(pl.multiple_of(TS * (3 - tile), TS), 2 * TS), :]


def image_kernel(rank_ref, m0, m1, m2, m3, kern_ref, fwd, rows_t, rows, turn, inv_t, adj, o0, o1, o2, o3, patch, goal, fields, inten, gsum, spec):
    rank = rank_ref[0]
    quarter = m0.shape[0]
    left, outer = rank < 2, (rank == 0) | (rank == 3)
    block_of = lambda j: pl.ds(pl.multiple_of((rank ^ j) * quarter, quarter), quarter)
    low_end, high_end = neighbour_marks(m0.at[:, 4 * TS : 4 * TS + SIDE], m0.at[:, 4 * TS + SIDE :])
    present = jnp.where(rank == 0, low_end, jnp.where(rank == 3, high_end, 1.0)) > 0.5
    for j, m in enumerate((m0, m1, m2, m3)):
        side = jnp.where(left, m[:, 4 * TS : 4 * TS + SIDE], m[:, 4 * TS + SIDE :])
        own = jnp.where(left, m[:, 2 * TS : 3 * TS], m[:, 3 * TS : 4 * TS])
        patch[block_of(j), : 2 * TS] = m[:, : 2 * TS]
        patch[block_of(j), 2 * TS :] = side[:, TS:]
        goal[block_of(j), :] = jnp.where(outer, side[:, :TS], own).astype(F32)
    s = 1.0 / math.sqrt(TS * PW)
    start = jnp.where(rank < 2, PW - rank * TS, 3 * TS - (rank - 2) * TS)
    side_table = fwd[pl.ds(pl.multiple_of(start, HALO), PW), :]
    table = jnp.concatenate([tile_columns(fwd, rank), side_table], axis=0)
    columns = mm(patch[...], table).astype(BF)
    sums = mm(rows_t[...], columns)
    spec[0] = s * (sums[:KB, :KB] + sums[KB:, KB:])
    spec[1] = s * (sums[:KB, KB:] - sums[KB:, :KB])
    inten[...] = jnp.zeros((TS, TS), F32)
    gsum[...] = jnp.zeros((KB, 2 * KB), F32)

    def forward(q, carry):
        ks = [q * UNROLL_I + e for e in range(UNROLL_I)]
        sr, si = spec[0], spec[1]
        blocks = []
        for k in ks:
            kr, ki = kern_ref[k, :, :KB].astype(F32), kern_ref[k, :, KB:].astype(F32)
            wr, wi = kr * sr + ki * si, kr * si - ki * sr
            blocks.append(jnp.concatenate([jnp.concatenate([wr, wi], axis=1), jnp.concatenate([-wi, wr], axis=1)], axis=0).astype(BF))
        waves = [mm(rows[...], b).astype(BF) for b in blocks]
        total = inten[...]
        for k, w in zip(ks, waves):
            field = mm(w, inv_t[...])
            fields[k] = field
            total = total + field * field
        inten[...] = total
        return carry

    lax.fori_loop(0, NR // UNROLL_I, forward, 0)
    resist = 1.0 / (1.0 + jnp.exp(-STEEPNESS * (inten[...] - THRESHOLD)))
    inten[...] = 4.0 * (resist - goal[...]) * STEEPNESS * resist * (1.0 - resist)
    goal[...] = resist

    def backward(q, carry):
        ks = [q * UNROLL_I + e for e in range(UNROLL_I)]
        cols = [mm((fields[k] * inten[...]).astype(BF), adj[...]) for k in ks]
        blocks = [jnp.concatenate([c, jnp.concatenate([-c[:, KB:], c[:, :KB]], axis=1)], axis=0).astype(BF) for c in cols]
        turned = [mm(turn[...], b) for b in blocks]
        gr, gi = gsum[:, :KB], gsum[:, KB:]
        for k, y in zip(ks, turned):
            kr, ki = kern_ref[k, :, :KB].astype(F32), kern_ref[k, :, KB:].astype(F32)
            gr = gr + kr * y[:, :KB] + ki * y[:, KB:]
            gi = gi + ki * y[:, :KB] - kr * y[:, KB:]
        gsum[:, :KB] = gr
        gsum[:, KB:] = gi
        return carry

    lax.fori_loop(0, NR // UNROLL_I, backward, 0)
    grad = jnp.where(present, s * gsum[...], 0.0)
    block = jnp.concatenate([grad, jnp.concatenate([-grad[:, KB:], grad[:, :KB]], axis=1)], axis=0).astype(BF)
    inten[...] = mm(rows[...], block)
    for j, o in enumerate((o0, o1, o2, o3)):
        o[:quarter, :] = inten[block_of(j), :].astype(BF)
        o[quarter:, :] = goal[block_of(j), :].astype(BF)


def imaging(rank, packs, kern):
    quarter = packs[0].shape[0]
    smem = pl.BlockSpec(memory_space=pltpu.SMEM)
    vmem = pl.BlockSpec(memory_space=pltpu.VMEM)
    tables = [jnp.asarray(x) for x in image_tables()]
    return pl.pallas_call(
        image_kernel,
        out_shape=(jax.ShapeDtypeStruct((2 * quarter, TS), BF),) * 4,
        in_specs=[smem] + [vmem] * (5 + len(tables)),
        out_specs=(vmem,) * 4,
        compiler_params=pltpu.CompilerParams(vmem_limit_bytes=VMEM_CAP),
        scratch_shapes=[
            pltpu.VMEM((TS, 2 * TS + PW), BF),
            pltpu.VMEM((TS, TS), F32),
            pltpu.VMEM((NR, TS, TS), F32),
            pltpu.VMEM((TS, TS), F32),
            pltpu.VMEM((KB, 2 * KB), F32),
            pltpu.VMEM((2, KB, KB), F32),
        ],
    )(rank.reshape(1), *near(*packs, kern, *tables))


def back_kernel(rank_ref, n0, n1, n2, n3, fwd, resist_ref, grad_ref, held):
    rank = rank_ref[0]
    quarter, width = grad_ref.shape
    for j, n in enumerate((n0, n1, n2, n3)):
        held[rank ^ j] = n[...]
    resist_ref[:, :TS] = held[1, quarter:, :]
    resist_ref[:, TS:] = held[2, quarter:, :]
    parts = []
    for tile in range(4):
        parts.append(nt(held[tile, :quarter, :], fwd[TS * (3 - tile) : TS * (5 - tile), :]))
    grad_ref[...] = (parts[0] + parts[1] + parts[2] + parts[3]).astype(BF)


def back(rank, notes):
    quarter = notes[0].shape[0] // 2
    smem = pl.BlockSpec(memory_space=pltpu.SMEM)
    vmem = pl.BlockSpec(memory_space=pltpu.VMEM)
    whole = jax.ShapeDtypeStruct((quarter, 2 * TS), BF)
    return pl.pallas_call(
        back_kernel,
        out_shape=(whole, whole),
        in_specs=[smem] + [vmem] * 5,
        out_specs=(vmem, vmem),
        compiler_params=pltpu.CompilerParams(vmem_limit_bytes=VMEM_CAP),
        scratch_shapes=[pltpu.VMEM((4, 2 * quarter, TS), BF)],
    )(rank.reshape(1), *near(*notes, jnp.asarray(column_table())))


def prep_kernel(slit_ref, mask, goal, right_ref, left_ref, pack_ref):
    quarter = mask.shape[0]
    lane = lanes((quarter, PW))
    pack_ref[:, : 2 * TS] = mask[...]
    pack_ref[:, 2 * TS : 4 * TS] = goal[...]
    right_ref[:, :TS] = goal[:, TS:]
    left_ref[:, :TS] = goal[:, :TS]
    first, second = (slit_ref[0] + 1).astype(F32), (slit_ref[1] + 1).astype(F32)
    right_ref[:, TS:] = jnp.where(lane < HALO, second, mask[:, 2 * TS - PW :].astype(F32)).astype(BF)
    left_ref[:, TS:] = jnp.where(lane >= PW - HALO, first, mask[:, :PW].astype(F32)).astype(BF)


def messages(tile_slit, mask, target):
    smem = pl.BlockSpec(memory_space=pltpu.SMEM)
    vmem = pl.BlockSpec(memory_space=pltpu.VMEM)
    return pl.pallas_call(
        prep_kernel,
        out_shape=tuple(jax.ShapeDtypeStruct((mask.shape[0], w), BF) for w in (SIDE, SIDE, 4 * TS + 2 * SIDE)),
        compiler_params=pltpu.CompilerParams(vmem_limit_bytes=VMEM_CAP),
        in_specs=[smem, vmem, vmem],
        out_specs=(vmem, vmem, vmem),
    )(*far(tile_slit, mask, target))


def swap(x, m, size):
    return lax.ppermute(x, "src", [(i, i ^ m) for i in range(size)])


def shift(x, step, count):
    pairs = [(i, i + step) for i in range(count) if 0 <= i + step < count]
    return lax.ppermute(x, "tile", pairs)


def on_device(mask, target, start_block, zernike, source_points, source_weight, tile_slit):
    groups = lax.axis_size("tile")
    size = lax.axis_size("src")
    rank = lax.axis_index("src").astype(jnp.int32)
    rightward, leftward, pack = messages(tile_slit, mask, target)
    from_left = shift(rightward, 1, groups)
    from_right = shift(leftward, -1, groups)
    pack = lax.dynamic_update_slice(pack, from_left, (0, 4 * TS))
    pack = lax.dynamic_update_slice(pack, from_right, (0, 4 * TS + SIDE))
    packs = [pack] + [swap(pack, m, size) for m in (1, 2, 3)]
    kern = synthesize(rank, tile_slit, (from_left, from_right), zernike, source_points, source_weight, start_block)
    notes = imaging(rank, packs, kern)
    return tuple(back(rank, [notes[0]] + [swap(notes[m], m, size) for m in (1, 2, 3)]))


def solution(mesh):
    placed = (P("src", "tile"), P("src", "tile"), P(), P(), P(), P(), P("tile"))
    return jax.shard_map(
        on_device,
        mesh=mesh,
        in_specs=placed,
        out_specs=(P("src", "tile"), P("src", "tile")),
        check_vma=False,
    )
```

```python
import math

import jax
import jax.numpy as jnp
import numpy as np
from jax import lax
from jax.experimental import pallas as pl
from jax.experimental.pallas import tpu as pltpu
from jax.sharding import PartitionSpec as P

KB = 128
NR = 24
NZ = 37
RAD = 40
SHIFT = 24
HALO = 64
ITERS = 4
TS = 256
PW = TS + 2 * HALO
GRID = 2 * SHIFT + 1
PUP = 2 * RAD + 1

STEEPNESS = 4.0
THRESHOLD = 0.5
RIDGE_SHARE = 0.001
BF = jnp.bfloat16
F32 = jnp.float32


def noll_terms(term_count):
    listing = []
    degree = 0
    while len(listing) < term_count:
        for azimuth in range(degree % 2, degree + 1, 2):
            if azimuth == 0:
                listing.append((degree, 0, 0))
            else:
                for repeat in range(2):
                    number = len(listing) + 1
                    listing.append((degree, azimuth, 2 if number % 2 == 0 else 1))
        degree += 1
    return listing[:term_count]


def radial_terms(degree, azimuth):
    powers = []
    for counter in range((degree - azimuth) // 2 + 1):
        factor = (
            (-1) ** counter
            * math.factorial(degree - counter)
            / (
                math.factorial(counter)
                * math.factorial((degree + azimuth) // 2 - counter)
                * math.factorial((degree - azimuth) // 2 - counter)
            )
        )
        powers.append((degree - 2 * counter, factor))
    return powers


def dft(rows, cols, sign, period=KB):
    return np.exp(sign * 2j * np.pi * np.mod(np.outer(rows, cols), period) / period)


def cmul(a, b):
    return (a[0] * b[0] - a[1] * b[1], a[0] * b[1] + a[1] * b[0])


SLOTS = 50
VMEM_CAP = 32 << 20
SIDE = TS + PW
ROWS = SLOTS * NR
PAD = 64
HI = lax.Precision.HIGHEST
UNROLL = 6
UNROLL_S = 12
UNROLL_F = 12
UNROLL_I = 12


ORDER = 9


def times(a, b):
    out = np.zeros((ORDER, ORDER), np.complex128)
    for i, j in zip(*np.nonzero(a)):
        for k, l in zip(*np.nonzero(b)):
            out[i + k, j + l] += a[i, j] * b[k, l]
    return out


def zernike_polynomials():
    one, step, square = (np.zeros((ORDER, ORDER), np.complex128) for _ in range(3))
    one[0, 0] = 1.0
    step[1, 0], step[0, 1] = 1.0, 1j
    square[2, 0] = square[0, 2] = 1.0
    lane = (np.arange(KB) - KB // 2) / RAD
    powers = lane[None, :] ** np.arange(ORDER)[:, None]
    out = np.zeros((NZ, 16, KB), np.float32)
    for number, (degree, azimuth, parity) in enumerate(noll_terms(NZ)):
        total = np.zeros((ORDER, ORDER))
        for power, scale in radial_terms(degree, azimuth):
            term = one
            for _ in range(azimuth):
                term = times(term, step)
            for _ in range((power - azimuth) // 2):
                term = times(term, square)
            total = total + scale * (term.real if azimuth == 0 or parity == 2 else term.imag)
        total = total * math.sqrt((1.0 if azimuth == 0 else 2.0) * (degree + 1.0))
        out[number, :ORDER] = total @ powers
    return out


def real_form(table):
    return np.block([[table.real, -table.imag], [table.imag, table.real]])


def split(table):
    high = table.astype(np.float32).astype(jnp.bfloat16)
    low = (table - high.astype(np.float64)).astype(jnp.bfloat16)
    return high, low


def block_tables():
    freq = np.arange(KB)
    big = real_form(dft(freq, np.arange(KB) - KB // 2, -1))
    offs = np.zeros((KB, PAD), np.complex128)
    offs[:, :GRID] = dft(freq, np.arange(GRID) - SHIFT, 1)
    small = real_form(offs)
    rev = np.zeros((PAD, KB), np.float32)
    for spot in range(GRID):
        rev[spot, KB // 2 + SHIFT - spot] = 1.0
    lb, lb_lo = split(big)
    lbt, lbt_lo = split(big.T.copy())
    lc, lc_lo = split(small)
    lct, lct_lo = split(small.T.copy())
    wide = lambda a, b: np.concatenate([a, b], axis=1)
    tall = lambda a, b: np.concatenate([a, b], axis=0)
    return (lb, lbt, lc, lct, tall(lct, lct_lo), wide(lc, lc_lo), lbt_lo, lb_lo, rev.astype(jnp.bfloat16), rev.T.copy().astype(jnp.bfloat16))


def near(*arrays):
    return tuple(pltpu.with_memory_space_constraint(x, pltpu.VMEM) for x in arrays)


def far(*arrays):
    return tuple(pltpu.with_memory_space_constraint(x, pltpu.HBM) for x in arrays)


def mm(a, b):
    return jnp.dot(a, b, preferred_element_type=F32)


def nt(a, b, precision=None):
    return lax.dot_general(a, b, (((1,), (1,)), ((), ())), precision=precision, preferred_element_type=F32)


def lanes(shape):
    return lax.broadcasted_iota(jnp.int32, shape, 1)


def sublanes(shape):
    return lax.broadcasted_iota(jnp.int32, shape, 0)


def halves(x):
    high = x.astype(BF)
    return high, (x - high.astype(F32)).astype(BF)


def stack_halves(x):
    return jnp.concatenate([part.astype(F32) for part in halves(x)], axis=0).astype(BF)


def fine_nt(a, b):
    full = nt(stack_halves(a), stack_halves(b))
    return full[:NR, :NR] + full[:NR, NR:] + full[NR:, :NR]


def fine_mm(a, b):
    ah, al = (x.astype(F32) for x in halves(a))
    bh, bl = (x.astype(F32) for x in halves(b))
    return mm(jnp.concatenate([ah, al, ah], axis=1).astype(BF), jnp.concatenate([bh, bh, bl], axis=0).astype(BF))


def factor(gram, floor):
    tile, blocks = 8, NR // 8
    rows = [slice(b * tile, (b + 1) * tile) for b in range(blocks)]
    wide_eye = (sublanes((NR, PAD)) == lanes((NR, PAD))).astype(F32)
    start = jnp.concatenate([gram, jnp.zeros((NR, PAD - NR), F32), wide_eye], axis=1)
    work = [start[x] for x in rows]
    col = [[jnp.broadcast_to(gram[x, j : j + 1], (tile, KB)) for x in rows] for j in range(NR)]
    row_no = sublanes((tile, KB))
    diag = [jnp.zeros((tile, KB), F32) for _ in rows]
    for k in range(NR):
        b0, r0 = divmod(k, tile)
        pick = lambda x: jnp.broadcast_to(x[r0 : r0 + 1, :], (tile, KB))
        pivot = jnp.maximum(pick(col[k][b0]), floor)
        diag[b0] = jnp.where(row_no == r0, pivot, diag[b0])
        inv = 1.0 / pivot
        ratio = [c * inv for c in col[k]]
        lead = pick(work[b0])
        for j in range(k + 1, NR):
            entry = pick(col[j][b0])
            for b in range(b0, blocks):
                col[j][b] = col[j][b] - ratio[b] * entry
        for b in range(b0, blocks):
            part = ratio[b] if b > b0 else jnp.where(row_no > r0, ratio[b], 0.0)
            work[b] = work[b] - part * lead
    done = jnp.concatenate([w * lax.rsqrt(d) for w, d in zip(work, diag)], axis=0)
    return done[:, :NR], done[:, PAD : PAD + NR]


def neighbour_marks(left_ref, right_ref):
    low = left_ref[0:16, TS : TS + KB].astype(F32)[0:1, 0:1]
    high = right_ref[0:16, SIDE - KB : SIDE].astype(F32)[0:1, KB - 1 : KB]
    return low, high


def synth_kernel(rank_ref, slit_ref, left_ref, right_ref, zern_ref, sp_ref, sw_ref, zt_ref, lb, lbt, lc, lct, lct2, lc2, rev, revt, b0_far, out_ref, inv_ref, hat, a1, f2, c_ref, h_ref, wf, bx, b0_ref, sem):
    b0_copy = pltpu.make_async_copy(b0_far, b0_ref, sem)
    b0_copy.start()
    weights = sw_ref[...]
    weights = weights / (math.pi * RAD * RAD * jnp.sum(weights, axis=1, keepdims=True))
    count = sp_ref.shape[1]
    offset = sublanes((KB, count))
    hot_x = jnp.where(offset - SHIFT == sp_ref[0:1, :], weights, 0.0)
    hot_y = (jnp.where(offset >= PAD, offset - PAD, offset) - SHIFT == sp_ref[1:2, :]).astype(F32).astype(BF)
    high, low = halves(hot_x)
    wmap = nt(high, hot_y) + nt(low, hot_y)
    for s in range(SLOTS):
        wf[s * NR : (s + 1) * NR, :] = jnp.broadcast_to(wmap[s : s + 1, :], (NR, KB))

    rank = rank_ref[0]
    low_end, high_end = neighbour_marks(left_ref, right_ref)
    slit = slit_ref[jnp.clip(rank - 1, 0, 1)].astype(F32)
    slit = jnp.where(rank == 0, low_end - 1.0, jnp.where(rank == 3, high_end - 1.0, slit))
    chosen = sublanes((zern_ref.shape[0], 1)).astype(F32) == jnp.maximum(slit, 0.0)
    coefs = jnp.sum(jnp.where(chosen, zern_ref[...], 0.0), axis=0, keepdims=True)
    by_row = jnp.zeros((16, KB), F32)
    for z in range(NZ):
        by_row = by_row + coefs[:, z : z + 1] * zt_ref[z]
    row_at, col_at = sublanes((96, KB)) - 48, lanes((96, KB)) - KB // 2
    scaled = row_at.astype(F32) / RAD
    turns = jnp.zeros((96, KB), F32)
    for power in range(ORDER - 1, -1, -1):
        turns = turns * scaled + by_row[power : power + 1, :]
    inside = (row_at * row_at + col_at * col_at <= RAD * RAD).astype(F32)
    turns = turns - jnp.floor(turns + 0.5)
    half = math.pi * turns
    sq = half * half
    sine = jnp.full_like(half, 1.0 / math.factorial(15))
    for n in (13, 11, 9, 7, 5, 3, 1):
        sine = 1.0 / math.factorial(n) - sine * sq
    sine = sine * half
    cosine = jnp.full_like(half, 1.0 / math.factorial(14))
    for n in (12, 10, 8, 6, 4, 2, 0):
        cosine = 1.0 / math.factorial(n) - cosine * sq
    pr = inside * (1.0 - 2.0 * sine * sine)
    pi = inside * (2.0 * sine * cosine)
    spot = lambda a, i, j: a[i : i + 1, j : j + 1]
    q1r, q1i = spot(pr, 88, 64), spot(pi, 88, 64)
    m1r, m1i = spot(pr, 8, 64), spot(pi, 8, 64)
    q2r, q2i = spot(pr, 48, 104), spot(pi, 48, 104)
    m2r, m2i = spot(pr, 48, 24), spot(pi, 48, 24)
    z1r, z1i = q1r * m1r + q1i * m1i, q1r * m1i - q1i * m1r
    z2r, z2i = q2r * m2r + q2i * m2i, q2r * m2i - q2i * m2r
    edge = jnp.zeros((16, 2 * KB), F32)
    both = jnp.concatenate([edge, jnp.concatenate([pr, pi], axis=1), edge], axis=0).astype(BF)
    ph = mm(both, lbt[...])
    stacked = jnp.concatenate([ph[:, :KB], ph[:, KB:]], axis=0).astype(BF)
    ph = mm(lb[...], stacked)
    hr, hi = ph[:KB], ph[KB:]
    hat[0] = jnp.concatenate([hr, hr], axis=1) / (KB * KB)
    hat[1] = jnp.concatenate([hi, hi], axis=1) / (KB * KB)
    power = (hr * hr + hi * hi) / (KB * KB)
    power = jnp.concatenate([power, power], axis=1)
    hat[2] = power

    rs, cs = sublanes((KB, KB)), lanes((KB, KB))
    at = lambda i, j, v: jnp.where((rs == i) & (cs == j), v, 0.0)
    one = jnp.ones((1, 1), F32)
    top = 2 * SHIFT
    ky = (
        at(0, 0, one) + at(PAD, PAD, one)
        + at(top, 0, z2r) + at(PAD + top, 0, -z2i) + at(top, PAD, z2i) + at(PAD + top, PAD, z2r)
        + at(0, top, z2r) + at(PAD, top, z2i) + at(0, PAD + top, -z2i) + at(PAD, PAD + top, z2r)
    ).astype(BF)
    none = jnp.zeros((KB, KB), BF)
    ky = jnp.concatenate([jnp.concatenate([ky, none], axis=1), jnp.concatenate([none, ky], axis=1)], axis=0)
    kq0 = jnp.concatenate([at(0, 0, q2r) + at(0, PAD, -q2i), at(0, 0, q2i) + at(0, PAD, q2r)], axis=0).astype(BF)
    kq2 = jnp.concatenate([at(0, 0, q2r) + at(PAD, 0, -q2i), at(0, 0, q2i) + at(PAD, 0, q2r)], axis=1).astype(BF)

    a1[:, ROWS:, :] = jnp.zeros((2, PAD * NR - ROWS, KB), F32)

    def pack(x0, x1):
        return jnp.concatenate(
            [jnp.concatenate([x0[:, :KB], x1[:, :KB]], axis=1), jnp.concatenate([x0[:, KB:], x1[:, KB:]], axis=1)], axis=0
        )

    def unpack(y, height):
        return (
            jnp.concatenate([y[:height, :KB], y[height:, :KB]], axis=1),
            jnp.concatenate([y[:height, KB:], y[height:, KB:]], axis=1),
        )

    def put(ref, k, x):
        ref[0, pl.ds(k, PAD, stride=NR), :] = x[:, :KB]
        ref[1, pl.ds(k, PAD, stride=NR), :] = x[:, KB:]

    def get(ref, k):
        return jnp.concatenate([ref[0, pl.ds(k, PAD, stride=NR), :], ref[1, pl.ds(k, PAD, stride=NR), :]], axis=1)

    def both_halves(ref):
        return jnp.concatenate([ref[0, :ROWS, :], ref[1, :ROWS, :]], axis=1).astype(BF)

    prow = sublanes((KB, 2 * KB))
    urow = sublanes((2 * KB, 2 * KB))

    def start(q, carry):
        pairs = [q * UNROLL_S + j for j in range(UNROLL_S)]
        blocks = [[jnp.concatenate([b0_ref[0, 2 * p + e], b0_ref[1, 2 * p + e]], axis=1).astype(BF) for e in range(2)] for p in pairs]
        xs = [pack(mm(b[0], lbt[...]), mm(b[1], lbt[...])) for b in blocks]
        revs = [[mm(rev[...], e) for e in b] for b in blocks]
        ys = [mm(lb[...], x.astype(BF)) for x in xs]
        ys = [jnp.concatenate([hat[0] * y[:KB] + hat[1] * y[KB:], hat[0] * y[KB:] - hat[1] * y[:KB]], axis=0).astype(BF) for y in ys]
        ds = [mm(lct[...], y) for y in ys]
        for p, x, d, rv in zip(pairs, xs, ds, revs):
            xr, xi = x[0:1], x[KB : KB + 1]
            cr, ci = (q1r * xr + q1i * xi) / KB, (q1r * xi - q1i * xr) / KB
            d = d - jnp.where(prow == 0, cr, 0.0) - jnp.where(prow == PAD, ci, 0.0)
            d0, d1 = unpack(d, PAD)
            put(f2, 2 * p, d0)
            put(f2, 2 * p + 1, d1)
            put(bx, 2 * p, rv[0])
            put(bx, 2 * p + 1, rv[1])
        return carry

    b0_copy.wait()
    lax.fori_loop(0, NR // 2 // UNROLL_S, start, 0)
    first = mm(both_halves(f2), lc[...]) - mm(both_halves(bx), kq0)
    c_ref[...] = wf[...] * first

    def wide(ref):
        return jnp.concatenate([ref[s * NR : (s + 1) * NR, :] for s in range(SLOTS)], axis=1)

    def tallput(ref, x):
        for s in range(SLOTS):
            ref[s * NR : (s + 1) * NR, :] = x[:, s * KB : (s + 1) * KB]

    def forward(p):
        return pack(get(a1, 2 * p), get(a1, 2 * p + 1)).astype(BF)

    def middle(q, carry):
        pairs = [q * UNROLL + j for j in range(UNROLL)]
        ys = [mm(lc[...], forward(p)) for p in pairs]
        ys = [jnp.concatenate([hat[2] * y[:KB], hat[2] * y[KB:]], axis=0).astype(BF) for y in ys]
        ds = [mm(lct[...], y) for y in ys]
        for p, d in zip(pairs, ds):
            d0, d1 = unpack(d, PAD)
            put(f2, 2 * p, d0)
            put(f2, 2 * p + 1, d1)
        return carry

    def apply():
        coef = c_ref[...].astype(BF)
        full = mm(coef, lct[...])
        a1[0, :ROWS, :] = full[:, :KB]
        a1[1, :ROWS, :] = full[:, KB:]
        lax.fori_loop(0, NR // 2 // UNROLL, middle, 0)
        last = slice(top * NR, (top + 1) * NR)
        lr, li, ur, ui = a1[0, 0:NR, :], a1[1, 0:NR, :], a1[0, last, :], a1[1, last, :]
        f2[0, 0:NR, :] = f2[0, 0:NR, :] - (lr + z1r * ur - z1i * ui) / KB
        f2[1, 0:NR, :] = f2[1, 0:NR, :] - (li + z1r * ui + z1i * ur) / KB
        f2[0, last, :] = f2[0, last, :] - (z1r * lr + z1i * li) / KB
        f2[1, last, :] = f2[1, last, :] - (z1r * li - z1i * lr) / KB
        corr = mm(jnp.concatenate([c_ref[: ROWS // 2, :], c_ref[ROWS // 2 :, :]], axis=1).astype(BF), ky)
        h_ref[...] = mm(both_halves(f2), lc[...]) - jnp.concatenate([corr[:, :KB], corr[:, KB:]], axis=0)
        gram = fine_nt(wide(c_ref), wide(h_ref))
        gram = 0.5 * (gram + gram.T)
        eye = sublanes((NR, NR)) == lanes((NR, NR))
        trace = jnp.sum(jnp.sum(jnp.where(eye, gram, 0.0), axis=1, keepdims=True), axis=0, keepdims=True)
        return factor(gram + jnp.where(eye, RIDGE_SHARE * trace / NR + 1e-06, 0.0), 0.0)[1]

    def step(iteration, carry):
        @pl.when(iteration > 0)
        def _():
            tallput(h_ref, fine_mm(inv_ref[:, :NR], wide(h_ref)))
            c_ref[...] = wf[...] * h_ref[...]

        inv_ref[:, :NR] = apply()
        return carry

    lax.fori_loop(0, ITERS, step, 0)
    inverse = inv_ref[:, :NR]
    f2[0, :ROWS, :] = wf[...] * h_ref[...]
    moment = fine_nt(jnp.concatenate([f2[0, s * NR : (s + 1) * NR, :] for s in range(SLOTS)], axis=1), wide(h_ref))
    moment = jnp.dot(inverse, moment, precision=HI, preferred_element_type=F32)
    mixing = nt(moment, inverse, HI)
    mixing = 0.5 * (mixing + mixing.T)
    eye = sublanes((NR, NR)) == lanes((NR, NR))
    trace = jnp.sum(jnp.sum(jnp.where(eye, mixing, 0.0), axis=1, keepdims=True), axis=0, keepdims=True)
    root = factor(mixing, 1e-6 * trace + 1e-30)[0]
    combine = jnp.dot(root, inverse, precision=HI, preferred_element_type=F32)
    tallput(c_ref, fine_mm(combine, wide(c_ref)))
    coef = c_ref[...].astype(BF)
    full = mm(jnp.concatenate([coef, coef], axis=1), lct2[...])
    a1[0, :ROWS, :] = full[:, :KB]
    a1[1, :ROWS, :] = full[:, KB:]
    shifted = mm(coef, kq2)
    f2[0, :ROWS, :] = shifted[:, :KB]
    f2[1, :ROWS, :] = shifted[:, KB:]
    f2[:, ROWS:, :] = jnp.zeros((2, PAD * NR - ROWS, KB), F32)

    def finish(q, carry):
        pairs = [q * UNROLL_F + j for j in range(UNROLL_F)]
        xs = [pack(get(a1, 2 * p), get(a1, 2 * p + 1)) for p in pairs]
        cols = [[mm(revt[...], get(f2, 2 * p + e).astype(BF)) for e in range(2)] for p in pairs]
        ys = [mm(lc2[...], jnp.concatenate([x, x], axis=0).astype(BF)) for x in xs]
        ys = [jnp.concatenate([hat[0] * y[:KB] - hat[1] * y[KB:], hat[0] * y[KB:] + hat[1] * y[:KB]], axis=0).astype(BF) for y in ys]
        us = [mm(lbt[...], y) for y in ys]
        for p, x, u, col in zip(pairs, xs, us, cols):
            xr, xi = x[0:1], x[PAD : PAD + 1]
            cr, ci = (q1r * xr - q1i * xi) / KB, (q1r * xi + q1i * xr) / KB
            u = u - jnp.where(urow == 0, cr, 0.0) - jnp.where(urow == KB, ci, 0.0)
            pair = unpack(u, KB)
            for e in range(2):
                ub = pair[e].astype(BF)
                out_ref[2 * p + e] = (mm(ub, lb[...]) - col[e]).astype(BF)
        return carry

    lax.fori_loop(0, NR // 2 // UNROLL_F, finish, 0)


def synthesize(rank, tile_slit, sides, zernike, source_points, source_weight, start_block):
    smem = pl.BlockSpec(memory_space=pltpu.SMEM)
    vmem = pl.BlockSpec(memory_space=pltpu.VMEM)
    tables = block_tables()
    tables = [jnp.asarray(tables[i]) for i in (0, 1, 2, 3, 4, 5, 8, 9)]
    big = (2, PAD * NR, KB)
    return pl.pallas_call(
        synth_kernel,
        out_shape=jax.ShapeDtypeStruct((NR, KB, 2 * KB), BF),
        in_specs=[smem] * 2 + [vmem] * (6 + len(tables)) + [pl.BlockSpec(memory_space=pl.ANY)],
        out_specs=vmem,
        compiler_params=pltpu.CompilerParams(vmem_limit_bytes=VMEM_CAP),
        scratch_shapes=[
            pltpu.VMEM((NR, KB), F32),
            pltpu.VMEM((3, KB, 2 * KB), F32),
            pltpu.VMEM(big, F32),
            pltpu.VMEM(big, F32),
            pltpu.VMEM((ROWS, KB), F32),
            pltpu.VMEM((ROWS, KB), F32),
            pltpu.VMEM((ROWS, KB), F32),
            pltpu.VMEM(big, F32),
            pltpu.VMEM(start_block.shape, F32),
            pltpu.SemaphoreType.DMA,
        ],
    )(rank.reshape(1), *far(tile_slit), *sides, *far(zernike, source_points.T, source_weight.reshape(1, -1), jnp.asarray(zernike_polynomials()), *tables, start_block))


def tables_of(count, period):
    t = dft(np.arange(count), np.arange(KB) - KB // 2, 1, period)
    return t.real.astype(np.float32), t.imag.astype(np.float32)


def cast(x):
    return np.ascontiguousarray(x).astype(jnp.bfloat16)


def column_table():
    cc, cs = tables_of(PW, PW)
    out = np.zeros((5 * TS, 2 * KB), np.float32)
    out[2 * TS - HALO : 2 * TS - HALO + PW] = np.concatenate([cc, -cs], 1)
    return cast(out)


def row_table():
    rc, rs = tables_of(TS, TS)
    return np.concatenate([rc, rs], 1)


def image_tables():
    rc, rs = tables_of(TS, TS)
    cc, cs = tables_of(PW, PW)
    turn = np.concatenate([rc.T, rs.T], 1)
    inv_t = np.concatenate([cc, -cs], 1)[HALO : HALO + TS].T
    adj = np.concatenate([cc, cs], 1)[HALO : HALO + TS]
    rows = row_table()
    return (column_table(),) + tuple(cast(x) for x in (rows.T, rows, turn, inv_t, adj))


def tile_columns(ref, tile):
    return ref[pl.ds(pl.multiple_of(TS * (3 - tile), TS), 2 * TS), :]


def image_kernel(rank_ref, m0, m1, m2, m3, kern_ref, fwd, rows_t, rows, turn, inv_t, adj, o0, o1, o2, o3, patch, goal, fields, inten, gsum, spec):
    rank = rank_ref[0]
    quarter = m0.shape[0]
    left, outer = rank < 2, (rank == 0) | (rank == 3)
    block_of = lambda j: pl.ds(pl.multiple_of((rank ^ j) * quarter, quarter), quarter)
    low_end, high_end = neighbour_marks(m0.at[:, 4 * TS : 4 * TS + SIDE], m0.at[:, 4 * TS + SIDE :])
    present = jnp.where(rank == 0, low_end, jnp.where(rank == 3, high_end, 1.0)) > 0.5
    for j, m in enumerate((m0, m1, m2, m3)):
        side = jnp.where(left, m[:, 4 * TS : 4 * TS + SIDE], m[:, 4 * TS + SIDE :])
        own = jnp.where(left, m[:, 2 * TS : 3 * TS], m[:, 3 * TS : 4 * TS])
        patch[block_of(j), : 2 * TS] = m[:, : 2 * TS]
        patch[block_of(j), 2 * TS :] = side[:, TS:]
        goal[block_of(j), :] = jnp.where(outer, side[:, :TS], own).astype(F32)
    s = 1.0 / math.sqrt(TS * PW)
    start = jnp.where(rank < 2, PW - rank * TS, 3 * TS - (rank - 2) * TS)
    side_table = fwd[pl.ds(pl.multiple_of(start, HALO), PW), :]
    table = jnp.concatenate([tile_columns(fwd, rank), side_table], axis=0)
    columns = mm(patch[...], table).astype(BF)
    sums = mm(rows_t[...], columns)
    spec[0] = s * (sums[:KB, :KB] + sums[KB:, KB:])
    spec[1] = s * (sums[:KB, KB:] - sums[KB:, :KB])
    inten[...] = jnp.zeros((TS, TS), F32)
    gsum[...] = jnp.zeros((KB, 2 * KB), F32)

    def forward(q, carry):
        ks = [q * UNROLL_I + e for e in range(UNROLL_I)]
        sr, si = spec[0], spec[1]
        blocks = []
        for k in ks:
            kr, ki = kern_ref[k, :, :KB].astype(F32), kern_ref[k, :, KB:].astype(F32)
            wr, wi = kr * sr + ki * si, kr * si - ki * sr
            blocks.append(jnp.concatenate([jnp.concatenate([wr, wi], axis=1), jnp.concatenate([-wi, wr], axis=1)], axis=0).astype(BF))
        waves = [mm(rows[...], b).astype(BF) for b in blocks]
        total = inten[...]
        for k, w in zip(ks, waves):
            field = mm(w, inv_t[...])
            fields[k] = field
            total = total + field * field
        inten[...] = total
        return carry

    lax.fori_loop(0, NR // UNROLL_I, forward, 0)
    resist = 1.0 / (1.0 + jnp.exp(-STEEPNESS * (inten[...] - THRESHOLD)))
    inten[...] = 4.0 * (resist - goal[...]) * STEEPNESS * resist * (1.0 - resist)
    goal[...] = resist

    def backward(q, carry):
        ks = [q * UNROLL_I + e for e in range(UNROLL_I)]
        cols = [mm((fields[k] * inten[...]).astype(BF), adj[...]) for k in ks]
        blocks = [jnp.concatenate([c, jnp.concatenate([-c[:, KB:], c[:, :KB]], axis=1)], axis=0).astype(BF) for c in cols]
        turned = [mm(turn[...], b) for b in blocks]
        gr, gi = gsum[:, :KB], gsum[:, KB:]
        for k, y in zip(ks, turned):
            kr, ki = kern_ref[k, :, :KB].astype(F32), kern_ref[k, :, KB:].astype(F32)
            gr = gr + kr * y[:, :KB] + ki * y[:, KB:]
            gi = gi + ki * y[:, :KB] - kr * y[:, KB:]
        gsum[:, :KB] = gr
        gsum[:, KB:] = gi
        return carry

    lax.fori_loop(0, NR // UNROLL_I, backward, 0)
    grad = jnp.where(present, s * gsum[...], 0.0)
    block = jnp.concatenate([grad, jnp.concatenate([-grad[:, KB:], grad[:, :KB]], axis=1)], axis=0).astype(BF)
    inten[...] = mm(rows[...], block)
    for j, o in enumerate((o0, o1, o2, o3)):
        o[:quarter, :] = inten[block_of(j), :].astype(BF)
        o[quarter:, :] = goal[block_of(j), :].astype(BF)


def imaging(rank, packs, kern):
    quarter = packs[0].shape[0]
    smem = pl.BlockSpec(memory_space=pltpu.SMEM)
    vmem = pl.BlockSpec(memory_space=pltpu.VMEM)
    tables = [jnp.asarray(x) for x in image_tables()]
    return pl.pallas_call(
        image_kernel,
        out_shape=(jax.ShapeDtypeStruct((2 * quarter, TS), BF),) * 4,
        in_specs=[smem] + [vmem] * (5 + len(tables)),
        out_specs=(vmem,) * 4,
        compiler_params=pltpu.CompilerParams(vmem_limit_bytes=VMEM_CAP),
        scratch_shapes=[
            pltpu.VMEM((TS, 2 * TS + PW), BF),
            pltpu.VMEM((TS, TS), F32),
            pltpu.VMEM((NR, TS, TS), F32),
            pltpu.VMEM((TS, TS), F32),
            pltpu.VMEM((KB, 2 * KB), F32),
            pltpu.VMEM((2, KB, KB), F32),
        ],
    )(rank.reshape(1), *near(*packs, kern, *tables))


def back_kernel(rank_ref, n0, n1, n2, n3, fwd, resist_ref, grad_ref, held):
    rank = rank_ref[0]
    quarter, width = grad_ref.shape
    for j, n in enumerate((n0, n1, n2, n3)):
        held[rank ^ j] = n[...]
    resist_ref[:, :TS] = held[1, quarter:, :]
    resist_ref[:, TS:] = held[2, quarter:, :]
    parts = []
    for tile in range(4):
        parts.append(nt(held[tile, :quarter, :], fwd[TS * (3 - tile) : TS * (5 - tile), :]))
    grad_ref[...] = (parts[0] + parts[1] + parts[2] + parts[3]).astype(BF)


def back(rank, notes):
    quarter = notes[0].shape[0] // 2
    smem = pl.BlockSpec(memory_space=pltpu.SMEM)
    vmem = pl.BlockSpec(memory_space=pltpu.VMEM)
    whole = jax.ShapeDtypeStruct((quarter, 2 * TS), BF)
    return pl.pallas_call(
        back_kernel,
        out_shape=(whole, whole),
        in_specs=[smem] + [vmem] * 5,
        out_specs=(vmem, vmem),
        compiler_params=pltpu.CompilerParams(vmem_limit_bytes=VMEM_CAP),
        scratch_shapes=[pltpu.VMEM((4, 2 * quarter, TS), BF)],
    )(rank.reshape(1), *near(*notes, jnp.asarray(column_table())))


def prep_kernel(slit_ref, mask, goal, right_ref, left_ref, pack_ref):
    quarter = mask.shape[0]
    lane = lanes((quarter, PW))
    pack_ref[:, : 2 * TS] = mask[...]
    pack_ref[:, 2 * TS : 4 * TS] = goal[...]
    right_ref[:, :TS] = goal[:, TS:]
    left_ref[:, :TS] = goal[:, :TS]
    first, second = (slit_ref[0] + 1).astype(F32), (slit_ref[1] + 1).astype(F32)
    right_ref[:, TS:] = jnp.where(lane < HALO, second, mask[:, 2 * TS - PW :].astype(F32)).astype(BF)
    left_ref[:, TS:] = jnp.where(lane >= PW - HALO, first, mask[:, :PW].astype(F32)).astype(BF)


def messages(tile_slit, mask, target):
    smem = pl.BlockSpec(memory_space=pltpu.SMEM)
    vmem = pl.BlockSpec(memory_space=pltpu.VMEM)
    return pl.pallas_call(
        prep_kernel,
        out_shape=tuple(jax.ShapeDtypeStruct((mask.shape[0], w), BF) for w in (SIDE, SIDE, 4 * TS + 2 * SIDE)),
        compiler_params=pltpu.CompilerParams(vmem_limit_bytes=VMEM_CAP),
        in_specs=[smem, vmem, vmem],
        out_specs=(vmem, vmem, vmem),
    )(*far(tile_slit, mask, target))


def swap(x, m, size):
    return lax.ppermute(x, "src", [(i, i ^ m) for i in range(size)])


def shift(x, step, count):
    pairs = [(i, i + step) for i in range(count) if 0 <= i + step < count]
    return lax.ppermute(x, "tile", pairs)


def on_device(mask, target, start_block, zernike, source_points, source_weight, tile_slit):
    groups = lax.axis_size("tile")
    size = lax.axis_size("src")
    rank = lax.axis_index("src").astype(jnp.int32)
    rightward, leftward, pack = messages(tile_slit, mask, target)
    from_left = shift(rightward, 1, groups)
    from_right = shift(leftward, -1, groups)
    pack = lax.dynamic_update_slice(pack, from_left, (0, 4 * TS))
    pack = lax.dynamic_update_slice(pack, from_right, (0, 4 * TS + SIDE))
    packs = [pack] + [swap(pack, m, size) for m in (1, 2, 3)]
    kern = synthesize(rank, tile_slit, (from_left, from_right), zernike, source_points, source_weight, start_block)
    notes = imaging(rank, packs, kern)
    return tuple(back(rank, [notes[0]] + [swap(notes[m], m, size) for m in (1, 2, 3)]))


def solution(mesh):
    placed = (P("src", "tile"), P("src", "tile"), P(), P(), P(), P(), P("tile"))
    return jax.shard_map(
        on_device,
        mesh=mesh,
        in_specs=placed,
        out_specs=(P("src", "tile"), P("src", "tile")),
        check_vma=False,
    )
```

```python
import math

import jax
import jax.numpy as jnp
import numpy as np
from jax import lax
from jax.experimental import pallas as pl
from jax.experimental.pallas import tpu as pltpu
from jax.sharding import PartitionSpec as P

KB = 128
NR = 24
NZ = 37
RAD = 40
SHIFT = 24
HALO = 64
ITERS = 4
TS = 256
PW = TS + 2 * HALO
GRID = 2 * SHIFT + 1
PUP = 2 * RAD + 1

STEEPNESS = 4.0
THRESHOLD = 0.5
RIDGE_SHARE = 0.001
BF = jnp.bfloat16
F32 = jnp.float32


def noll_terms(term_count):
    listing = []
    degree = 0
    while len(listing) < term_count:
        for azimuth in range(degree % 2, degree + 1, 2):
            if azimuth == 0:
                listing.append((degree, 0, 0))
            else:
                for repeat in range(2):
                    number = len(listing) + 1
                    listing.append((degree, azimuth, 2 if number % 2 == 0 else 1))
        degree += 1
    return listing[:term_count]


def radial_terms(degree, azimuth):
    powers = []
    for counter in range((degree - azimuth) // 2 + 1):
        factor = (
            (-1) ** counter
            * math.factorial(degree - counter)
            / (
                math.factorial(counter)
                * math.factorial((degree + azimuth) // 2 - counter)
                * math.factorial((degree - azimuth) // 2 - counter)
            )
        )
        powers.append((degree - 2 * counter, factor))
    return powers


def dft(rows, cols, sign, period=KB):
    return np.exp(sign * 2j * np.pi * np.mod(np.outer(rows, cols), period) / period)


def cmul(a, b):
    return (a[0] * b[0] - a[1] * b[1], a[0] * b[1] + a[1] * b[0])


SLOTS = 50
VMEM_CAP = 32 << 20
SIDE = TS + PW
ROWS = SLOTS * NR
PAD = 64
HI = lax.Precision.HIGHEST
UNROLL = 6
UNROLL_S = 12
UNROLL_F = 12
UNROLL_I = 12


ORDER = 9


def times(a, b):
    out = np.zeros((ORDER, ORDER), np.complex128)
    for i, j in zip(*np.nonzero(a)):
        for k, l in zip(*np.nonzero(b)):
            out[i + k, j + l] += a[i, j] * b[k, l]
    return out


def zernike_polynomials():
    one, step, square = (np.zeros((ORDER, ORDER), np.complex128) for _ in range(3))
    one[0, 0] = 1.0
    step[1, 0], step[0, 1] = 1.0, 1j
    square[2, 0] = square[0, 2] = 1.0
    lane = (np.arange(KB) - KB // 2) / RAD
    powers = lane[None, :] ** np.arange(ORDER)[:, None]
    out = np.zeros((NZ, 16, KB), np.float32)
    for number, (degree, azimuth, parity) in enumerate(noll_terms(NZ)):
        total = np.zeros((ORDER, ORDER))
        for power, scale in radial_terms(degree, azimuth):
            term = one
            for _ in range(azimuth):
                term = times(term, step)
            for _ in range((power - azimuth) // 2):
                term = times(term, square)
            total = total + scale * (term.real if azimuth == 0 or parity == 2 else term.imag)
        total = total * math.sqrt((1.0 if azimuth == 0 else 2.0) * (degree + 1.0))
        out[number, :ORDER] = total @ powers
    return out


def real_form(table):
    return np.block([[table.real, -table.imag], [table.imag, table.real]])


def split(table):
    high = table.astype(np.float32).astype(jnp.bfloat16)
    low = (table - high.astype(np.float64)).astype(jnp.bfloat16)
    return high, low


def block_tables():
    freq = np.arange(KB)
    big = real_form(dft(freq, np.arange(KB) - KB // 2, -1))
    offs = np.zeros((KB, PAD), np.complex128)
    offs[:, :GRID] = dft(freq, np.arange(GRID) - SHIFT, 1)
    small = real_form(offs)
    rev = np.zeros((PAD, KB), np.float32)
    for spot in range(GRID):
        rev[spot, KB // 2 + SHIFT - spot] = 1.0
    lb, lb_lo = split(big)
    lbt, lbt_lo = split(big.T.copy())
    lc, lc_lo = split(small)
    lct, lct_lo = split(small.T.copy())
    wide = lambda a, b: np.concatenate([a, b], axis=1)
    tall = lambda a, b: np.concatenate([a, b], axis=0)
    return (lb, lbt, lc, lct, tall(lct, lct_lo), wide(lc, lc_lo), lbt_lo, lb_lo, rev.astype(jnp.bfloat16), rev.T.copy().astype(jnp.bfloat16))


def near(*arrays):
    return tuple(pltpu.with_memory_space_constraint(x, pltpu.VMEM) for x in arrays)


def far(*arrays):
    return tuple(pltpu.with_memory_space_constraint(x, pltpu.HBM) for x in arrays)


def mm(a, b):
    return jnp.dot(a, b, preferred_element_type=F32)


def nt(a, b, precision=None):
    return lax.dot_general(a, b, (((1,), (1,)), ((), ())), precision=precision, preferred_element_type=F32)


def lanes(shape):
    return lax.broadcasted_iota(jnp.int32, shape, 1)


def sublanes(shape):
    return lax.broadcasted_iota(jnp.int32, shape, 0)


def halves(x):
    high = x.astype(BF)
    return high, (x - high.astype(F32)).astype(BF)


def stack_halves(x):
    return jnp.concatenate([part.astype(F32) for part in halves(x)], axis=0).astype(BF)


def fine_nt(a, b):
    full = nt(stack_halves(a), stack_halves(b))
    return full[:NR, :NR] + full[:NR, NR:] + full[NR:, :NR]


def fine_mm(a, b):
    ah, al = (x.astype(F32) for x in halves(a))
    bh, bl = (x.astype(F32) for x in halves(b))
    return mm(jnp.concatenate([ah, al, ah], axis=1).astype(BF), jnp.concatenate([bh, bh, bl], axis=0).astype(BF))


def factor(gram, floor):
    tile, blocks = 8, NR // 8
    rows = [slice(b * tile, (b + 1) * tile) for b in range(blocks)]
    wide_eye = (sublanes((NR, PAD)) == lanes((NR, PAD))).astype(F32)
    start = jnp.concatenate([gram, jnp.zeros((NR, PAD - NR), F32), wide_eye], axis=1)
    work = [start[x] for x in rows]
    col = [[jnp.broadcast_to(gram[x, j : j + 1], (tile, KB)) for x in rows] for j in range(NR)]
    row_no = sublanes((tile, KB))
    diag = [jnp.zeros((tile, KB), F32) for _ in rows]
    for k in range(NR):
        b0, r0 = divmod(k, tile)
        pick = lambda x: jnp.broadcast_to(x[r0 : r0 + 1, :], (tile, KB))
        pivot = jnp.maximum(pick(col[k][b0]), floor)
        diag[b0] = jnp.where(row_no == r0, pivot, diag[b0])
        inv = 1.0 / pivot
        ratio = [c * inv for c in col[k]]
        lead = pick(work[b0])
        for j in range(k + 1, NR):
            entry = pick(col[j][b0])
            for b in range(b0, blocks):
                col[j][b] = col[j][b] - ratio[b] * entry
        for b in range(b0, blocks):
            part = ratio[b] if b > b0 else jnp.where(row_no > r0, ratio[b], 0.0)
            work[b] = work[b] - part * lead
    done = jnp.concatenate([w * lax.rsqrt(d) for w, d in zip(work, diag)], axis=0)
    return done[:, :NR], done[:, PAD : PAD + NR]


def neighbour_marks(left_ref, right_ref):
    low = left_ref[0:16, TS : TS + KB].astype(F32)[0:1, 0:1]
    high = right_ref[0:16, SIDE - KB : SIDE].astype(F32)[0:1, KB - 1 : KB]
    return low, high


def synth_kernel(rank_ref, slit_ref, left_ref, right_ref, zern_ref, sp_ref, sw_ref, zt_ref, lb, lbt, lc, lct, lct2, lc2, rev, revt, b0_far, out_ref, inv_ref, hat, a1, f2, c_ref, h_ref, wf, bx, b0_ref, sem):
    b0_copy = pltpu.make_async_copy(b0_far, b0_ref, sem)
    b0_copy.start()
    weights = sw_ref[...]
    weights = weights / (math.pi * RAD * RAD * jnp.sum(weights, axis=1, keepdims=True))
    count = sp_ref.shape[1]
    offset = sublanes((KB, count))
    hot_x = jnp.where(offset - SHIFT == sp_ref[0:1, :], weights, 0.0)
    hot_y = (jnp.where(offset >= PAD, offset - PAD, offset) - SHIFT == sp_ref[1:2, :]).astype(F32).astype(BF)
    high, low = halves(hot_x)
    wmap = nt(high, hot_y) + nt(low, hot_y)
    for s in range(SLOTS):
        wf[s * NR : (s + 1) * NR, :] = jnp.broadcast_to(wmap[s : s + 1, :], (NR, KB))

    rank = rank_ref[0]
    low_end, high_end = neighbour_marks(left_ref, right_ref)
    slit = slit_ref[jnp.clip(rank - 1, 0, 1)].astype(F32)
    slit = jnp.where(rank == 0, low_end - 1.0, jnp.where(rank == 3, high_end - 1.0, slit))
    chosen = sublanes((zern_ref.shape[0], 1)).astype(F32) == jnp.maximum(slit, 0.0)
    coefs = jnp.sum(jnp.where(chosen, zern_ref[...], 0.0), axis=0, keepdims=True)
    by_row = jnp.zeros((16, KB), F32)
    for z in range(NZ):
        by_row = by_row + coefs[:, z : z + 1] * zt_ref[z]
    row_at, col_at = sublanes((96, KB)) - 48, lanes((96, KB)) - KB // 2
    scaled = row_at.astype(F32) / RAD
    turns = jnp.zeros((96, KB), F32)
    for power in range(ORDER - 1, -1, -1):
        turns = turns * scaled + by_row[power : power + 1, :]
    inside = (row_at * row_at + col_at * col_at <= RAD * RAD).astype(F32)
    turns = turns - jnp.floor(turns + 0.5)
    half = math.pi * turns
    sq = half * half
    sine = jnp.full_like(half, 1.0 / math.factorial(15))
    for n in (13, 11, 9, 7, 5, 3, 1):
        sine = 1.0 / math.factorial(n) - sine * sq
    sine = sine * half
    cosine = jnp.full_like(half, 1.0 / math.factorial(14))
    for n in (12, 10, 8, 6, 4, 2, 0):
        cosine = 1.0 / math.factorial(n) - cosine * sq
    pr = inside * (1.0 - 2.0 * sine * sine)
    pi = inside * (2.0 * sine * cosine)
    spot = lambda a, i, j: a[i : i + 1, j : j + 1]
    q1r, q1i = spot(pr, 88, 64), spot(pi, 88, 64)
    m1r, m1i = spot(pr, 8, 64), spot(pi, 8, 64)
    q2r, q2i = spot(pr, 48, 104), spot(pi, 48, 104)
    m2r, m2i = spot(pr, 48, 24), spot(pi, 48, 24)
    z1r, z1i = q1r * m1r + q1i * m1i, q1r * m1i - q1i * m1r
    z2r, z2i = q2r * m2r + q2i * m2i, q2r * m2i - q2i * m2r
    edge = jnp.zeros((16, 2 * KB), F32)
    both = jnp.concatenate([edge, jnp.concatenate([pr, pi], axis=1), edge], axis=0).astype(BF)
    ph = mm(both, lbt[...])
    stacked = jnp.concatenate([ph[:, :KB], ph[:, KB:]], axis=0).astype(BF)
    ph = mm(lb[...], stacked)
    hr, hi = ph[:KB], ph[KB:]
    hat[0] = jnp.concatenate([hr, hr], axis=1) / (KB * KB)
    hat[1] = jnp.concatenate([hi, hi], axis=1) / (KB * KB)
    power = (hr * hr + hi * hi) / (KB * KB)
    power = jnp.concatenate([power, power], axis=1)
    hat[2] = power

    rs, cs = sublanes((KB, KB)), lanes((KB, KB))
    at = lambda i, j, v: jnp.where((rs == i) & (cs == j), v, 0.0)
    one = jnp.ones((1, 1), F32)
    top = 2 * SHIFT
    ky = (
        at(0, 0, one) + at(PAD, PAD, one)
        + at(top, 0, z2r) + at(PAD + top, 0, -z2i) + at(top, PAD, z2i) + at(PAD + top, PAD, z2r)
        + at(0, top, z2r) + at(PAD, top, z2i) + at(0, PAD + top, -z2i) + at(PAD, PAD + top, z2r)
    ).astype(BF)
    none = jnp.zeros((KB, KB), BF)
    ky = jnp.concatenate([jnp.concatenate([ky, none], axis=1), jnp.concatenate([none, ky], axis=1)], axis=0)
    kq0 = jnp.concatenate([at(0, 0, q2r) + at(0, PAD, -q2i), at(0, 0, q2i) + at(0, PAD, q2r)], axis=0).astype(BF)
    kq2 = jnp.concatenate([at(0, 0, q2r) + at(PAD, 0, -q2i), at(0, 0, q2i) + at(PAD, 0, q2r)], axis=1).astype(BF)

    a1[:, ROWS:, :] = jnp.zeros((2, PAD * NR - ROWS, KB), F32)

    def pack(x0, x1):
        return jnp.concatenate(
            [jnp.concatenate([x0[:, :KB], x1[:, :KB]], axis=1), jnp.concatenate([x0[:, KB:], x1[:, KB:]], axis=1)], axis=0
        )

    def unpack(y, height):
        return (
            jnp.concatenate([y[:height, :KB], y[height:, :KB]], axis=1),
            jnp.concatenate([y[:height, KB:], y[height:, KB:]], axis=1),
        )

    def put(ref, k, x):
        ref[0, pl.ds(k, PAD, stride=NR), :] = x[:, :KB]
        ref[1, pl.ds(k, PAD, stride=NR), :] = x[:, KB:]

    def get(ref, k):
        return jnp.concatenate([ref[0, pl.ds(k, PAD, stride=NR), :], ref[1, pl.ds(k, PAD, stride=NR), :]], axis=1)

    def both_halves(ref):
        return jnp.concatenate([ref[0, :ROWS, :], ref[1, :ROWS, :]], axis=1).astype(BF)

    prow = sublanes((KB, 2 * KB))
    urow = sublanes((2 * KB, 2 * KB))

    def start(q, carry):
        pairs = [q * UNROLL_S + j for j in range(UNROLL_S)]
        blocks = [[jnp.concatenate([b0_ref[0, 2 * p + e], b0_ref[1, 2 * p + e]], axis=1).astype(BF) for e in range(2)] for p in pairs]
        xs = [pack(mm(b[0], lbt[...]), mm(b[1], lbt[...])) for b in blocks]
        revs = [[mm(rev[...], e) for e in b] for b in blocks]
        ys = [mm(lb[...], x.astype(BF)) for x in xs]
        ys = [jnp.concatenate([hat[0] * y[:KB] + hat[1] * y[KB:], hat[0] * y[KB:] - hat[1] * y[:KB]], axis=0).astype(BF) for y in ys]
        ds = [mm(lct[...], y) for y in ys]
        for p, x, d, rv in zip(pairs, xs, ds, revs):
            xr, xi = x[0:1], x[KB : KB + 1]
            cr, ci = (q1r * xr + q1i * xi) / KB, (q1r * xi - q1i * xr) / KB
            d = d - jnp.where(prow == 0, cr, 0.0) - jnp.where(prow == PAD, ci, 0.0)
            d0, d1 = unpack(d, PAD)
            put(f2, 2 * p, d0)
            put(f2, 2 * p + 1, d1)
            put(bx, 2 * p, rv[0])
            put(bx, 2 * p + 1, rv[1])
        return carry

    b0_copy.wait()
    lax.fori_loop(0, NR // 2 // UNROLL_S, start, 0)
    first = mm(both_halves(f2), lc[...]) - mm(both_halves(bx), kq0)
    c_ref[...] = wf[...] * first

    def wide(ref):
        return jnp.concatenate([ref[s * NR : (s + 1) * NR, :] for s in range(SLOTS)], axis=1)

    def tallput(ref, x):
        for s in range(SLOTS):
            ref[s * NR : (s + 1) * NR, :] = x[:, s * KB : (s + 1) * KB]

    def forward(p):
        return pack(get(a1, 2 * p), get(a1, 2 * p + 1)).astype(BF)

    def middle(q, carry):
        pairs = [q * UNROLL + j for j in range(UNROLL)]
        ys = [mm(lc[...], forward(p)) for p in pairs]
        ys = [jnp.concatenate([hat[2] * y[:KB], hat[2] * y[KB:]], axis=0).astype(BF) for y in ys]
        ds = [mm(lct[...], y) for y in ys]
        for p, d in zip(pairs, ds):
            d0, d1 = unpack(d, PAD)
            put(f2, 2 * p, d0)
            put(f2, 2 * p + 1, d1)
        return carry

    def apply():
        coef = c_ref[...].astype(BF)
        full = mm(coef, lct[...])
        a1[0, :ROWS, :] = full[:, :KB]
        a1[1, :ROWS, :] = full[:, KB:]
        lax.fori_loop(0, NR // 2 // UNROLL, middle, 0)
        last = slice(top * NR, (top + 1) * NR)
        lr, li, ur, ui = a1[0, 0:NR, :], a1[1, 0:NR, :], a1[0, last, :], a1[1, last, :]
        f2[0, 0:NR, :] = f2[0, 0:NR, :] - (lr + z1r * ur - z1i * ui) / KB
        f2[1, 0:NR, :] = f2[1, 0:NR, :] - (li + z1r * ui + z1i * ur) / KB
        f2[0, last, :] = f2[0, last, :] - (z1r * lr + z1i * li) / KB
        f2[1, last, :] = f2[1, last, :] - (z1r * li - z1i * lr) / KB
        corr = mm(jnp.concatenate([c_ref[: ROWS // 2, :], c_ref[ROWS // 2 :, :]], axis=1).astype(BF), ky)
        h_ref[...] = mm(both_halves(f2), lc[...]) - jnp.concatenate([corr[:, :KB], corr[:, KB:]], axis=0)
        gram = nt(wide(c_ref).astype(BF), stack_halves(wide(h_ref)))
        gram = gram[:, :NR] + gram[:, NR:]
        gram = 0.5 * (gram + gram.T)
        eye = sublanes((NR, NR)) == lanes((NR, NR))
        trace = jnp.sum(jnp.sum(jnp.where(eye, gram, 0.0), axis=1, keepdims=True), axis=0, keepdims=True)
        return factor(gram + jnp.where(eye, RIDGE_SHARE * trace / NR + 1e-06, 0.0), 0.0)[1]

    def step(iteration, carry):
        @pl.when(iteration > 0)
        def _():
            tallput(h_ref, fine_mm(inv_ref[:, :NR], wide(h_ref)))
            c_ref[...] = wf[...] * h_ref[...]

        inv_ref[:, :NR] = apply()
        return carry

    lax.fori_loop(0, ITERS, step, 0)
    inverse = inv_ref[:, :NR]
    f2[0, :ROWS, :] = wf[...] * h_ref[...]
    moment = fine_nt(jnp.concatenate([f2[0, s * NR : (s + 1) * NR, :] for s in range(SLOTS)], axis=1), wide(h_ref))
    moment = jnp.dot(inverse, moment, precision=HI, preferred_element_type=F32)
    mixing = nt(moment, inverse, HI)
    mixing = 0.5 * (mixing + mixing.T)
    eye = sublanes((NR, NR)) == lanes((NR, NR))
    trace = jnp.sum(jnp.sum(jnp.where(eye, mixing, 0.0), axis=1, keepdims=True), axis=0, keepdims=True)
    root = factor(mixing, 1e-6 * trace + 1e-30)[0]
    combine = jnp.dot(root, inverse, precision=HI, preferred_element_type=F32)
    tallput(c_ref, fine_mm(combine, wide(c_ref).astype(BF).astype(F32)))
    coef = c_ref[...].astype(BF)
    full = mm(jnp.concatenate([coef, coef], axis=1), lct2[...])
    a1[0, :ROWS, :] = full[:, :KB]
    a1[1, :ROWS, :] = full[:, KB:]
    shifted = mm(coef, kq2)
    f2[0, :ROWS, :] = shifted[:, :KB]
    f2[1, :ROWS, :] = shifted[:, KB:]
    f2[:, ROWS:, :] = jnp.zeros((2, PAD * NR - ROWS, KB), F32)

    def finish(q, carry):
        pairs = [q * UNROLL_F + j for j in range(UNROLL_F)]
        xs = [pack(get(a1, 2 * p), get(a1, 2 * p + 1)) for p in pairs]
        cols = [[mm(revt[...], get(f2, 2 * p + e).astype(BF)) for e in range(2)] for p in pairs]
        ys = [mm(lc2[...], jnp.concatenate([x, x], axis=0).astype(BF)) for x in xs]
        ys = [jnp.concatenate([hat[0] * y[:KB] - hat[1] * y[KB:], hat[0] * y[KB:] + hat[1] * y[:KB]], axis=0).astype(BF) for y in ys]
        us = [mm(lbt[...], y) for y in ys]
        for p, x, u, col in zip(pairs, xs, us, cols):
            xr, xi = x[0:1], x[PAD : PAD + 1]
            cr, ci = (q1r * xr - q1i * xi) / KB, (q1r * xi + q1i * xr) / KB
            u = u - jnp.where(urow == 0, cr, 0.0) - jnp.where(urow == KB, ci, 0.0)
            pair = unpack(u, KB)
            for e in range(2):
                ub = pair[e].astype(BF)
                out_ref[2 * p + e] = (mm(ub, lb[...]) - col[e]).astype(BF)
        return carry

    lax.fori_loop(0, NR // 2 // UNROLL_F, finish, 0)


def synthesize(rank, tile_slit, sides, zernike, source_points, source_weight, start_block):
    smem = pl.BlockSpec(memory_space=pltpu.SMEM)
    vmem = pl.BlockSpec(memory_space=pltpu.VMEM)
    tables = block_tables()
    tables = [jnp.asarray(tables[i]) for i in (0, 1, 2, 3, 4, 5, 8, 9)]
    big = (2, PAD * NR, KB)
    return pl.pallas_call(
        synth_kernel,
        out_shape=jax.ShapeDtypeStruct((NR, KB, 2 * KB), BF),
        in_specs=[smem] * 2 + [vmem] * (6 + len(tables)) + [pl.BlockSpec(memory_space=pl.ANY)],
        out_specs=vmem,
        compiler_params=pltpu.CompilerParams(vmem_limit_bytes=VMEM_CAP),
        scratch_shapes=[
            pltpu.VMEM((NR, KB), F32),
            pltpu.VMEM((3, KB, 2 * KB), F32),
            pltpu.VMEM(big, F32),
            pltpu.VMEM(big, F32),
            pltpu.VMEM((ROWS, KB), F32),
            pltpu.VMEM((ROWS, KB), F32),
            pltpu.VMEM((ROWS, KB), F32),
            pltpu.VMEM(big, F32),
            pltpu.VMEM(start_block.shape, F32),
            pltpu.SemaphoreType.DMA,
        ],
    )(rank.reshape(1), *far(tile_slit), *sides, *far(zernike, source_points.T, source_weight.reshape(1, -1), jnp.asarray(zernike_polynomials()), *tables, start_block))


def tables_of(count, period):
    t = dft(np.arange(count), np.arange(KB) - KB // 2, 1, period)
    return t.real.astype(np.float32), t.imag.astype(np.float32)


def cast(x):
    return np.ascontiguousarray(x).astype(jnp.bfloat16)


def column_table():
    cc, cs = tables_of(PW, PW)
    out = np.zeros((5 * TS, 2 * KB), np.float32)
    out[2 * TS - HALO : 2 * TS - HALO + PW] = np.concatenate([cc, -cs], 1)
    return cast(out)


def row_table():
    rc, rs = tables_of(TS, TS)
    return np.concatenate([rc, rs], 1)


def image_tables():
    rc, rs = tables_of(TS, TS)
    cc, cs = tables_of(PW, PW)
    turn = np.concatenate([rc.T, rs.T], 1)
    inv_t = np.concatenate([cc, -cs], 1)[HALO : HALO + TS].T
    adj = np.concatenate([cc, cs], 1)[HALO : HALO + TS]
    rows = row_table()
    return (column_table(),) + tuple(cast(x) for x in (rows.T, rows, turn, inv_t, adj))


def tile_columns(ref, tile):
    return ref[pl.ds(pl.multiple_of(TS * (3 - tile), TS), 2 * TS), :]


def image_kernel(rank_ref, m0, m1, m2, m3, kern_ref, fwd, rows_t, rows, turn, inv_t, adj, o0, o1, o2, o3, patch, goal, fields, inten, gsum, spec):
    rank = rank_ref[0]
    quarter = m0.shape[0]
    left, outer = rank < 2, (rank == 0) | (rank == 3)
    block_of = lambda j: pl.ds(pl.multiple_of((rank ^ j) * quarter, quarter), quarter)
    low_end, high_end = neighbour_marks(m0.at[:, 4 * TS : 4 * TS + SIDE], m0.at[:, 4 * TS + SIDE :])
    present = jnp.where(rank == 0, low_end, jnp.where(rank == 3, high_end, 1.0)) > 0.5
    for j, m in enumerate((m0, m1, m2, m3)):
        side = jnp.where(left, m[:, 4 * TS : 4 * TS + SIDE], m[:, 4 * TS + SIDE :])
        own = jnp.where(left, m[:, 2 * TS : 3 * TS], m[:, 3 * TS : 4 * TS])
        patch[block_of(j), : 2 * TS] = m[:, : 2 * TS]
        patch[block_of(j), 2 * TS :] = side[:, TS:]
        goal[block_of(j), :] = jnp.where(outer, side[:, :TS], own).astype(F32)
    s = 1.0 / math.sqrt(TS * PW)
    start = jnp.where(rank < 2, PW - rank * TS, 3 * TS - (rank - 2) * TS)
    side_table = fwd[pl.ds(pl.multiple_of(start, HALO), PW), :]
    table = jnp.concatenate([tile_columns(fwd, rank), side_table], axis=0)
    columns = mm(patch[...], table).astype(BF)
    sums = mm(rows_t[...], columns)
    spec[0] = s * (sums[:KB, :KB] + sums[KB:, KB:])
    spec[1] = s * (sums[:KB, KB:] - sums[KB:, :KB])
    inten[...] = jnp.zeros((TS, TS), F32)
    gsum[...] = jnp.zeros((KB, 2 * KB), F32)

    def forward(q, carry):
        ks = [q * UNROLL_I + e for e in range(UNROLL_I)]
        sr, si = spec[0], spec[1]
        blocks = []
        for k in ks:
            kr, ki = kern_ref[k, :, :KB].astype(F32), kern_ref[k, :, KB:].astype(F32)
            wr, wi = kr * sr + ki * si, kr * si - ki * sr
            blocks.append(jnp.concatenate([jnp.concatenate([wr, wi], axis=1), jnp.concatenate([-wi, wr], axis=1)], axis=0).astype(BF))
        waves = [mm(rows[...], b).astype(BF) for b in blocks]
        total = inten[...]
        for k, w in zip(ks, waves):
            field = mm(w, inv_t[...])
            fields[k] = field
            total = total + field * field
        inten[...] = total
        return carry

    lax.fori_loop(0, NR // UNROLL_I, forward, 0)
    resist = 1.0 / (1.0 + jnp.exp(-STEEPNESS * (inten[...] - THRESHOLD)))
    inten[...] = 4.0 * (resist - goal[...]) * STEEPNESS * resist * (1.0 - resist)
    goal[...] = resist

    def backward(q, carry):
        ks = [q * UNROLL_I + e for e in range(UNROLL_I)]
        cols = [mm((fields[k] * inten[...]).astype(BF), adj[...]) for k in ks]
        blocks = [jnp.concatenate([c, jnp.concatenate([-c[:, KB:], c[:, :KB]], axis=1)], axis=0).astype(BF) for c in cols]
        turned = [mm(turn[...], b) for b in blocks]
        gr, gi = gsum[:, :KB], gsum[:, KB:]
        for k, y in zip(ks, turned):
            kr, ki = kern_ref[k, :, :KB].astype(F32), kern_ref[k, :, KB:].astype(F32)
            gr = gr + kr * y[:, :KB] + ki * y[:, KB:]
            gi = gi + ki * y[:, :KB] - kr * y[:, KB:]
        gsum[:, :KB] = gr
        gsum[:, KB:] = gi
        return carry

    lax.fori_loop(0, NR // UNROLL_I, backward, 0)
    grad = jnp.where(present, s * gsum[...], 0.0)
    block = jnp.concatenate([grad, jnp.concatenate([-grad[:, KB:], grad[:, :KB]], axis=1)], axis=0).astype(BF)
    inten[...] = mm(rows[...], block)
    for j, o in enumerate((o0, o1, o2, o3)):
        o[:quarter, :] = inten[block_of(j), :].astype(BF)
        o[quarter:, :] = goal[block_of(j), :].astype(BF)


def imaging(rank, packs, kern):
    quarter = packs[0].shape[0]
    smem = pl.BlockSpec(memory_space=pltpu.SMEM)
    vmem = pl.BlockSpec(memory_space=pltpu.VMEM)
    tables = [jnp.asarray(x) for x in image_tables()]
    return pl.pallas_call(
        image_kernel,
        out_shape=(jax.ShapeDtypeStruct((2 * quarter, TS), BF),) * 4,
        in_specs=[smem] + [vmem] * (5 + len(tables)),
        out_specs=(vmem,) * 4,
        compiler_params=pltpu.CompilerParams(vmem_limit_bytes=VMEM_CAP),
        scratch_shapes=[
            pltpu.VMEM((TS, 2 * TS + PW), BF),
            pltpu.VMEM((TS, TS), F32),
            pltpu.VMEM((NR, TS, TS), F32),
            pltpu.VMEM((TS, TS), F32),
            pltpu.VMEM((KB, 2 * KB), F32),
            pltpu.VMEM((2, KB, KB), F32),
        ],
    )(rank.reshape(1), *near(*packs, kern, *tables))


def back_kernel(rank_ref, n0, n1, n2, n3, fwd, resist_ref, grad_ref, held):
    rank = rank_ref[0]
    quarter, width = grad_ref.shape
    for j, n in enumerate((n0, n1, n2, n3)):
        held[rank ^ j] = n[...]
    resist_ref[:, :TS] = held[1, quarter:, :]
    resist_ref[:, TS:] = held[2, quarter:, :]
    parts = []
    for tile in range(4):
        parts.append(nt(held[tile, :quarter, :], fwd[TS * (3 - tile) : TS * (5 - tile), :]))
    grad_ref[...] = (parts[0] + parts[1] + parts[2] + parts[3]).astype(BF)


def back(rank, notes):
    quarter = notes[0].shape[0] // 2
    smem = pl.BlockSpec(memory_space=pltpu.SMEM)
    vmem = pl.BlockSpec(memory_space=pltpu.VMEM)
    whole = jax.ShapeDtypeStruct((quarter, 2 * TS), BF)
    return pl.pallas_call(
        back_kernel,
        out_shape=(whole, whole),
        in_specs=[smem] + [vmem] * 5,
        out_specs=(vmem, vmem),
        compiler_params=pltpu.CompilerParams(vmem_limit_bytes=VMEM_CAP),
        scratch_shapes=[pltpu.VMEM((4, 2 * quarter, TS), BF)],
    )(rank.reshape(1), *near(*notes, jnp.asarray(column_table())))


def prep_kernel(slit_ref, mask, goal, right_ref, left_ref, pack_ref):
    quarter = mask.shape[0]
    lane = lanes((quarter, PW))
    pack_ref[:, : 2 * TS] = mask[...]
    pack_ref[:, 2 * TS : 4 * TS] = goal[...]
    right_ref[:, :TS] = goal[:, TS:]
    left_ref[:, :TS] = goal[:, :TS]
    first, second = (slit_ref[0] + 1).astype(F32), (slit_ref[1] + 1).astype(F32)
    right_ref[:, TS:] = jnp.where(lane < HALO, second, mask[:, 2 * TS - PW :].astype(F32)).astype(BF)
    left_ref[:, TS:] = jnp.where(lane >= PW - HALO, first, mask[:, :PW].astype(F32)).astype(BF)


def messages(tile_slit, mask, target):
    smem = pl.BlockSpec(memory_space=pltpu.SMEM)
    vmem = pl.BlockSpec(memory_space=pltpu.VMEM)
    return pl.pallas_call(
        prep_kernel,
        out_shape=tuple(jax.ShapeDtypeStruct((mask.shape[0], w), BF) for w in (SIDE, SIDE, 4 * TS + 2 * SIDE)),
        compiler_params=pltpu.CompilerParams(vmem_limit_bytes=VMEM_CAP),
        in_specs=[smem, vmem, vmem],
        out_specs=(vmem, vmem, vmem),
    )(*far(tile_slit, mask, target))


def swap(x, m, size):
    return lax.ppermute(x, "src", [(i, i ^ m) for i in range(size)])


def shift(x, step, count):
    pairs = [(i, i + step) for i in range(count) if 0 <= i + step < count]
    return lax.ppermute(x, "tile", pairs)


def on_device(mask, target, start_block, zernike, source_points, source_weight, tile_slit):
    groups = lax.axis_size("tile")
    size = lax.axis_size("src")
    rank = lax.axis_index("src").astype(jnp.int32)
    rightward, leftward, pack = messages(tile_slit, mask, target)
    from_left = shift(rightward, 1, groups)
    from_right = shift(leftward, -1, groups)
    pack = lax.dynamic_update_slice(pack, from_left, (0, 4 * TS))
    pack = lax.dynamic_update_slice(pack, from_right, (0, 4 * TS + SIDE))
    packs = [pack] + [swap(pack, m, size) for m in (1, 2, 3)]
    kern = synthesize(rank, tile_slit, (from_left, from_right), zernike, source_points, source_weight, start_block)
    notes = imaging(rank, packs, kern)
    return tuple(back(rank, [notes[0]] + [swap(notes[m], m, size) for m in (1, 2, 3)]))


def solution(mesh):
    placed = (P("src", "tile"), P("src", "tile"), P(), P(), P(), P(), P("tile"))
    return jax.shard_map(
        on_device,
        mesh=mesh,
        in_specs=placed,
        out_specs=(P("src", "tile"), P("src", "tile")),
        check_vma=False,
    )
```
